32 devices in a mesh: row: 16 (over z, y, core), col: 2 (over x).
Axes of the slice: x: 2, y: 2, z: 4, core: 2. Of those that a mesh axis runs over, the one named last changes fastest.
Arguments:
- specimen_slices: float32 [2, 2, 4096, 512], P(None, None, 'row', 'col'), may hold values from -6 to 6
- illumination_probe: float32 [2, 128, 128], replicated, may hold values from -6 to 6
- propagation_phase: float32 [128, 128], replicated, may hold values from -3.140625 to 3.140625
- amplitudes: float32 [16, 2, 4, 128, 128], P('row', 'col'), may hold values from 0.5 to 4
- positions: int32 [16, 2, 4, 2], P('row', 'col'), may hold values from 0 to 255
- counts: int32 [16, 2], P('row', 'col'), may hold values from 1 to 4, as said below
- measurement_index: int32 [16, 2, 4], P('row', 'col'), may hold values from 0 to 3, each once within a row
Outputs:
- updated: float32 [2, 2, 4096, 512], P(None, None, 'row', 'col')
The draws below stay inside these ranges and needn't reach their ends.
Inputs may be any that keep to these rules, and one draw needn't show every extreme that they name: `counts`: some tile holds exactly 4 probe positions.
All inputs are finite; a program needn't handle non-finite values.
Results may differ from the reference program's by a relative error of at most 0.0001.
Values sent between devices are 32-bit elements; how exact they have to be, the bound alone decides.
No kernel may reach another device: no remote copies, remote signals or barrier semaphores. Data moves between devices by JAX's collectives and lax.ppermute only.
A program may use at most 64 MiB of HBM per device.

```python
import math
import jax
import jax.numpy as jnp
from jax import lax

TILE = 256
PATCH = 128
MAX_PROBE_SPOTS = 4
ITERS = 2
NR = 4096
NC = 512
N_ROW = 16
N_COL = 2


def draw_counts(key, part):
    rows_tiles = NR // TILE
    cols_tiles = NC // TILE
    key_one, key_two, key_three = jax.random.split(key, 3)
    first = jax.random.randint(key_one, (rows_tiles * cols_tiles,), 1, MAX_PROBE_SPOTS + 1)
    second = jax.random.randint(key_two, (rows_tiles * cols_tiles,), 1, MAX_PROBE_SPOTS + 1)
    values = jnp.minimum(first, second)
    chosen = jax.random.randint(key_three, (), 0, rows_tiles * cols_tiles)
    values = jnp.where(jnp.arange(rows_tiles * cols_tiles) == chosen, MAX_PROBE_SPOTS, values)
    return values.reshape(rows_tiles, cols_tiles).astype(jnp.int32)


def with_ends(entries, rng, smallest, top_value):
    spot = [jax.random.randint(jax.random.fold_in(rng, axis), (), 0, length) for axis, length in enumerate(entries.shape)]
    main_axis = entries.shape.index(max(entries.shape))
    beside = spot[:main_axis] + [(spot[main_axis] + 1) % entries.shape[main_axis]] + spot[main_axis + 1:]
    return entries.at[tuple(spot)].set(smallest).at[tuple(beside)].set(top_value)


def levels(key, shape, pieces, least, largest):
    loudness = 1.0
    for axis_at, parts in pieces:
        heights = jax.random.uniform(jax.random.fold_in(jax.random.fold_in(key, 6), axis_at), (parts,), jnp.float32, least / len(pieces), largest / len(pieces))
        loudness = loudness * jnp.repeat(jnp.exp(heights), shape[axis_at] // parts).reshape((-1,) + (1,) * (len(shape) - 1 - axis_at))
    return loudness


def scatter_about(own_key, shape, scale, reach, shards=(), kind=jnp.bfloat16):
    entries = scale * jax.random.normal(own_key, shape, jnp.float32)
    if shards:
        entries = entries * levels(own_key, shape, shards, -0.22, 0.18)
    return jnp.clip(entries, -reach, reach).astype(kind)


def setup_inputs(seed: int = 0) -> dict:
    arg_keys = jax.random.split(jax.random.key(seed), 8)
    return {
        "specimen_slices": scatter_about(arg_keys[0], (2, 2, NR, NC), 1.0, 6.0, ((2, 16), (3, 2)), jnp.float32),
        "illumination_probe": scatter_about(arg_keys[1], (2, PATCH, PATCH), 1.0, 6.0, (), jnp.float32),
        "propagation_phase": jnp.clip(jax.random.uniform(arg_keys[2], (PATCH, PATCH), jnp.float32, -3.140625, 3.140625), -3.140625, 3.140625),
        "amplitudes": jnp.clip(jnp.exp(math.log(4.0) - 2.0794415 * jax.random.uniform(arg_keys[3], (N_ROW, N_COL, MAX_PROBE_SPOTS, PATCH, PATCH), jnp.float32) ** levels(arg_keys[3], (N_ROW, N_COL, MAX_PROBE_SPOTS, PATCH, PATCH), ((0, 16), (1, 2)), -0.2, 0.2)), 0.5, 4.0),
        "positions": with_ends(jax.random.randint(arg_keys[4], (N_ROW, N_COL, MAX_PROBE_SPOTS, 2), 0, TILE), jax.random.fold_in(arg_keys[4], 1), 0, TILE - 1).astype(jnp.int32),
        "counts": draw_counts(jax.random.fold_in(arg_keys[7], 71), 0),
        "measurement_index": jax.vmap(lambda own: jax.random.permutation(own, MAX_PROBE_SPOTS))(jax.random.split(arg_keys[6], N_ROW * N_COL)).reshape((N_ROW, N_COL, MAX_PROBE_SPOTS)).astype(jnp.int32),
    }


step_size = 0.02
floor_amp = 0.5

def dft_table(width):
    index = jnp.arange(width, dtype=jnp.int32)
    phase_int = index[:, None] * index[None, :] % width
    angle = phase_int.astype(jnp.float32) * (2.0 * math.pi / width)
    scale = 1.0 / math.sqrt(width)
    return (jnp.cos(angle) * scale, -jnp.sin(angle) * scale)

def real_dot(left, right):
    return jnp.dot(left, right, precision=lax.Precision.HIGHEST)

def complex_dot(left, right):
    return (real_dot(left[0], right[0]) - real_dot(left[1], right[1]), real_dot(left[0], right[1]) + real_dot(left[1], right[0]))

def complex_mul(left, right):
    return (left[0] * right[0] - left[1] * right[1], left[0] * right[1] + left[1] * right[0])

def conjugate(pair):
    return (pair[0], -pair[1])

def transform(pair, table, sign):
    matrix = (table[0], sign * table[1])
    return complex_dot(complex_dot(matrix, pair), matrix)

def probe_gradient(windows, probe_pair, prop_pair, recorded_intensity, table):
    first = (windows[0], windows[1])
    second = (windows[2], windows[3])
    exit_one = complex_mul(probe_pair, first)
    moved = transform(complex_mul(prop_pair, transform(exit_one, table, 1.0)), table, -1.0)
    exit_two = complex_mul(moved, second)
    psi_wave = transform(exit_two, table, 1.0)
    magnitude = jnp.sqrt(psi_wave[0] * psi_wave[0] + psi_wave[1] * psi_wave[1])
    factor = 1.0 - recorded_intensity / jnp.maximum(magnitude, floor_amp)
    residual = (psi_wave[0] * factor, psi_wave[1] * factor)
    back_two = transform(residual, table, -1.0)
    grad_two = complex_mul(conjugate(moved), back_two)
    back_moved = complex_mul(conjugate(second), back_two)
    back_one = transform(complex_mul(conjugate(prop_pair), transform(back_moved, table, 1.0)), table, -1.0)
    grad_one = complex_mul(conjugate(probe_pair), back_one)
    return jnp.stack([grad_one[0], grad_one[1], grad_two[0], grad_two[1]])

def reference(specimen_slices, illumination_probe, propagation_phase, amplitudes, positions, counts, measurement_index):
    table = dft_table(PATCH)
    probe_pair = (illumination_probe[0], illumination_probe[1])
    prop_pair = (jnp.cos(propagation_phase), jnp.sin(propagation_phase))
    current = specimen_slices.reshape(4, NR, NC)
    zero_index = jnp.int32(0)
    for iteration in range(ITERS):
        padded = jnp.concatenate([current, current[:, :PATCH, :]], 1)
        padded = jnp.concatenate([padded, padded[:, :, :PATCH]], 2)
        gradient = jnp.zeros_like(padded)

        def per_tile(tile_number, gradient):
            row_of_tile = (tile_number // N_COL).astype(jnp.int32)
            column_of_tile = (tile_number % N_COL).astype(jnp.int32)

            def per_probe(measurement_slot_count, gradient):
                row_start = (row_of_tile * TILE + positions[row_of_tile, column_of_tile, measurement_slot_count, 0]).astype(jnp.int32)
                col_start = (column_of_tile * TILE + positions[row_of_tile, column_of_tile, measurement_slot_count, 1]).astype(jnp.int32)
                windows = lax.dynamic_slice(padded, (zero_index, row_start, col_start), (4, PATCH, PATCH))
                recorded_intensity = amplitudes[row_of_tile, column_of_tile, measurement_index[row_of_tile, column_of_tile, measurement_slot_count]]
                update = probe_gradient(windows, probe_pair, prop_pair, recorded_intensity, table)
                before = lax.dynamic_slice(gradient, (zero_index, row_start, col_start), (4, PATCH, PATCH))
                return lax.dynamic_update_slice(gradient, before + update, (zero_index, row_start, col_start))
            return lax.fori_loop(0, counts[row_of_tile, column_of_tile], per_probe, gradient)
        gradient = lax.fori_loop(0, N_ROW * N_COL, per_tile, gradient)
        folded = gradient[:, :NR, :NC]
        folded = folded.at[:, :PATCH, :].add(gradient[:, NR:, :NC])
        folded = folded.at[:, :, :PATCH].add(gradient[:, :NR, NC:])
        folded = folded.at[:, :PATCH, :PATCH].add(gradient[:, NR:, NC:])
        current = current - step_size * folded
    return current.reshape(2, 2, NR, NC)
```

```python
import functools
import math

import jax
import jax.numpy as jnp
import ml_dtypes
import numpy as np
from jax import lax
from jax.experimental import pallas as pl
from jax.experimental.pallas import tpu as pltpu
from jax.sharding import PartitionSpec as P

ITERS = 2
LANES = 128

step_size = 0.02
floor_amp = 0.5


def from_behind(block, axis, distance):
    devices = range(lax.axis_size(axis))
    route = [((i - distance) % len(devices), i) for i in devices]
    return lax.ppermute(block, axis, route)


def two_parts(value):
    high = value.astype(ml_dtypes.bfloat16)
    low = (value - high.astype(np.float64)).astype(ml_dtypes.bfloat16)
    return high, low


def dft_operands(width):
    index = np.arange(width)
    angle = (index[:, None] * index[None, :] % width) * (2.0 * math.pi / width)
    real = np.cos(angle) / math.sqrt(width)
    imag = -np.sin(angle) / math.sqrt(width)
    right = np.block([[real, imag], [-imag, real]])
    right_high, right_low = two_parts(right)
    left_high, left_low = two_parts(right.T)
    return (
        np.concatenate([right_high, right_high], 0),
        right_low,
        np.concatenate([left_high, left_high], 1),
        left_low,
    )


def split(value):
    high = value.astype(jnp.bfloat16)
    low = (value - high.astype(jnp.float32)).astype(jnp.bfloat16)
    return high, low


def probe_kernel(
    pos_ref, count_ref, slot_ref,
    tile_ref, below_ref, beside_ref, corner_ref,
    probe_ref, prop_ref, amp_ref,
    right_high_ref, right_low_ref, left_high_ref, left_low_ref,
    own_ref, down_ref, side_ref, diag_ref,
    ext_ref, grad_ref, win_ref, moved_ref, a_ref, b_ref,
    *, spots, tile_px, width,
):
    blocks = tile_px // LANES
    for c in range(4):
        for b in range(blocks):
            ext_ref[c, b, :tile_px, :] = tile_ref[c, :, b * LANES:(b + 1) * LANES]
            ext_ref[c, b, tile_px:, :] = below_ref[c, :, b * LANES:(b + 1) * LANES]
        ext_ref[c, blocks, :tile_px, :] = beside_ref[c]
        ext_ref[c, blocks, tile_px:, :] = corner_ref[c]
    grad_ref[...] = jnp.zeros(grad_ref.shape, jnp.float32)
    lane = lax.broadcasted_iota(jnp.int32, (width, LANES), 1)
    total = count_ref[0]

    def rows(j):
        return slice(j * width, (j + 1) * width)

    def put(j, real, imag):
        real_high, real_low = split(real)
        imag_high, imag_low = split(imag)
        a_ref[rows(j), 0:width] = real_high
        a_ref[rows(j), width:2 * width] = imag_high
        a_ref[rows(j), 2 * width:3 * width] = real_low
        a_ref[rows(j), 3 * width:4 * width] = imag_low

    def transform():
        half = jnp.dot(a_ref[...], right_high_ref[...], preferred_element_type=jnp.float32)
        half += jnp.dot(a_ref[:, :2 * width], right_low_ref[...], preferred_element_type=jnp.float32)
        for j in range(spots):
            real_high, real_low = split(half[rows(j), :width])
            imag_high, imag_low = split(half[rows(j), width:])
            b_ref[0:width, rows(j)] = real_high
            b_ref[width:2 * width, rows(j)] = imag_high
            b_ref[2 * width:3 * width, rows(j)] = real_low
            b_ref[3 * width:4 * width, rows(j)] = imag_low
        full = jnp.dot(left_high_ref[...], b_ref[...], preferred_element_type=jnp.float32)
        full += jnp.dot(left_low_ref[...], b_ref[:2 * width, :], preferred_element_type=jnp.float32)
        return [(full[:width, rows(j)], full[width:, rows(j)]) for j in range(spots)]

    starts = []
    for j in range(spots):
        row = pos_ref[2 * j]
        col = pos_ref[2 * j + 1]
        block = col // LANES
        shift = col % LANES
        starts.append((row, block, shift))
        for c in range(4):
            near = ext_ref[c, block, pl.ds(row, width), :]
            far = ext_ref[c, block + 1, pl.ds(row, width), :]
            win_ref[j, c] = pltpu.roll(jnp.where(lane >= shift, near, far), LANES - shift, 1)
        put(
            j,
            probe_ref[0] * win_ref[j, 0] - probe_ref[1] * win_ref[j, 1],
            probe_ref[0] * win_ref[j, 1] + probe_ref[1] * win_ref[j, 0],
        )
    for j, (real, imag) in enumerate(transform()):
        put(
            j,
            prop_ref[0] * real - prop_ref[1] * imag,
            -(prop_ref[0] * imag + prop_ref[1] * real),
        )
    for j, (real, negative) in enumerate(transform()):
        imag = -negative
        moved_ref[j, 0] = real
        moved_ref[j, 1] = imag
        put(
            j,
            real * win_ref[j, 2] - imag * win_ref[j, 3],
            real * win_ref[j, 3] + imag * win_ref[j, 2],
        )
    for j, (real, imag) in enumerate(transform()):
        measured = amp_ref[slot_ref[j]]
        power = jnp.maximum(real * real + imag * imag, floor_amp * floor_amp)
        factor = 1.0 - measured * lax.rsqrt(power)
        put(j, real * factor, -(imag * factor))

    def scatter(j, c, update):
        row, block, shift = starts[j]
        update = jnp.where(j < total, update, 0.0)
        turned = pltpu.roll(update, shift, 1)
        near = lane >= shift
        grad_ref[c, block, pl.ds(row, width), :] += jnp.where(near, turned, 0.0)
        grad_ref[c, block + 1, pl.ds(row, width), :] += jnp.where(near, 0.0, turned)

    for j, (real, negative) in enumerate(transform()):
        imag = -negative
        scatter(j, 2, moved_ref[j, 0] * real + moved_ref[j, 1] * imag)
        scatter(j, 3, moved_ref[j, 0] * imag - moved_ref[j, 1] * real)
        put(
            j,
            win_ref[j, 2] * real + win_ref[j, 3] * imag,
            win_ref[j, 2] * imag - win_ref[j, 3] * real,
        )
    for j, (real, imag) in enumerate(transform()):
        put(
            j,
            prop_ref[0] * real + prop_ref[1] * imag,
            -(prop_ref[0] * imag - prop_ref[1] * real),
        )
    for j, (real, negative) in enumerate(transform()):
        imag = -negative
        scatter(j, 0, probe_ref[0] * real + probe_ref[1] * imag)
        scatter(j, 1, probe_ref[0] * imag - probe_ref[1] * real)
    for c in range(4):
        for b in range(blocks):
            own_ref[c, :, b * LANES:(b + 1) * LANES] = grad_ref[c, b, :tile_px, :]
            down_ref[c, :, b * LANES:(b + 1) * LANES] = grad_ref[c, b, tile_px:, :]
        side_ref[c] = grad_ref[c, blocks, :tile_px, :]
        diag_ref[c] = grad_ref[c, blocks, tile_px:, :]


def tile_gradient(scalars, tile, halo, shared, tables, spots, width):
    tile_px = tile.shape[1]
    ext = tile_px + width
    f32 = functools.partial(jax.ShapeDtypeStruct, dtype=jnp.float32)
    smem = pl.BlockSpec(memory_space=pltpu.SMEM)
    vmem = pl.BlockSpec(memory_space=pltpu.VMEM)
    body = functools.partial(probe_kernel, spots=spots, tile_px=tile_px, width=width)
    return pl.pallas_call(
        body,
        in_specs=[smem] * 3 + [vmem] * 11,
        out_specs=[vmem] * 4,
        out_shape=[
            f32((4, tile_px, tile_px)),
            f32((4, width, tile_px)),
            f32((4, tile_px, width)),
            f32((4, width, width)),
        ],
        scratch_shapes=[
            pltpu.VMEM((4, ext // LANES, ext, LANES), jnp.float32),
            pltpu.VMEM((4, ext // LANES, ext, LANES), jnp.float32),
            pltpu.VMEM((spots, 4, width, width), jnp.float32),
            pltpu.VMEM((spots, 2, width, width), jnp.float32),
            pltpu.VMEM((spots * width, 4 * width), jnp.bfloat16),
            pltpu.VMEM((4 * width, spots * width), jnp.bfloat16),
        ],
        name="tile_gradient",
    )(*scalars, tile, *halo, *shared, *tables)


def body(
    specimen_slices,
    illumination_probe,
    propagation_phase,
    amplitudes,
    positions,
    counts,
    measurement_index,
):
    tile_px = specimen_slices.shape[2]
    width = illumination_probe.shape[1]
    spots = positions.shape[2]
    tables = [jnp.asarray(t) for t in dft_operands(width)]
    prop = jnp.stack([jnp.cos(propagation_phase), jnp.sin(propagation_phase)])
    scalars = (positions.reshape(-1), counts.reshape(-1), measurement_index.reshape(-1))
    shared = (illumination_probe, prop, amplitudes[0, 0])
    current = specimen_slices.reshape(4, tile_px, tile_px)
    for iteration in range(ITERS):
        below = from_behind(current[:, :width, :], "row", -1)
        beside = from_behind(current[:, :, :width], "col", -1)
        corner = from_behind(below[:, :, :width], "col", -1)
        own, down, side, diag = tile_gradient(
            scalars, current, (below, beside, corner), shared, tables, spots, width
        )
        from_above = from_behind(down, "row", 1)
        from_left = from_behind(side, "col", 1)
        corner_back = from_behind(from_behind(diag, "col", 1), "row", 1)
        own = own.at[:, :width, :].add(from_above)
        own = own.at[:, :, :width].add(from_left)
        own = own.at[:, :width, :width].add(corner_back)
        current = current - step_size * own
    return current.reshape(specimen_slices.shape)


def solution(mesh):
    placed = (
        P(None, None, "row", "col"),
        P(),
        P(),
        P("row", "col", None, None, None),
        P("row", "col", None, None),
        P("row", "col"),
        P("row", "col", None),
    )
    return jax.shard_map(
        body, mesh=mesh, in_specs=placed, out_specs=P(None, None, "row", "col"), check_vma=False
    )
```

```python
import functools
import math

import jax
import jax.numpy as jnp
import ml_dtypes
import numpy as np
from jax import lax
from jax.experimental import pallas as pl
from jax.experimental.pallas import tpu as pltpu
from jax.sharding import PartitionSpec as P

ITERS = 2
LANES = 128

step_size = 0.02
floor_amp = 0.5


def from_behind(block, axis, distance):
    devices = range(lax.axis_size(axis))
    route = [((i - distance) % len(devices), i) for i in devices]
    return lax.ppermute(block, axis, route)


def two_parts(value):
    high = value.astype(ml_dtypes.bfloat16)
    low = (value - high.astype(np.float64)).astype(ml_dtypes.bfloat16)
    return high, low


def dft_operands(width):
    index = np.arange(width)
    angle = (index[:, None] * index[None, :] % width) * (2.0 * math.pi / width)
    real = np.cos(angle) / math.sqrt(width)
    imag = -np.sin(angle) / math.sqrt(width)
    right = np.block([[real, imag], [-imag, real]])
    right_high, right_low = two_parts(right)
    left_high, left_low = two_parts(right.T)
    return (
        np.concatenate([right_high, right_high], 0),
        right_low,
        np.concatenate([left_high, left_high], 1),
        left_low,
    )


def split(value):
    high = value.astype(jnp.bfloat16)
    low = (value - high.astype(jnp.float32)).astype(jnp.bfloat16)
    return high, low


def rows_of(j, width):
    return slice(j * width, (j + 1) * width)


def put(a_ref, j, width, real, imag):
    real_high, real_low = split(real)
    imag_high, imag_low = split(imag)
    rows = rows_of(j, width)
    a_ref[rows, 0:width] = real_high
    a_ref[rows, width:2 * width] = imag_high
    a_ref[rows, 2 * width:3 * width] = real_low
    a_ref[rows, 3 * width:4 * width] = imag_low


def transform(a_ref, b_ref, tables, spots, width):
    right_high_ref, right_low_ref, left_high_ref, left_low_ref = tables
    half = jnp.dot(a_ref[...], right_high_ref[...], preferred_element_type=jnp.float32)
    half += jnp.dot(a_ref[:, :2 * width], right_low_ref[...], preferred_element_type=jnp.float32)
    for j in range(spots):
        rows = rows_of(j, width)
        real_high, real_low = split(half[rows, :width])
        imag_high, imag_low = split(half[rows, width:])
        b_ref[0:width, rows] = real_high
        b_ref[width:2 * width, rows] = imag_high
        b_ref[2 * width:3 * width, rows] = real_low
        b_ref[3 * width:4 * width, rows] = imag_low
    full = jnp.dot(left_high_ref[...], b_ref[...], preferred_element_type=jnp.float32)
    full += jnp.dot(left_low_ref[...], b_ref[:2 * width, :], preferred_element_type=jnp.float32)
    return [
        (full[:width, rows_of(j, width)], full[width:, rows_of(j, width)]) for j in range(spots)
    ]


def fill_ext(ext_ref, tile_ref, below_ref, upper_ref, lower_ref, corner_ref, width):
    tile_px = tile_ref.shape[1]
    blocks = tile_px // LANES
    for c in range(2):
        for b in range(blocks):
            lanes = slice(b * LANES, (b + 1) * LANES)
            ext_ref[c, b, :tile_px, :] = tile_ref[c, :, lanes]
            ext_ref[c, b, tile_px:, :] = below_ref[c, :, lanes]
        ext_ref[c, blocks, :width, :] = upper_ref[c]
        ext_ref[c, blocks, width:tile_px, :] = lower_ref[c]
        ext_ref[c, blocks, tile_px:, :] = corner_ref[c]


def place(pos_ref, j):
    col = pos_ref[2 * j + 1]
    return pos_ref[2 * j], col // LANES, col % LANES


def window(ext_ref, c, spot, width, lane):
    row, block, shift = spot
    near = ext_ref[c, block, pl.ds(row, width), :]
    far = ext_ref[c, block + 1, pl.ds(row, width), :]
    return pltpu.roll(jnp.where(lane >= shift, near, far), LANES - shift, 1)


def scatter(grad_ref, c, spot, width, lane, used, update):
    row, block, shift = spot
    turned = pltpu.roll(jnp.where(used, update, 0.0), shift, 1)
    near = lane >= shift
    grad_ref[c, block, pl.ds(row, width), :] += jnp.where(near, turned, 0.0)
    grad_ref[c, block + 1, pl.ds(row, width), :] += jnp.where(near, 0.0, turned)


def emit(grad_ref, own_ref, down_ref, upper_ref, lower_ref, diag_ref, width):
    tile_px = own_ref.shape[1]
    blocks = tile_px // LANES
    for c in range(2):
        for b in range(blocks):
            lanes = slice(b * LANES, (b + 1) * LANES)
            own_ref[c, :, lanes] = grad_ref[c, b, :tile_px, :]
            down_ref[c, :, lanes] = grad_ref[c, b, tile_px:, :]
        upper_ref[c] = grad_ref[c, blocks, :width, :]
        lower_ref[c] = grad_ref[c, blocks, width:tile_px, :]
        diag_ref[c] = grad_ref[c, blocks, tile_px:, :]


def lanes_of(width):
    return lax.broadcasted_iota(jnp.int32, (width, LANES), 1)


def forward_kernel(
    pos_ref, tile_ref, below_ref, upper_ref, lower_ref, corner_ref, probe_ref, prop_ref,
    rh_ref, rl_ref, lh_ref, ll_ref, moved_ref, ext_ref, a_ref, b_ref, *, spots, width,
):
    tables = (rh_ref, rl_ref, lh_ref, ll_ref)
    fill_ext(ext_ref, tile_ref, below_ref, upper_ref, lower_ref, corner_ref, width)
    lane = lanes_of(width)
    for j in range(spots):
        spot = place(pos_ref, j)
        real = window(ext_ref, 0, spot, width, lane)
        imag = window(ext_ref, 1, spot, width, lane)
        put(
            a_ref, j, width,
            probe_ref[0] * real - probe_ref[1] * imag,
            probe_ref[0] * imag + probe_ref[1] * real,
        )
    for j, (real, imag) in enumerate(transform(a_ref, b_ref, tables, spots, width)):
        put(
            a_ref, j, width,
            prop_ref[0] * real - prop_ref[1] * imag,
            -(prop_ref[0] * imag + prop_ref[1] * real),
        )
    for j, (real, negative) in enumerate(transform(a_ref, b_ref, tables, spots, width)):
        moved_ref[j, 0] = real
        moved_ref[j, 1] = -negative


def middle_kernel(
    pos_ref, count_ref, slot_ref, tile_ref, below_ref, upper_ref, lower_ref, corner_ref,
    moved_ref, amp_ref, rh_ref, rl_ref, lh_ref, ll_ref,
    own_ref, down_ref, up_out_ref, low_out_ref, diag_ref, back_ref,
    ext_ref, win_ref, a_ref, b_ref, *, spots, width,
):
    tables = (rh_ref, rl_ref, lh_ref, ll_ref)
    fill_ext(ext_ref, tile_ref, below_ref, upper_ref, lower_ref, corner_ref, width)
    lane = lanes_of(width)
    total = count_ref[0]
    spot_list = [place(pos_ref, j) for j in range(spots)]
    for j in range(spots):
        second_real = window(ext_ref, 0, spot_list[j], width, lane)
        second_imag = window(ext_ref, 1, spot_list[j], width, lane)
        win_ref[j, 0] = second_real
        win_ref[j, 1] = second_imag
        put(
            a_ref, j, width,
            moved_ref[j, 0] * second_real - moved_ref[j, 1] * second_imag,
            moved_ref[j, 0] * second_imag + moved_ref[j, 1] * second_real,
        )
    ext_ref[...] = jnp.zeros(ext_ref.shape, jnp.float32)
    for j, (real, imag) in enumerate(transform(a_ref, b_ref, tables, spots, width)):
        measured = amp_ref[slot_ref[j]]
        power = jnp.maximum(real * real + imag * imag, floor_amp * floor_amp)
        factor = 1.0 - measured * lax.rsqrt(power)
        put(a_ref, j, width, real * factor, -(imag * factor))
    for j, (real, negative) in enumerate(transform(a_ref, b_ref, tables, spots, width)):
        imag = -negative
        used = j < total
        scatter(ext_ref, 0, spot_list[j], width, lane, used, moved_ref[j, 0] * real + moved_ref[j, 1] * imag)
        scatter(ext_ref, 1, spot_list[j], width, lane, used, moved_ref[j, 0] * imag - moved_ref[j, 1] * real)
        back_ref[j, 0] = win_ref[j, 0] * real + win_ref[j, 1] * imag
        back_ref[j, 1] = win_ref[j, 0] * imag - win_ref[j, 1] * real
    emit(ext_ref, own_ref, down_ref, up_out_ref, low_out_ref, diag_ref, width)


def backward_kernel(
    pos_ref, count_ref, back_ref, probe_ref, prop_ref, rh_ref, rl_ref, lh_ref, ll_ref,
    own_ref, down_ref, up_out_ref, low_out_ref, diag_ref,
    ext_ref, a_ref, b_ref, *, spots, width,
):
    tables = (rh_ref, rl_ref, lh_ref, ll_ref)
    lane = lanes_of(width)
    total = count_ref[0]
    for j in range(spots):
        put(a_ref, j, width, back_ref[j, 0], back_ref[j, 1])
    ext_ref[...] = jnp.zeros(ext_ref.shape, jnp.float32)
    for j, (real, imag) in enumerate(transform(a_ref, b_ref, tables, spots, width)):
        put(
            a_ref, j, width,
            prop_ref[0] * real + prop_ref[1] * imag,
            -(prop_ref[0] * imag - prop_ref[1] * real),
        )
    for j, (real, negative) in enumerate(transform(a_ref, b_ref, tables, spots, width)):
        imag = -negative
        spot = place(pos_ref, j)
        used = j < total
        scatter(ext_ref, 0, spot, width, lane, used, probe_ref[0] * real + probe_ref[1] * imag)
        scatter(ext_ref, 1, spot, width, lane, used, probe_ref[0] * imag - probe_ref[1] * real)
    emit(ext_ref, own_ref, down_ref, up_out_ref, low_out_ref, diag_ref, width)


def folded(tile_ref, own_ref, above_ref, upper_ref, lower_ref, c, width):
    tile_px = own_ref.shape[1]
    top, low = slice(0, width), slice(width, tile_px)
    left, rest = slice(0, width), slice(width, tile_px)
    yield top, left, tile_ref[c, top, left] - step_size * (
        own_ref[c, top, left] + above_ref[c, :, left] + upper_ref[c]
    )
    yield top, rest, tile_ref[c, top, rest] - step_size * (own_ref[c, top, rest] + above_ref[c, :, rest])
    yield low, left, tile_ref[c, low, left] - step_size * (own_ref[c, low, left] + lower_ref[c])
    yield low, rest, tile_ref[c, low, rest] - step_size * own_ref[c, low, rest]


def update_kernel(
    tile_ref, own_ref, above_ref, upper_ref, lower_ref,
    new_ref, top_ref, left_up_ref, left_low_ref, *, width,
):
    for c in range(2):
        for k, (rows, lanes, value) in enumerate(
            folded(tile_ref, own_ref, above_ref, upper_ref, lower_ref, c, width)
        ):
            new_ref[c, rows, lanes] = value
            if k < 2:
                top_ref[c, :, lanes] = value
            if k == 0:
                left_up_ref[c] = value
            if k == 2:
                left_low_ref[c] = value


def finish_kernel(*refs, width):
    out_ref = refs[-1]
    for s in range(2):
        for c in range(2):
            for rows, lanes, value in folded(*refs[5 * s:5 * s + 5], c, width):
                out_ref[s, c, rows, lanes] = value


F32 = functools.partial(jax.ShapeDtypeStruct, dtype=jnp.float32)
SMEM = pl.BlockSpec(memory_space=pltpu.SMEM)
VMEM = pl.BlockSpec(memory_space=pltpu.VMEM)
LIMIT = pltpu.CompilerParams(vmem_limit_bytes=16 * 1024 * 1024)


def call(kernel, scalars, arrays, outs, scratch, name, **static):
    return pl.pallas_call(
        functools.partial(kernel, **static),
        in_specs=[SMEM] * len(scalars) + [VMEM] * len(arrays),
        out_specs=[VMEM] * len(outs),
        out_shape=outs,
        scratch_shapes=scratch,
        compiler_params=LIMIT,
        name=name,
    )(*scalars, *arrays)


def body(
    specimen_slices,
    illumination_probe,
    propagation_phase,
    amplitudes,
    positions,
    counts,
    measurement_index,
):
    tile_px = specimen_slices.shape[2]
    width = illumination_probe.shape[1]
    spots = positions.shape[2]
    ext = tile_px + width
    tables = [jnp.asarray(t) for t in dft_operands(width)]
    prop = jnp.stack([jnp.cos(propagation_phase), jnp.sin(propagation_phase)])
    where = positions.reshape(-1)
    count = counts.reshape(-1)
    slots = measurement_index.reshape(-1)
    measured = amplitudes[0, 0]
    static = dict(spots=spots, width=width)
    ext_space = pltpu.VMEM((2, ext // LANES, ext, LANES), jnp.float32)
    work = [
        pltpu.VMEM((spots * width, 4 * width), jnp.bfloat16),
        pltpu.VMEM((4 * width, spots * width), jnp.bfloat16),
    ]
    wave = F32((spots, 2, width, width))
    square = F32((2, width, width))
    whole = F32((2, tile_px, tile_px))
    strip = F32((2, width, tile_px))
    gradient = [whole, strip, square, square, square]

    def halo(top, left_up, left_low):
        upper = from_behind(left_up, "col", -1)
        lower = from_behind(left_low, "col", -1)
        below = from_behind(top, "row", -1)
        corner = from_behind(upper, "row", -1)
        return below, upper, lower, corner

    def fold(own, down, side_up, side_low, diag):
        corner = from_behind(diag, "row", 1)
        lower = from_behind(side_low, "col", 1)
        above = from_behind(down, "row", 1)
        upper = from_behind(side_up + corner, "col", 1)
        return own, above, upper, lower

    tiles = [specimen_slices[0], specimen_slices[1]]
    sends = [(t[:, :width, :], t[:, :width, :width], t[:, width:, :width]) for t in tiles]
    for iteration in range(ITERS):
        halo_one = halo(*sends[0])
        halo_two = halo(*sends[1])
        (moved,) = call(
            forward_kernel, (where,), (tiles[0], *halo_one, illumination_probe, prop, *tables),
            [wave], [ext_space, *work], "forward_wave", **static,
        )
        *grad_two, back = call(
            middle_kernel, (where, count, slots), (tiles[1], *halo_two, moved, measured, *tables),
            [*gradient, wave], [ext_space, pltpu.VMEM((spots, 2, width, width), jnp.float32), *work],
            "residual_wave", **static,
        )
        fold_two = fold(*grad_two)
        grad_one = call(
            backward_kernel, (where, count), (back, illumination_probe, prop, *tables),
            gradient, [ext_space, *work], "backward_wave", **static,
        )
        fold_one = fold(*grad_one)
        if iteration + 1 < ITERS:
            fresh, sends = [], []
            for tile, received in zip(tiles, (fold_one, fold_two)):
                new, *send = call(
                    update_kernel, (), (tile, *received), [whole, strip, square, square], [],
                    "update_slice", width=width,
                )
                fresh.append(new)
                sends.append(send)
            tiles = fresh
        else:
            (updated,) = call(
                finish_kernel, (), (tiles[0], *fold_one, tiles[1], *fold_two),
                [F32(specimen_slices.shape)], [], "finish", width=width,
            )
    return updated


def solution(mesh):
    placed = (
        P(None, None, "row", "col"),
        P(),
        P(),
        P("row", "col", None, None, None),
        P("row", "col", None, None),
        P("row", "col"),
        P("row", "col", None),
    )
    return jax.shard_map(
        body, mesh=mesh, in_specs=placed, out_specs=P(None, None, "row", "col"), check_vma=False
    )
```

```python
import functools
import math

import jax
import jax.numpy as jnp
import ml_dtypes
import numpy as np
from jax import lax
from jax.experimental import pallas as pl
from jax.experimental.pallas import tpu as pltpu
from jax.sharding import PartitionSpec as P

ITERS = 2
LANES = 128

step_size = 0.02
floor_amp = 0.5


def from_behind(block, axis, distance):
    devices = range(lax.axis_size(axis))
    route = [((i - distance) % len(devices), i) for i in devices]
    return lax.ppermute(block, axis, route)


def two_parts(value):
    high = value.astype(ml_dtypes.bfloat16)
    low = (value - high.astype(np.float64)).astype(ml_dtypes.bfloat16)
    return high, low


def dft_operands(width):
    index = np.arange(width)
    angle = (index[:, None] * index[None, :] % width) * (2.0 * math.pi / width)
    real = np.cos(angle) / math.sqrt(width)
    imag = -np.sin(angle) / math.sqrt(width)
    right = np.block([[real, imag], [-imag, real]])
    right_high, right_low = two_parts(right)
    left_high, left_low = two_parts(right.T)
    return (
        np.concatenate([right_high, right_high], 0),
        right_low,
        np.concatenate([left_high, left_high], 1),
        left_low,
    )


def split(value):
    high = value.astype(jnp.bfloat16)
    low = (value - high.astype(jnp.float32)).astype(jnp.bfloat16)
    return high, low


def rows_of(j, width):
    return slice(j * width, (j + 1) * width)


def put(a_ref, j, width, real, imag):
    real_high, real_low = split(real)
    imag_high, imag_low = split(imag)
    rows = rows_of(j, width)
    a_ref[rows, 0:width] = real_high
    a_ref[rows, width:2 * width] = imag_high
    a_ref[rows, 2 * width:3 * width] = real_low
    a_ref[rows, 3 * width:4 * width] = imag_low


def transform(a_ref, b_ref, tables, spots, width):
    right_high_ref, right_low_ref, left_high_ref, left_low_ref = tables
    half = jnp.dot(a_ref[...], right_high_ref[...], preferred_element_type=jnp.float32)
    half += jnp.dot(a_ref[:, :2 * width], right_low_ref[...], preferred_element_type=jnp.float32)
    for j in range(spots):
        rows = rows_of(j, width)
        real_high, real_low = split(half[rows, :width])
        imag_high, imag_low = split(half[rows, width:])
        b_ref[0:width, rows] = real_high
        b_ref[width:2 * width, rows] = imag_high
        b_ref[2 * width:3 * width, rows] = real_low
        b_ref[3 * width:4 * width, rows] = imag_low
    full = jnp.dot(left_high_ref[...], b_ref[...], preferred_element_type=jnp.float32)
    full += jnp.dot(left_low_ref[...], b_ref[:2 * width, :], preferred_element_type=jnp.float32)
    return [
        (full[:width, rows_of(j, width)], full[width:, rows_of(j, width)]) for j in range(spots)
    ]


def slice_of(ref, part):
    return ref.at[part] if len(ref.shape) == 4 else ref


def fill_ext(ext_ref, tile_ref, below_ref, upper_ref, lower_ref, corner_ref, width):
    tile_px = tile_ref.shape[1]
    blocks = tile_px // LANES
    for c in range(2):
        for b in range(blocks):
            lanes = slice(b * LANES, (b + 1) * LANES)
            ext_ref[c, b, :tile_px, :] = tile_ref[c, :, lanes]
            ext_ref[c, b, tile_px:, :] = below_ref[c, :, lanes]
        ext_ref[c, blocks, :width, :] = upper_ref[c]
        ext_ref[c, blocks, width:tile_px, :] = lower_ref[c]
        ext_ref[c, blocks, tile_px:, :] = corner_ref[c]


def place(scalar_ref, j):
    col = scalar_ref[2 * j + 1]
    return scalar_ref[2 * j], col // LANES, col % LANES


def window(ext_ref, c, spot, width, lane):
    row, block, shift = spot
    near = ext_ref[c, block, pl.ds(row, width), :]
    far = ext_ref[c, block + 1, pl.ds(row, width), :]
    return pltpu.roll(jnp.where(lane >= shift, near, far), LANES - shift, 1)


def scatter(grad_ref, c, spot, width, lane, used, update):
    row, block, shift = spot
    turned = pltpu.roll(jnp.where(used, update, 0.0), shift, 1)
    near = lane >= shift
    grad_ref[c, block, pl.ds(row, width), :] += jnp.where(near, turned, 0.0)
    grad_ref[c, block + 1, pl.ds(row, width), :] += jnp.where(near, 0.0, turned)


def emit(grad_ref, own_ref, down_ref, upper_ref, lower_ref, diag_ref, width):
    tile_px = own_ref.shape[1]
    blocks = tile_px // LANES
    for c in range(2):
        for b in range(blocks):
            lanes = slice(b * LANES, (b + 1) * LANES)
            own_ref[c, :, lanes] = grad_ref[c, b, :tile_px, :]
            down_ref[c, :, lanes] = grad_ref[c, b, tile_px:, :]
        upper_ref[c] = grad_ref[c, blocks, :width, :]
        lower_ref[c] = grad_ref[c, blocks, width:tile_px, :]
        diag_ref[c] = grad_ref[c, blocks, tile_px:, :]


def lanes_of(width):
    return lax.broadcasted_iota(jnp.int32, (width, LANES), 1)


def forward_kernel(
    scalar_ref, tile_ref, below_ref, upper_ref, lower_ref, corner_ref, probe_ref, prop_ref,
    rh_ref, rl_ref, lh_ref, ll_ref, moved_ref, ext_ref, a_ref, b_ref, *, spots, width, part,
):
    tables = (rh_ref, rl_ref, lh_ref, ll_ref)
    fill_ext(ext_ref, slice_of(tile_ref, part), below_ref, upper_ref, lower_ref, corner_ref, width)
    lane = lanes_of(width)
    for j in range(spots):
        spot = place(scalar_ref, j)
        real = window(ext_ref, 0, spot, width, lane)
        imag = window(ext_ref, 1, spot, width, lane)
        put(
            a_ref, j, width,
            probe_ref[0] * real - probe_ref[1] * imag,
            probe_ref[0] * imag + probe_ref[1] * real,
        )
    for j, (real, imag) in enumerate(transform(a_ref, b_ref, tables, spots, width)):
        put(
            a_ref, j, width,
            prop_ref[0] * real - prop_ref[1] * imag,
            -(prop_ref[0] * imag + prop_ref[1] * real),
        )
    for j, (real, negative) in enumerate(transform(a_ref, b_ref, tables, spots, width)):
        moved_ref[j, 0] = real
        moved_ref[j, 1] = -negative


def middle_kernel(
    scalar_ref, tile_ref, below_ref, upper_ref, lower_ref, corner_ref,
    moved_ref, amp_ref, rh_ref, rl_ref, lh_ref, ll_ref,
    own_ref, down_ref, up_out_ref, low_out_ref, diag_ref, back_ref,
    ext_ref, win_ref, a_ref, b_ref, *, spots, width, part,
):
    tables = (rh_ref, rl_ref, lh_ref, ll_ref)
    fill_ext(ext_ref, slice_of(tile_ref, part), below_ref, upper_ref, lower_ref, corner_ref, width)
    lane = lanes_of(width)
    total = scalar_ref[2 * spots]
    spot_list = [place(scalar_ref, j) for j in range(spots)]
    for j in range(spots):
        second_real = window(ext_ref, 0, spot_list[j], width, lane)
        second_imag = window(ext_ref, 1, spot_list[j], width, lane)
        win_ref[j, 0] = second_real
        win_ref[j, 1] = second_imag
        put(
            a_ref, j, width,
            moved_ref[j, 0] * second_real - moved_ref[j, 1] * second_imag,
            moved_ref[j, 0] * second_imag + moved_ref[j, 1] * second_real,
        )
    ext_ref[...] = jnp.zeros(ext_ref.shape, jnp.float32)
    for j, (real, imag) in enumerate(transform(a_ref, b_ref, tables, spots, width)):
        measured = amp_ref[scalar_ref[2 * spots + 1 + j]]
        power = jnp.maximum(real * real + imag * imag, floor_amp * floor_amp)
        factor = 1.0 - measured * lax.rsqrt(power)
        put(a_ref, j, width, real * factor, -(imag * factor))
    for j, (real, negative) in enumerate(transform(a_ref, b_ref, tables, spots, width)):
        imag = -negative
        used = j < total
        scatter(ext_ref, 0, spot_list[j], width, lane, used, moved_ref[j, 0] * real + moved_ref[j, 1] * imag)
        scatter(ext_ref, 1, spot_list[j], width, lane, used, moved_ref[j, 0] * imag - moved_ref[j, 1] * real)
        back_ref[j, 0] = win_ref[j, 0] * real + win_ref[j, 1] * imag
        back_ref[j, 1] = win_ref[j, 0] * imag - win_ref[j, 1] * real
    emit(ext_ref, own_ref, down_ref, up_out_ref, low_out_ref, diag_ref, width)


def backward_kernel(
    scalar_ref, back_ref, probe_ref, prop_ref, rh_ref, rl_ref, lh_ref, ll_ref,
    own_ref, down_ref, up_out_ref, low_out_ref, diag_ref,
    ext_ref, a_ref, b_ref, *, spots, width,
):
    tables = (rh_ref, rl_ref, lh_ref, ll_ref)
    lane = lanes_of(width)
    total = scalar_ref[2 * spots]
    for j in range(spots):
        put(a_ref, j, width, back_ref[j, 0], back_ref[j, 1])
    ext_ref[...] = jnp.zeros(ext_ref.shape, jnp.float32)
    for j, (real, imag) in enumerate(transform(a_ref, b_ref, tables, spots, width)):
        put(
            a_ref, j, width,
            prop_ref[0] * real + prop_ref[1] * imag,
            -(prop_ref[0] * imag - prop_ref[1] * real),
        )
    for j, (real, negative) in enumerate(transform(a_ref, b_ref, tables, spots, width)):
        imag = -negative
        spot = place(scalar_ref, j)
        used = j < total
        scatter(ext_ref, 0, spot, width, lane, used, probe_ref[0] * real + probe_ref[1] * imag)
        scatter(ext_ref, 1, spot, width, lane, used, probe_ref[0] * imag - probe_ref[1] * real)
    emit(ext_ref, own_ref, down_ref, up_out_ref, low_out_ref, diag_ref, width)


def folded(tile_ref, own_ref, above_ref, upper_ref, lower_ref, c, width):
    tile_px = own_ref.shape[1]
    top, low = slice(0, width), slice(width, tile_px)
    left, rest = slice(0, width), slice(width, tile_px)
    yield top, left, tile_ref[c, top, left] - step_size * (
        own_ref[c, top, left] + above_ref[c, :, left] + upper_ref[c]
    )
    yield top, rest, tile_ref[c, top, rest] - step_size * (own_ref[c, top, rest] + above_ref[c, :, rest])
    yield low, left, tile_ref[c, low, left] - step_size * (own_ref[c, low, left] + lower_ref[c])
    yield low, rest, tile_ref[c, low, rest] - step_size * own_ref[c, low, rest]


def update_kernel(
    tile_ref, own_ref, above_ref, upper_ref, lower_ref,
    new_ref, top_ref, left_up_ref, left_low_ref, *, width, part,
):
    tile_ref = slice_of(tile_ref, part)
    for c in range(2):
        for k, (rows, lanes, value) in enumerate(
            folded(tile_ref, own_ref, above_ref, upper_ref, lower_ref, c, width)
        ):
            new_ref[c, rows, lanes] = value
            if k < 2:
                top_ref[c, :, lanes] = value
            if k == 0:
                left_up_ref[c] = value
            if k == 2:
                left_low_ref[c] = value


def finish_kernel(*refs, width):
    out_ref = refs[-1]
    for s in range(2):
        for c in range(2):
            for rows, lanes, value in folded(*refs[5 * s:5 * s + 5], c, width):
                out_ref[s, c, rows, lanes] = value


F32 = functools.partial(jax.ShapeDtypeStruct, dtype=jnp.float32)
SMEM = pl.BlockSpec(memory_space=pltpu.SMEM)
VMEM = pl.BlockSpec(memory_space=pltpu.VMEM)
LIMIT = pltpu.CompilerParams(vmem_limit_bytes=16 * 1024 * 1024)


def call(kernel, scalars, arrays, outs, scratch, **static):
    return pl.pallas_call(
        functools.partial(kernel, **static),
        in_specs=[SMEM] * len(scalars) + [VMEM] * len(arrays),
        out_specs=[VMEM] * len(outs),
        out_shape=outs,
        scratch_shapes=scratch,
        compiler_params=LIMIT,
    )(*scalars, *arrays)


def pack_kernel(whole_ref, *refs, width):
    outs, sems = refs[:-1], refs[-1]
    tile_px = whole_ref.shape[2]
    copies = []
    for s in range(2):
        up, low, top = outs[3 * s:3 * s + 3]
        left = pl.ds(0, width)
        copies.append((whole_ref.at[s, :, pl.ds(0, width), left], up))
        copies.append((whole_ref.at[s, :, pl.ds(width, tile_px - width), left], low))
        copies.append((whole_ref.at[s, :, pl.ds(0, width), :], top))
    copies = [pltpu.make_async_copy(a, b, sems.at[k]) for k, (a, b) in enumerate(copies)]
    for copy in copies:
        copy.start()
    for copy in copies:
        copy.wait()


def body(
    specimen_slices,
    illumination_probe,
    propagation_phase,
    amplitudes,
    positions,
    counts,
    measurement_index,
):
    tile_px = specimen_slices.shape[2]
    width = illumination_probe.shape[1]
    spots = positions.shape[2]
    ext = tile_px + width
    tables = [jnp.asarray(t) for t in dft_operands(width)]
    prop = jnp.stack([jnp.cos(propagation_phase), jnp.sin(propagation_phase)])
    scalars = (jnp.concatenate([positions.reshape(-1), counts.reshape(-1), measurement_index.reshape(-1)]),)
    measured = amplitudes[0, 0]
    static = dict(spots=spots, width=width)
    ext_space = pltpu.VMEM((2, ext // LANES, ext, LANES), jnp.float32)
    work = [
        pltpu.VMEM((spots * width, 4 * width), jnp.bfloat16),
        pltpu.VMEM((4 * width, spots * width), jnp.bfloat16),
    ]
    wave = F32((spots, 2, width, width))
    square = F32((2, width, width))
    whole = F32((2, tile_px, tile_px))
    strip = F32((2, width, tile_px))
    gradient = [whole, strip, square, square, square]

    def halo(left_up, left_low, top):
        upper = from_behind(left_up, "col", -1)
        lower = from_behind(left_low, "col", -1)
        below = from_behind(top, "row", -1)
        corner = from_behind(upper, "row", -1)
        return below, upper, lower, corner

    def fold(own, down, side_up, side_low, diag):
        corner = from_behind(diag, "row", 1)
        lower = from_behind(side_low, "col", 1)
        above = from_behind(down, "row", 1)
        upper = from_behind(side_up + corner, "col", 1)
        return own, above, upper, lower

    packed = pl.pallas_call(
        functools.partial(pack_kernel, width=width),
        in_specs=[pl.BlockSpec(memory_space=pl.ANY)],
        out_specs=[VMEM] * 6,
        out_shape=[square, square, strip] * 2,
        scratch_shapes=[pltpu.SemaphoreType.DMA((6,))],
        compiler_params=LIMIT,
        name="pack",
    )(specimen_slices)
    tiles = [specimen_slices, specimen_slices]
    sends = [packed[:3], packed[3:]]
    for i in range(ITERS):
        halo_one = halo(*sends[0])
        halo_two = halo(*sends[1])
        (moved,) = call(
            forward_kernel, scalars, (tiles[0], *halo_one, illumination_probe, prop, *tables),
            [wave], [ext_space, *work], part=0, **static,
        )
        *grad_two, back = call(
            middle_kernel, scalars, (tiles[1], *halo_two, moved, measured, *tables),
            [*gradient, wave], [ext_space, pltpu.VMEM((spots, 2, width, width), jnp.float32), *work],
            part=1, **static,
        )
        fold_two = fold(*grad_two)
        grad_one = call(
            backward_kernel, scalars, (back, illumination_probe, prop, *tables),
            gradient, [ext_space, *work], **static,
        )
        fold_one = fold(*grad_one)
        if i + 1 < ITERS:
            fresh, sends = [], []
            for part, (tile, received) in enumerate(zip(tiles, (fold_one, fold_two))):
                new, top, left_up, left_low = call(
                    update_kernel, (), (tile, *received), [whole, strip, square, square], [],
                    width=width, part=part,
                )
                fresh.append(new)
                sends.append((left_up, left_low, top))
            tiles = fresh
        else:
            (updated,) = call(
                finish_kernel, (), (tiles[0], *fold_one, tiles[1], *fold_two),
                [F32(specimen_slices.shape)], [], width=width,
            )
    return updated


def solution(mesh):
    placed = (
        P(None, None, "row", "col"),
        P(),
        P(),
        P("row", "col", None, None, None),
        P("row", "col", None, None),
        P("row", "col"),
        P("row", "col", None),
    )

    return jax.shard_map(
        body, mesh=mesh, in_specs=placed, out_specs=P(None, None, "row", "col"), check_vma=False
    )
```

```python
import functools
import math

import jax
import jax.numpy as jnp
import ml_dtypes
import numpy as np
from jax import lax
from jax.experimental import pallas as pl
from jax.experimental.pallas import tpu as pltpu
from jax.sharding import PartitionSpec as P

ITERS = 2
LANES = 128

step_size = 0.02
floor_amp = 0.5


def from_behind(block, axis, distance):
    devices = range(lax.axis_size(axis))
    route = [((i - distance) % len(devices), i) for i in devices]
    return lax.ppermute(block, axis, route)


def two_parts(value):
    high = value.astype(ml_dtypes.bfloat16)
    low = (value - high.astype(np.float64)).astype(ml_dtypes.bfloat16)
    return high, low


def dft_operands(width):
    index = np.arange(width)
    angle = (index[:, None] * index[None, :] % width) * (2.0 * math.pi / width)
    real = np.cos(angle) / math.sqrt(width)
    imag = -np.sin(angle) / math.sqrt(width)
    right = np.block([[real, imag], [-imag, real]])
    right_high, right_low = two_parts(right)
    left_high, left_low = two_parts(right.T)
    return np.stack([right_high, right_low, left_high, left_low])


def split(value):
    high = value.astype(jnp.bfloat16)
    low = (value - high.astype(jnp.float32)).astype(jnp.bfloat16)
    return high, low


def rows_of(j, width):
    return slice(j * width, (j + 1) * width)


def put(a_ref, j, width, real, imag):
    real_high, real_low = split(real)
    imag_high, imag_low = split(imag)
    rows = rows_of(j, width)
    a_ref[rows, 0:width] = real_high
    a_ref[rows, width:2 * width] = imag_high
    a_ref[rows, 2 * width:3 * width] = real_low
    a_ref[rows, 3 * width:4 * width] = imag_low


def product(left, right):
    return jnp.dot(left, right, preferred_element_type=jnp.float32)


def transform(a_ref, b_ref, table_ref, spots, width):
    both = 2 * width
    half = product(a_ref[:, :both], table_ref[0]) + product(a_ref[:, both:], table_ref[0])
    half += product(a_ref[:, :both], table_ref[1])
    for j in range(spots):
        rows = rows_of(j, width)
        real_high, real_low = split(half[rows, :width])
        imag_high, imag_low = split(half[rows, width:])
        b_ref[0:width, rows] = real_high
        b_ref[width:2 * width, rows] = imag_high
        b_ref[2 * width:3 * width, rows] = real_low
        b_ref[3 * width:4 * width, rows] = imag_low
    full = product(table_ref[2], b_ref[:both, :]) + product(table_ref[2], b_ref[both:, :])
    full += product(table_ref[3], b_ref[:both, :])
    return [
        (full[:width, rows_of(j, width)], full[width:, rows_of(j, width)]) for j in range(spots)
    ]


def fill_ext(ext_ref, tile_ref, below_ref, upper_ref, lower_ref, corner_ref, width):
    tile_px = tile_ref.shape[1]
    blocks = tile_px // LANES
    for c in range(2):
        for b in range(blocks):
            lanes = slice(b * LANES, (b + 1) * LANES)
            ext_ref[c, b, :tile_px, :] = tile_ref[c, :, lanes]
            ext_ref[c, b, tile_px:, :] = below_ref[c, :, lanes]
        ext_ref[c, blocks, :width, :] = upper_ref[c]
        ext_ref[c, blocks, width:tile_px, :] = lower_ref[c]
        ext_ref[c, blocks, tile_px:, :] = corner_ref[c]


def place(scalar_ref, j):
    col = scalar_ref[2 * j + 1]
    return scalar_ref[2 * j], col // LANES, col % LANES


def window(ext_ref, c, spot, width, lane):
    row, block, shift = spot
    near = ext_ref[c, block, pl.ds(row, width), :]
    far = ext_ref[c, block + 1, pl.ds(row, width), :]
    return pltpu.roll(jnp.where(lane >= shift, near, far), LANES - shift, 1)


def scatter(grad_ref, c, spot, width, lane, used, update):
    row, block, shift = spot
    turned = pltpu.roll(jnp.where(used, update, 0.0), shift, 1)
    near = lane >= shift
    grad_ref[c, block, pl.ds(row, width), :] += jnp.where(near, turned, 0.0)
    grad_ref[c, block + 1, pl.ds(row, width), :] += jnp.where(near, 0.0, turned)


def emit(grad_ref, own_ref, down_ref, upper_ref, lower_ref, diag_ref, width):
    tile_px = own_ref.shape[1]
    blocks = tile_px // LANES
    for c in range(2):
        for b in range(blocks):
            lanes = slice(b * LANES, (b + 1) * LANES)
            own_ref[c, :, lanes] = grad_ref[c, b, :tile_px, :]
            down_ref[c, :, lanes] = grad_ref[c, b, tile_px:, :]
        upper_ref[c] = grad_ref[c, blocks, :width, :]
        lower_ref[c] = grad_ref[c, blocks, width:tile_px, :]
        diag_ref[c] = grad_ref[c, blocks, tile_px:, :]


def lanes_of(width):
    return lax.broadcasted_iota(jnp.int32, (width, LANES), 1)


def views(refs, s):
    picked = []
    for ref in refs:
        if isinstance(ref, (list, tuple)):
            picked.append(ref[s])
        elif len(ref.shape) == 4:
            picked.append(ref.at[s])
        else:
            picked.append(ref.at[pl.ds(2 * s, 2)])
    return picked


def paired(refs, kinds):
    refs = list(refs)
    return [refs.pop(0) if kind == 1 else (refs.pop(0), refs.pop(0)) for kind in kinds]


def fetch(far_refs, near_refs, sems):
    copies = [
        pltpu.make_async_copy(far, near, sems.at[k])
        for k, (far, near) in enumerate(zip(far_refs, near_refs))
    ]
    for copy in copies:
        copy.start()
    return copies


def wave_kernel(*refs, spots, width, kinds):
    count = 1 + sum(kinds)
    scalar_ref, halo_refs, rest = refs[0], paired(refs[1:count], kinds), refs[count:]
    prop_ref, *far = rest[:4]
    own_ref, down_ref, up_out_ref, low_out_ref, diag_ref, back_ref = rest[4:10]
    ext_ref, win_ref, moved_ref, a_ref, b_ref, *near, sems = rest[10:]
    fetches = fetch(far, near, sems)
    probe_ref, amp_ref, table_ref = near
    lane = lanes_of(width)
    total = scalar_ref[2 * spots]
    spot_list = [place(scalar_ref, j) for j in range(spots)]
    fill_ext(ext_ref, *views(halo_refs, 0), width)
    for fetched in fetches:
        fetched.wait()
    for j in range(spots):
        real = window(ext_ref, 0, spot_list[j], width, lane)
        imag = window(ext_ref, 1, spot_list[j], width, lane)
        put(
            a_ref, j, width,
            probe_ref[0] * real - probe_ref[1] * imag,
            probe_ref[0] * imag + probe_ref[1] * real,
        )
    fill_ext(ext_ref, *views(halo_refs, 1), width)
    for j in range(spots):
        win_ref[j, 0] = window(ext_ref, 0, spot_list[j], width, lane)
        win_ref[j, 1] = window(ext_ref, 1, spot_list[j], width, lane)
    for j, (real, imag) in enumerate(transform(a_ref, b_ref, table_ref, spots, width)):
        put(
            a_ref, j, width,
            prop_ref[0] * real - prop_ref[1] * imag,
            -(prop_ref[0] * imag + prop_ref[1] * real),
        )
    for j, (real, negative) in enumerate(transform(a_ref, b_ref, table_ref, spots, width)):
        imag = -negative
        moved_ref[j, 0] = real
        moved_ref[j, 1] = imag
        put(
            a_ref, j, width,
            real * win_ref[j, 0] - imag * win_ref[j, 1],
            real * win_ref[j, 1] + imag * win_ref[j, 0],
        )
    ext_ref[...] = jnp.zeros(ext_ref.shape, jnp.float32)
    for j, (real, imag) in enumerate(transform(a_ref, b_ref, table_ref, spots, width)):
        measured = amp_ref[scalar_ref[2 * spots + 1 + j]]
        power = jnp.maximum(real * real + imag * imag, floor_amp * floor_amp)
        factor = 1.0 - measured * lax.rsqrt(power)
        put(a_ref, j, width, real * factor, -(imag * factor))
    for j, (real, negative) in enumerate(transform(a_ref, b_ref, table_ref, spots, width)):
        imag = -negative
        used = j < total
        scatter(ext_ref, 0, spot_list[j], width, lane, used, moved_ref[j, 0] * real + moved_ref[j, 1] * imag)
        scatter(ext_ref, 1, spot_list[j], width, lane, used, moved_ref[j, 0] * imag - moved_ref[j, 1] * real)
        back_ref[j, 0] = win_ref[j, 0] * real + win_ref[j, 1] * imag
        back_ref[j, 1] = win_ref[j, 0] * imag - win_ref[j, 1] * real
    emit(ext_ref, own_ref, down_ref, up_out_ref, low_out_ref, diag_ref, width)


def backward_kernel(
    scalar_ref, back_ref, other_down_ref, prop_ref, probe_far_ref, table_far_ref,
    own_ref, down_ref, up_out_ref, low_out_ref, diag_ref,
    ext_ref, a_ref, b_ref, probe_ref, table_ref, sems, *, spots, width,
):
    fetches = fetch((probe_far_ref, table_far_ref), (probe_ref, table_ref), sems)
    lane = lanes_of(width)
    total = scalar_ref[2 * spots]
    for j in range(spots):
        put(a_ref, j, width, back_ref[j, 0], back_ref[j, 1])
    ext_ref[...] = jnp.zeros(ext_ref.shape, jnp.float32)
    down_ref[2:] = other_down_ref[...]
    for fetched in fetches:
        fetched.wait()
    for j, (real, imag) in enumerate(transform(a_ref, b_ref, table_ref, spots, width)):
        put(
            a_ref, j, width,
            prop_ref[0] * real + prop_ref[1] * imag,
            -(prop_ref[0] * imag - prop_ref[1] * real),
        )
    for j, (real, negative) in enumerate(transform(a_ref, b_ref, table_ref, spots, width)):
        imag = -negative
        spot = place(scalar_ref, j)
        used = j < total
        scatter(ext_ref, 0, spot, width, lane, used, probe_ref[0] * real + probe_ref[1] * imag)
        scatter(ext_ref, 1, spot, width, lane, used, probe_ref[0] * imag - probe_ref[1] * real)
    emit(ext_ref, own_ref, down_ref, up_out_ref, low_out_ref, diag_ref, width)


def folded(tile_ref, own_ref, above_ref, upper_ref, lower_ref, c, width):
    tile_px = own_ref.shape[1]
    top, low = slice(0, width), slice(width, tile_px)
    left, rest = slice(0, width), slice(width, tile_px)
    yield top, left, tile_ref[c, top, left] - step_size * (
        own_ref[c, top, left] + above_ref[c, :, left] + upper_ref[c]
    )
    yield top, rest, tile_ref[c, top, rest] - step_size * (own_ref[c, top, rest] + above_ref[c, :, rest])
    yield low, left, tile_ref[c, low, left] - step_size * (own_ref[c, low, left] + lower_ref[c])
    yield low, rest, tile_ref[c, low, rest] - step_size * own_ref[c, low, rest]


def update_second_kernel(
    tile_ref, own_ref, above_ref, upper_ref, lower_ref, new_ref, left_up_ref, *, width,
):
    tile_ref, above_ref = views((tile_ref, above_ref), 1)
    for c in range(2):
        for k, (rows, lanes, value) in enumerate(
            folded(tile_ref, own_ref, above_ref, upper_ref, lower_ref, c, width)
        ):
            new_ref[c, rows, lanes] = value
            if k == 0:
                left_up_ref[c] = value


def update_first_kernel(
    tile_ref, own_ref, above_ref, upper_ref, lower_ref, second_ref,
    new_ref, left_up_ref, left_low_ref, top_ref, *, width,
):
    tile_ref, above_ref = views((tile_ref, above_ref), 0)
    for c in range(2):
        for k, (rows, lanes, value) in enumerate(
            folded(tile_ref, own_ref, above_ref, upper_ref, lower_ref, c, width)
        ):
            new_ref[c, rows, lanes] = value
            if k < 2:
                top_ref[c, :, lanes] = value
            if k == 0:
                left_up_ref[c] = value
            if k == 2:
                left_low_ref[c] = value
        top_ref[2 + c] = second_ref[c, :width, :]
        left_low_ref[2 + c] = second_ref[c, width:, :width]


def finish_kernel(first_ref, second_ref, own_one, own_two, above_ref, up_one, up_two, low_one, low_two, out_ref, *, width):
    refs = ((first_ref, second_ref), (own_one, own_two), above_ref, (up_one, up_two), (low_one, low_two))
    for s in (1, 0):
        for c in range(2):
            for rows, lanes, value in folded(*views(refs, s), c, width):
                out_ref[s, c, rows, lanes] = value


F32 = functools.partial(jax.ShapeDtypeStruct, dtype=jnp.float32)
SMEM = pl.BlockSpec(memory_space=pltpu.SMEM)
VMEM = pl.BlockSpec(memory_space=pltpu.VMEM)
LIMIT = pltpu.CompilerParams(vmem_limit_bytes=16 * 1024 * 1024)


FAR = pl.BlockSpec(memory_space=pltpu.MemorySpace.HBM)


def call(kernel, scalars, arrays, outs, scratch, far=(), **static):
    fetched = [pltpu.VMEM(x.shape, x.dtype) for x in far]
    if far:
        fetched.append(pltpu.SemaphoreType.DMA((len(far),)))
    return pl.pallas_call(
        functools.partial(kernel, **static),
        in_specs=[SMEM] * len(scalars) + [VMEM] * len(arrays) + [FAR] * len(far),
        out_specs=[VMEM] * len(outs),
        out_shape=outs,
        scratch_shapes=[*scratch, *fetched],
        compiler_params=LIMIT,
    )(*scalars, *arrays, *far)


def pack_kernel(whole_ref, up_ref, low_ref, top_ref, sems, *, width):
    tile_px = whole_ref.shape[2]
    left = pl.ds(0, width)
    copies = []
    for s in range(2):
        both = pl.ds(2 * s, 2)
        copies.append((whole_ref.at[s, :, pl.ds(0, width), left], up_ref.at[both]))
        copies.append((whole_ref.at[s, :, pl.ds(width, tile_px - width), left], low_ref.at[both]))
        copies.append((whole_ref.at[s, :, pl.ds(0, width), :], top_ref.at[both]))
    copies = [pltpu.make_async_copy(a, b, sems.at[k]) for k, (a, b) in enumerate(copies)]
    for copy in copies:
        copy.start()
    for copy in copies:
        copy.wait()


def in_hbm(array):
    return pltpu.with_memory_space_constraint(array, pltpu.MemorySpace.HBM)


def body(
    specimen_slices,
    illumination_probe,
    propagation_phase,
    amplitudes,
    positions,
    counts,
    measurement_index,
):
    tile_px = specimen_slices.shape[2]
    width = illumination_probe.shape[1]
    spots = positions.shape[2]
    ext = tile_px + width
    table = in_hbm(jnp.asarray(dft_operands(width)))
    probe = in_hbm(illumination_probe)
    prop = jnp.stack([jnp.cos(propagation_phase), jnp.sin(propagation_phase)])
    scalars = (jnp.concatenate([positions.reshape(-1), counts.reshape(-1), measurement_index.reshape(-1)]),)
    measured = in_hbm(amplitudes[0, 0])
    static = dict(spots=spots, width=width)
    ext_space = pltpu.VMEM((2, ext // LANES, ext, LANES), jnp.float32)
    work = [
        pltpu.VMEM((spots * width, 4 * width), jnp.bfloat16),
        pltpu.VMEM((4 * width, spots * width), jnp.bfloat16),
    ]
    wave = F32((spots, 2, width, width))
    square = F32((2, width, width))
    squares = F32((4, width, width))
    whole = F32((2, tile_px, tile_px))
    strip = F32((2, width, tile_px))
    strips = F32((4, width, tile_px))
    wave_space = pltpu.VMEM((spots, 2, width, width), jnp.float32)

    def add_and_send(block, corner):
        return from_behind(block + corner, "col", 1)

    left_up, left_low, top = pl.pallas_call(
        functools.partial(pack_kernel, width=width),
        in_specs=[FAR],
        out_specs=[VMEM] * 3,
        out_shape=[squares, squares, strips],
        scratch_shapes=[pltpu.SemaphoreType.DMA((6,))],
        compiler_params=LIMIT,
        name="pack",
    )(in_hbm(specimen_slices))
    upper = from_behind(left_up, "col", -1)
    lower = from_behind(left_low, "col", -1)
    below = from_behind(top, "row", -1)
    corner = from_behind(upper, "row", -1)
    halo, kinds = [specimen_slices, below, upper, lower, corner], (1, 1, 1, 1, 1)
    tiles = (specimen_slices,)
    for i in range(ITERS):
        own_two, down_two, up_two, low_two, diag_two, back = call(
            wave_kernel, scalars, (*halo, prop),
            [whole, strip, square, square, square, wave],
            [ext_space, wave_space, wave_space, *work],
            far=(probe, measured, table), kinds=kinds, **static,
        )
        corner_two = from_behind(diag_two, "row", 1)
        low_two = from_behind(low_two, "col", 1)
        own_one, down, up_one, low_one, diag_one = call(
            backward_kernel, scalars, (back, down_two, prop),
            [whole, strips, square, square, square], [ext_space, *work],
            far=(probe, table), **static,
        )
        low_one = from_behind(low_one, "col", 1)
        corner_one = from_behind(diag_one, "row", 1)
        above = from_behind(down, "row", 1)
        up_two = add_and_send(up_two, corner_two)
        up_one = add_and_send(up_one, corner_one)
        if i + 1 < ITERS:
            second, left_up_two = call(
                update_second_kernel, (), (tiles[-1], own_two, above, up_two, low_two),
                [whole, square], [], width=width,
            )
            upper_two = from_behind(left_up_two, "col", -1)
            first, left_up_one, left_low, top = call(
                update_first_kernel, (), (tiles[0], own_one, above, up_one, low_one, second),
                [whole, square, squares, strips], [], width=width,
            )
            upper_one = from_behind(left_up_one, "col", -1)
            lower = from_behind(left_low, "col", -1)
            below = from_behind(top, "row", -1)
            corner_one = from_behind(upper_one, "row", -1)
            corner_two = from_behind(upper_two, "row", -1)
            tiles = (first, second)
            halo = [*tiles, below, upper_one, upper_two, lower, corner_one, corner_two]
            kinds = (2, 1, 2, 1, 2)
        else:
            (updated,) = call(
                finish_kernel, (),
                (*tiles, own_one, own_two, above, up_one, up_two, low_one, low_two),
                [F32(specimen_slices.shape)], [], width=width,
            )
    return updated


def solution(mesh):
    placed = (
        P(None, None, "row", "col"),
        P(),
        P(),
        P("row", "col", None, None, None),
        P("row", "col", None, None),
        P("row", "col"),
        P("row", "col", None),
    )

    return jax.shard_map(
        body, mesh=mesh, in_specs=placed, out_specs=P(None, None, "row", "col"), check_vma=False
    )
```

```python
import functools
import math

import jax
import jax.numpy as jnp
import ml_dtypes
import numpy as np
from jax import lax
from jax.experimental import pallas as pl
from jax.experimental.pallas import tpu as pltpu
from jax.sharding import PartitionSpec as P


ITERS = 2
LANES = 128

step_size = 0.02
floor_amp = 0.5


def send_corner(block, distance):
    count = lax.axis_size("row")
    route = [(i, i + distance) for i in range(count) if 0 <= i + distance < count]
    return lax.ppermute(block, "row", route)


def send_wrap(block, distance):
    rows, cols = lax.axis_size("row"), lax.axis_size("col")
    start, end = (rows - 1, 0) if distance > 0 else (0, rows - 1)
    route = [(start * cols + c, end * cols + (c + distance) % cols) for c in range(cols)]
    return lax.ppermute(block, ("row", "col"), route)


def from_behind(block, axis, distance):
    devices = range(lax.axis_size(axis))
    route = [((i - distance) % len(devices), i) for i in devices]
    return lax.ppermute(block, axis, route)


def two_parts(value):
    high = value.astype(ml_dtypes.bfloat16)
    low = (value - high.astype(np.float64)).astype(ml_dtypes.bfloat16)
    return high, low


def dft_operands(width):
    index = np.arange(width)
    angle = (index[:, None] * index[None, :] % width) * (2.0 * math.pi / width)
    real = np.cos(angle) / math.sqrt(width)
    imag = -np.sin(angle) / math.sqrt(width)
    right = np.block([[real, imag], [-imag, real]])
    right_high, right_low = two_parts(right)
    left_high, left_low = two_parts(right.T)
    return np.stack([right_high, right_low, left_high, left_low])


def split(value):
    high = value.astype(jnp.bfloat16)
    low = (value - high.astype(jnp.float32)).astype(jnp.bfloat16)
    return high, low


def rows_of(j, width):
    return slice(j * width, (j + 1) * width)


def product(left, right):
    return jnp.dot(left, right, preferred_element_type=jnp.float32)


def right_side(pairs, table_ref):
    high, low = split(jnp.concatenate([jnp.concatenate(pair, 1) for pair in pairs], 0))
    return product(high, table_ref[0]) + product(low, table_ref[0]) + product(high, table_ref[1])


def left_side(half, table_ref, width):
    count = half.shape[0] // width
    parts = [half[rows_of(k, width)] for k in range(count)]
    tall = [jnp.concatenate([part[:, :width], part[:, width:]], 0) for part in parts]
    high, low = split(jnp.concatenate(tall, 1))
    full = product(table_ref[2], high) + product(table_ref[2], low) + product(table_ref[3], high)
    return [(full[:width, rows_of(k, width)], full[width:, rows_of(k, width)]) for k in range(count)]


def interleave(chains, lag):
    waiting = [(n * lag, chain) for n, chain in enumerate(chains)]
    while waiting:
        after = []
        for delay, chain in waiting:
            if delay:
                after.append((delay - 1, chain))
            elif next(chain, None) is not None:
                after.append((0, chain))
        waiting = after


def fill_ext(ext_ref, pieces):
    for row, col, *sources in pieces:
        height, across = sources[0].shape[1:]
        for c in range(2):
            for b in range(across // LANES):
                lanes = slice(b * LANES, (b + 1) * LANES)
                value = sources[0][c, :, lanes]
                for source in sources[1:]:
                    value += source[c, :, lanes]
                ext_ref[c, col // LANES + b, row:row + height, :] = value


def place(scalar_ref, j):
    col = scalar_ref[2 * j + 1]
    return scalar_ref[2 * j], col // LANES, col % LANES


def window(ext_ref, c, spot, width, lane):
    row, block, shift = spot
    near = ext_ref[c, block, pl.ds(row, width), :]
    far = ext_ref[c, block + 1, pl.ds(row, width), :]
    return pltpu.roll(jnp.where(lane >= shift, near, far), LANES - shift, 1)


def scatter(grad_ref, c, spot, width, lane, used, update):
    row, block, shift = spot
    turned = pltpu.roll(jnp.where(used, update, 0.0), shift, 1)
    near = lane >= shift
    grad_ref[c, block, pl.ds(row, width), :] += jnp.where(near, turned, 0.0)
    grad_ref[c, block + 1, pl.ds(row, width), :] += jnp.where(near, 0.0, turned)


def emit(grad_ref, own_ref, down_ref, upper_ref, lower_ref, diag_ref, width):
    tile_px = own_ref.shape[1]
    blocks = tile_px // LANES
    for c in range(2):
        for b in range(blocks):
            lanes = slice(b * LANES, (b + 1) * LANES)
            own_ref[c, :, lanes] = grad_ref[c, b, :tile_px, :]
            down_ref[c, :, lanes] = grad_ref[c, b, tile_px:, :]
        upper_ref[c] = grad_ref[c, blocks, :width, :]
        lower_ref[c] = grad_ref[c, blocks, width:tile_px, :]
        diag_ref[c] = grad_ref[c, blocks, tile_px:, :]


def lanes_of(width):
    return lax.broadcasted_iota(jnp.int32, (width, LANES), 1)


LAG = 1


def groups_of(spots):
    return [range(j, min(j + 2, spots)) for j in range(0, spots, 2)]


def forward_steps(group, enter_ref, leave_ref, cos_ref, sin_ref, table_ref, width):
    half = right_side([(enter_ref[j, 0], enter_ref[j, 1]) for j in group], table_ref)
    yield True
    pairs = left_side(half, table_ref, width)
    yield True
    half = right_side([
        (cos_ref[...] * real - sin_ref[...] * imag, -(cos_ref[...] * imag + sin_ref[...] * real))
        for real, imag in pairs
    ], table_ref)
    yield True
    pairs = left_side(half, table_ref, width)
    yield True
    for j, (real, negative) in zip(group, pairs):
        leave_ref[j, 0] = real
        leave_ref[j, 1] = -negative


def residual_steps(group, moved_ref, win_ref, measured_of, finish, table_ref, width):
    half = right_side([
        (
            moved_ref[j, 0] * win_ref[j, 0] - moved_ref[j, 1] * win_ref[j, 1],
            moved_ref[j, 0] * win_ref[j, 1] + moved_ref[j, 1] * win_ref[j, 0],
        )
        for j in group
    ], table_ref)
    yield True
    pairs = left_side(half, table_ref, width)
    yield True
    residuals = []
    for j, (real, imag) in zip(group, pairs):
        power = jnp.maximum(real * real + imag * imag, floor_amp * floor_amp)
        factor = 1.0 - measured_of(j) * lax.rsqrt(power)
        residuals.append((real * factor, -(imag * factor)))
    half = right_side(residuals, table_ref)
    yield True
    pairs = left_side(half, table_ref, width)
    yield True
    for j, (real, negative) in zip(group, pairs):
        finish(j, real, -negative)


def joined(*parts):
    for part in parts:
        yield from part


def whole_pieces(refs, s, tile_px, width):
    tile_ref, below_ref, upper_ref, lower_ref, corner_ref, wrapped_ref = refs
    both = pl.ds(2 * s, 2)
    return [
        (0, 0, tile_ref.at[s]),
        (tile_px, 0, below_ref.at[both]),
        (0, tile_px, upper_ref.at[both]),
        (width, tile_px, lower_ref.at[both]),
        (tile_px, tile_px, corner_ref.at[both], wrapped_ref.at[both]),
    ]


def slice_pieces(refs, s, tile_px, width):
    (
        rest_ref, quad_ref, below_left_ref, below_right_ref, upper_ref, lower_ref, corner_ref, wrapped_ref,
    ) = refs
    both = pl.ds(2 * s, 2)
    across = tile_px - width
    return [
        (width, 0, rest_ref.at[:, pl.ds(width, across), :]),
        (0, width, rest_ref.at[:, pl.ds(0, width), pl.ds(width, across)]),
        (0, 0, quad_ref),
        (tile_px, 0, below_left_ref.at[both]),
        (tile_px, width, below_right_ref.at[both]),
        (0, tile_px, upper_ref),
        (width, tile_px, lower_ref),
        (tile_px, tile_px, corner_ref, wrapped_ref.at[both]),
    ]


def take_windows(ext_ref, spot_list, win_ref, width, lane):
    for j, spot in enumerate(spot_list):
        win_ref[j, 0] = window(ext_ref, 0, spot, width, lane)
        win_ref[j, 1] = window(ext_ref, 1, spot, width, lane)


def light(ext_ref, spot_list, probe_ref, enter_ref, width, lane):
    for j, spot in enumerate(spot_list):
        real = window(ext_ref, 0, spot, width, lane)
        imag = window(ext_ref, 1, spot, width, lane)
        enter_ref[j, 0] = probe_ref[0] * real - probe_ref[1] * imag
        enter_ref[j, 1] = probe_ref[0] * imag + probe_ref[1] * real


def residual_end(scalar_ref, spots, spot_list, ext_ref, moved_ref, win_ref, back_ref, width, lane):
    total = scalar_ref[2 * spots]

    def finish(j, real, imag):
        used = j < total
        scatter(ext_ref, 0, spot_list[j], width, lane, used, moved_ref[j, 0] * real + moved_ref[j, 1] * imag)
        scatter(ext_ref, 1, spot_list[j], width, lane, used, moved_ref[j, 0] * imag - moved_ref[j, 1] * real)
        back_ref[j, 0] = win_ref[j, 0] * real + win_ref[j, 1] * imag
        back_ref[j, 1] = win_ref[j, 0] * imag - win_ref[j, 1] * real

    return finish


def wave_kernel(
    scalar_ref, tile_ref, below_ref, upper_ref, lower_ref, corner_ref, wrapped_ref,
    cos_ref, sin_ref, probe_ref, amp_ref, table_ref,
    own_ref, down_ref, up_out_ref, low_out_ref, diag_ref, back_ref,
    ext_ref, win_ref, moved_ref, *, spots, width,
):
    lane = lanes_of(width)
    tile_px = own_ref.shape[1]
    spot_list = [place(scalar_ref, j) for j in range(spots)]
    halo = (tile_ref, below_ref, upper_ref, lower_ref, corner_ref, wrapped_ref)
    fill_ext(ext_ref, whole_pieces(halo, 0, tile_px, width))
    light(ext_ref, spot_list, probe_ref, back_ref, width, lane)
    fill_ext(ext_ref, whole_pieces(halo, 1, tile_px, width))
    take_windows(ext_ref, spot_list, win_ref, width, lane)
    ext_ref[...] = jnp.zeros(ext_ref.shape, jnp.float32)
    finish = residual_end(scalar_ref, spots, spot_list, ext_ref, moved_ref, win_ref, back_ref, width, lane)
    interleave([
        joined(
            forward_steps(group, back_ref, moved_ref, cos_ref, sin_ref, table_ref, width),
            residual_steps(
                group, moved_ref, win_ref, lambda j: amp_ref[scalar_ref[2 * spots + 1 + j]],
                finish, table_ref, width,
            ),
        )
        for group in groups_of(spots)
    ], LAG)
    emit(ext_ref, own_ref, down_ref, up_out_ref, low_out_ref, diag_ref, width)


def forward_kernel(
    scalar_ref, rest_ref, quad_ref, left_ref, right_ref, upper_ref, lower_ref, corner_ref, wrapped_ref,
    cos_ref, sin_ref, probe_ref, table_ref, moved_ref, ext_ref, enter_ref, *, spots, width,
):
    lane = lanes_of(width)
    spot_list = [place(scalar_ref, j) for j in range(spots)]
    halo = (rest_ref, quad_ref, left_ref, right_ref, upper_ref, lower_ref, corner_ref, wrapped_ref)
    fill_ext(ext_ref, slice_pieces(halo, 0, rest_ref.shape[1], width))
    light(ext_ref, spot_list, probe_ref, enter_ref, width, lane)
    interleave([
        forward_steps(group, enter_ref, moved_ref, cos_ref, sin_ref, table_ref, width)
        for group in groups_of(spots)
    ], LAG)


def residual_kernel(
    scalar_ref, rest_ref, quad_ref, left_ref, right_ref, upper_ref, lower_ref, corner_ref, wrapped_ref,
    moved_ref, amp_ref, table_ref,
    own_ref, down_ref, up_out_ref, low_out_ref, diag_ref, back_ref,
    ext_ref, win_ref, *, spots, width,
):
    lane = lanes_of(width)
    spot_list = [place(scalar_ref, j) for j in range(spots)]
    halo = (rest_ref, quad_ref, left_ref, right_ref, upper_ref, lower_ref, corner_ref, wrapped_ref)
    fill_ext(ext_ref, slice_pieces(halo, 1, rest_ref.shape[1], width))
    take_windows(ext_ref, spot_list, win_ref, width, lane)
    ext_ref[...] = jnp.zeros(ext_ref.shape, jnp.float32)
    finish = residual_end(scalar_ref, spots, spot_list, ext_ref, moved_ref, win_ref, back_ref, width, lane)
    interleave([
        residual_steps(
            group, moved_ref, win_ref, lambda j: amp_ref[scalar_ref[2 * spots + 1 + j]],
            finish, table_ref, width,
        )
        for group in groups_of(spots)
    ], LAG)
    emit(ext_ref, own_ref, down_ref, up_out_ref, low_out_ref, diag_ref, width)


def backward_kernel(
    scalar_ref, back_ref, other_diag_ref, cos_ref, sin_ref, probe_ref, table_ref,
    own_ref, down_ref, up_out_ref, low_out_ref, diag_ref, diags_ref, ext_ref, *, spots, width,
):
    lane = lanes_of(width)
    total = scalar_ref[2 * spots]
    ext_ref[...] = jnp.zeros(ext_ref.shape, jnp.float32)

    def chain(group):
        half = right_side([(back_ref[j, 0], back_ref[j, 1]) for j in group], table_ref)
        yield True
        pairs = left_side(half, table_ref, width)
        yield True
        half = right_side([
            (cos_ref[...] * real + sin_ref[...] * imag, -(cos_ref[...] * imag - sin_ref[...] * real))
            for real, imag in pairs
        ], table_ref)
        yield True
        pairs = left_side(half, table_ref, width)
        yield True
        for j, (real, negative) in zip(group, pairs):
            imag = -negative
            spot = place(scalar_ref, j)
            used = j < total
            scatter(ext_ref, 0, spot, width, lane, used, probe_ref[0] * real + probe_ref[1] * imag)
            scatter(ext_ref, 1, spot, width, lane, used, probe_ref[0] * imag - probe_ref[1] * real)

    interleave([chain(group) for group in groups_of(spots)], LAG)
    emit(ext_ref, own_ref, down_ref, up_out_ref, low_out_ref, diag_ref, width)
    diags_ref[:2] = diag_ref[...]
    diags_ref[2:] = other_diag_ref[...]


def step(value, gradient):
    return value - step_size * gradient


def rest_values(tile_ref, own_ref, above_ref, lower_ref, c, width):
    tile_px = own_ref.shape[1]
    top, low = slice(0, width), slice(width, tile_px)
    left, right = slice(0, width), slice(width, tile_px)
    yield top, right, step(tile_ref[c, top, right], own_ref[c, top, right] + above_ref[c, :, right])
    yield low, left, step(tile_ref[c, low, left], own_ref[c, low, left] + lower_ref[c])
    yield low, right, step(tile_ref[c, low, right], own_ref[c, low, right])


def quad_value(quad_ref, own_ref, above_ref, upper_ref, wrap_ref, c, width):
    top, left = slice(0, width), slice(0, width)
    received = above_ref[c, :, left] + upper_ref[c] + wrap_ref[c]
    return step(quad_ref[c, top, left], own_ref[c, top, left] + received)


def update_second_kernel(
    tile_ref, own_ref, above_ref, low_ref, rest_ref, left_ref, right_ref, *, width,
):
    for c in range(2):
        pieces = list(rest_values(tile_ref.at[1], own_ref, above_ref, low_ref, c, width))
        for rows, lanes, value in pieces:
            rest_ref[c, rows, lanes] = value
        right_ref[c] = pieces[0][2]
        left_ref[c] = pieces[1][2]


def update_first_kernel(
    tile_ref, own_ref, above_ref, low_ref, second_ref, rest_ref, left_ref, right_ref, *, width,
):
    for c in range(2):
        pieces = list(rest_values(tile_ref.at[0], own_ref, above_ref, low_ref, c, width))
        for rows, lanes, value in pieces:
            rest_ref[c, rows, lanes] = value
        right_ref[c] = pieces[0][2]
        right_ref[2 + c] = second_ref[c]
        left_ref[c] = pieces[1][2]


def update_quad_kernel(
    tile_ref, own_one, own_two, above_one, above_two, up_one, up_two, wrap_ref,
    quad_one, quad_two, left_ref, *, width,
):
    parts = ((own_one, above_one, up_one, quad_one), (own_two, above_two, up_two, quad_two))
    for s, (own_ref, above_ref, up_ref, quad_ref) in enumerate(parts):
        for c in range(2):
            wrap = wrap_ref.at[pl.ds(2 * s, 2)]
            value = quad_value(tile_ref.at[s], own_ref, above_ref, up_ref, wrap, c, width)
            quad_ref[c] = value
            left_ref[2 * s + c] = value


def finish_rest_kernel(rest_ref, own_ref, above_ref, low_ref, *refs, width, part):
    out_ref, tile_ref, sem = refs[-3:]
    for c in range(2):
        for rows, lanes, value in rest_values(rest_ref, own_ref, above_ref, low_ref, c, width):
            tile_ref[c, rows, lanes] = value
        tile_ref[c, :width, :width] = jnp.zeros((width, width), jnp.float32)
    copy = pltpu.make_async_copy(tile_ref, out_ref.at[part], sem)
    copy.start()
    copy.wait()


def finish_quad_kernel(
    quad_one, quad_two, own_one, own_two, above_one, above_two, up_one, up_two, wrap_ref, part_ref, out_ref,
    quads_ref, sem, *, width,
):
    del part_ref
    parts = ((quad_one, own_one, above_one, up_one), (quad_two, own_two, above_two, up_two))
    for s, refs in enumerate(parts):
        for c in range(2):
            quads_ref[s, c] = quad_value(*refs, wrap_ref.at[pl.ds(2 * s, 2)], c, width)
    copy = pltpu.make_async_copy(quads_ref, out_ref.at[:, :, pl.ds(0, width), pl.ds(0, width)], sem)
    copy.start()
    copy.wait()


def stage_kernel(*refs):
    sems = refs[-1]
    count = (len(refs) - 1) // 2
    copies = [pltpu.make_async_copy(refs[k], refs[count + k], sems.at[k]) for k in range(count)]
    for copy in copies:
        copy.start()
    for copy in copies:
        copy.wait()


F32 = functools.partial(jax.ShapeDtypeStruct, dtype=jnp.float32)
SMEM = pl.BlockSpec(memory_space=pltpu.SMEM)
VMEM = pl.BlockSpec(memory_space=pltpu.VMEM)
LIMIT = pltpu.CompilerParams(vmem_limit_bytes=16 * 1024 * 1024)


FAR = pl.BlockSpec(memory_space=pltpu.MemorySpace.HBM)


def call(kernel, scalars, arrays, outs, scratch, **static):
    return pl.pallas_call(
        functools.partial(kernel, **static),
        in_specs=[SMEM] * len(scalars) + [VMEM] * len(arrays),
        out_specs=[VMEM] * len(outs),
        out_shape=outs,
        scratch_shapes=scratch,
        compiler_params=LIMIT,
    )(*scalars, *arrays)


def pack_kernel(whole_ref, *refs, boxes):
    outs, sems = refs[:-1], refs[-1]
    copies = []
    for (rows, lanes), out_ref in zip(boxes, outs):
        for s in range(2):
            source = whole_ref.at[s, :, pl.ds(*rows), pl.ds(*lanes)]
            copies.append(pltpu.make_async_copy(source, out_ref.at[pl.ds(2 * s, 2)], sems.at[len(copies)]))
    for copy in copies:
        copy.start()
    for copy in copies:
        copy.wait()


def pack(whole, boxes):
    return pl.pallas_call(
        functools.partial(pack_kernel, boxes=boxes),
        in_specs=[FAR],
        out_specs=[VMEM] * len(boxes),
        out_shape=[F32((4, rows[1], lanes[1])) for rows, lanes in boxes],
        scratch_shapes=[pltpu.SemaphoreType.DMA((2 * len(boxes),))],
        compiler_params=LIMIT,
    )(in_hbm(whole))


def in_hbm(array):
    return pltpu.with_memory_space_constraint(array, pltpu.MemorySpace.HBM)


def body(
    specimen_slices,
    illumination_probe,
    propagation_phase,
    amplitudes,
    positions,
    counts,
    measurement_index,
):
    tile_px = specimen_slices.shape[2]
    width = illumination_probe.shape[1]
    spots = positions.shape[2]
    ext = tile_px + width
    across = tile_px - width
    cos, sin = jnp.cos(propagation_phase), jnp.sin(propagation_phase)
    scalars = (jnp.concatenate([positions.reshape(-1), counts.reshape(-1), measurement_index.reshape(-1)]),)
    static = dict(spots=spots, width=width)
    ext_space = pltpu.VMEM((2, ext // LANES, ext, LANES), jnp.float32)
    wave_space = pltpu.VMEM((spots, 2, width, width), jnp.float32)
    wave = F32((spots, 2, width, width))
    square = F32((2, width, width))
    squares = F32((4, width, width))
    whole = F32((2, tile_px, tile_px))
    strip = F32((2, width, tile_px))
    gradient = [whole, strip, square, square, square]

    (left_up,) = pack(specimen_slices, [((0, width), (0, width))])
    upper = from_behind(left_up, "col", -1)
    left_low, top = pack(specimen_slices, [((width, across), (0, width)), ((0, width), (0, tile_px))])
    lower = from_behind(left_low, "col", -1)
    below = from_behind(top, "row", -1)
    wrapped = send_wrap(left_up, -1)
    far = (specimen_slices, illumination_probe, amplitudes[0, 0], jnp.asarray(dft_operands(width)))
    tile, probe, measured, table = pl.pallas_call(
        stage_kernel,
        in_specs=[FAR] * len(far),
        out_specs=[VMEM] * len(far),
        out_shape=[jax.ShapeDtypeStruct(x.shape, x.dtype) for x in far],
        scratch_shapes=[pltpu.SemaphoreType.DMA((len(far),))],
        compiler_params=LIMIT,
        name="stage",
    )(*[in_hbm(x) for x in far])
    corner = send_corner(upper, -1)
    for i in range(ITERS):
        if i == 0:
            own_two, down_two, up_two, low_two, diag_two, back = call(
                wave_kernel, scalars,
                (tile, below, upper, lower, corner, wrapped, cos, sin, probe, measured, table),
                [*gradient, wave], [ext_space, wave_space, wave_space], **static,
            )
        else:
            (moved,) = call(
                forward_kernel, scalars, (*halo[0], cos, sin, probe, table),
                [wave], [ext_space, wave_space], **static,
            )
            own_two, down_two, up_two, low_two, diag_two, back = call(
                residual_kernel, scalars, (*halo[1], moved, measured, table),
                [*gradient, wave], [ext_space, wave_space], **static,
            )
        low_two = from_behind(low_two, "col", 1)
        corner_two = send_corner(diag_two, 1)
        above_two = from_behind(down_two, "row", 1)
        own_one, down_one, up_one, low_one, diag_one, diags = call(
            backward_kernel, scalars, (back, diag_two, cos, sin, probe, table),
            [*gradient, squares], [ext_space], **static,
        )
        low_one = from_behind(low_one, "col", 1)
        corner_one = send_corner(diag_one, 1)
        above_one = from_behind(down_one, "row", 1)
        up_two = up_two + corner_two
        up_one = up_one + corner_one
        up_two = from_behind(up_two, "col", 1)
        up_one = from_behind(up_one, "col", 1)
        from_wrap = send_wrap(diags, 1)
        if i + 1 < ITERS:
            rest_two, left_two, right = call(
                update_second_kernel, (), (tile, own_two, above_two, low_two),
                [whole, square, F32((2, width, across))], [], width=width,
            )
            rest_one, left_one, right = call(
                update_first_kernel, (), (tile, own_one, above_one, low_one, right),
                [whole, square, F32((4, width, across))], [], width=width,
            )
            lower_one = from_behind(left_one, "col", -1)
            below_right = from_behind(right, "row", -1)
            quad_one, quad_two, left = call(
                update_quad_kernel, (),
                (tile, own_one, own_two, above_one, above_two, up_one, up_two, from_wrap),
                [square, square, squares], [], width=width,
            )
            upper_one = from_behind(quad_one, "col", -1)
            upper_two = from_behind(quad_two, "col", -1)
            below_left = from_behind(left, "row", -1)
            lower_two = from_behind(left_two, "col", -1)
            wrapped = send_wrap(left, -1)
            corner_one = send_corner(upper_one, -1)
            corner_two = send_corner(upper_two, -1)
            halo = (
                (rest_one, quad_one, below_left, below_right, upper_one, lower_one, corner_one, wrapped),
                (rest_two, quad_two, below_left, below_right, upper_two, lower_two, corner_two, wrapped),
            )
        else:
            part = []
            for slice_at, operands in (
                (1, (rest_two, own_two, above_two, low_two)), (0, (rest_one, own_one, above_one, low_one))
            ):
                part = [pl.pallas_call(
                    functools.partial(finish_rest_kernel, width=width, part=slice_at),
                    in_specs=[VMEM] * 4 + [FAR] * len(part),
                    out_specs=FAR,
                    out_shape=F32(specimen_slices.shape),
                    input_output_aliases={4: 0} if part else {},
                    scratch_shapes=[
                        pltpu.VMEM((2, tile_px, tile_px), jnp.float32), pltpu.SemaphoreType.DMA(()),
                    ],
                    compiler_params=LIMIT,
                    name="finish_rest",
                )(*operands, *map(in_hbm, part))]
            updated = pl.pallas_call(
                functools.partial(finish_quad_kernel, width=width),
                in_specs=[VMEM] * 9 + [FAR],
                out_specs=FAR,
                out_shape=F32(specimen_slices.shape),
                input_output_aliases={9: 0},
                scratch_shapes=[
                    pltpu.VMEM((2, 2, width, width), jnp.float32), pltpu.SemaphoreType.DMA(()),
                ],
                compiler_params=LIMIT,
                name="finish_quad",
            )(quad_one, quad_two, own_one, own_two, above_one, above_two, up_one, up_two, from_wrap, in_hbm(part[0]))
    return updated


def solution(mesh):
    placed = (
        P(None, None, "row", "col"),
        P(),
        P(),
        P("row", "col", None, None, None),
        P("row", "col", None, None),
        P("row", "col"),
        P("row", "col", None),
    )

    return jax.shard_map(body, mesh=mesh, in_specs=placed, out_specs=P(None, None, "row", "col"), check_vma=False)
```

```python
import functools
import math

import jax
import jax.numpy as jnp
import ml_dtypes
import numpy as np
from jax import lax
from jax.experimental import pallas as pl
from jax.experimental.pallas import tpu as pltpu
from jax.sharding import PartitionSpec as P


ITERS = 2
LANES = 128

step_size = 0.02
floor_amp = 0.5


def from_behind(block, axis, distance):
    devices = range(lax.axis_size(axis))
    route = [((i - distance) % len(devices), i) for i in devices]
    return lax.ppermute(block, axis, route)


def two_parts(value):
    high = value.astype(ml_dtypes.bfloat16)
    low = (value - high.astype(np.float64)).astype(ml_dtypes.bfloat16)
    return high, low


def dft_operands(width):
    index = np.arange(width)
    angle = (index[:, None] * index[None, :] % width) * (2.0 * math.pi / width)
    real = np.cos(angle) / math.sqrt(width)
    imag = -np.sin(angle) / math.sqrt(width)
    right = np.block([[real, imag], [-imag, real]])
    right_high, right_low = two_parts(right)
    left_high, left_low = two_parts(right.T)
    return np.stack([right_high, right_low, left_high, left_low])


def split(value):
    high = value.astype(jnp.bfloat16)
    low = (value - high.astype(jnp.float32)).astype(jnp.bfloat16)
    return high, low


def rows_of(j, width):
    return slice(j * width, (j + 1) * width)


def product(left, right):
    return jnp.dot(left, right, preferred_element_type=jnp.float32)


def right_side(pairs, table_ref):
    high, low = split(jnp.concatenate([jnp.concatenate(pair, 1) for pair in pairs], 0))
    return product(high, table_ref[0]) + product(low, table_ref[0]) + product(high, table_ref[1])


def left_side(half, table_ref, width):
    count = half.shape[0] // width
    parts = [half[rows_of(k, width)] for k in range(count)]
    tall = [jnp.concatenate([part[:, :width], part[:, width:]], 0) for part in parts]
    high, low = split(jnp.concatenate(tall, 1))
    full = product(table_ref[2], high) + product(table_ref[2], low) + product(table_ref[3], high)
    return [(full[:width, rows_of(k, width)], full[width:, rows_of(k, width)]) for k in range(count)]


def interleave(chains, lag):
    waiting = [(n * lag, chain) for n, chain in enumerate(chains)]
    while waiting:
        after = []
        for delay, chain in waiting:
            if delay:
                after.append((delay - 1, chain))
            elif next(chain, None) is not None:
                after.append((0, chain))
        waiting = after


def fill_ext(ext_ref, pieces):
    for row, col, source in pieces:
        height, across = source.shape[1:]
        for c in range(2):
            for b in range(across // LANES):
                ext_ref[c, col // LANES + b, row:row + height, :] = source[c, :, b * LANES:(b + 1) * LANES]


def place(scalar_ref, j):
    col = scalar_ref[2 * j + 1]
    return scalar_ref[2 * j], col // LANES, col % LANES


def window(ext_ref, c, spot, width, lane):
    row, block, shift = spot
    near = ext_ref[c, block, pl.ds(row, width), :]
    far = ext_ref[c, block + 1, pl.ds(row, width), :]
    return pltpu.roll(jnp.where(lane >= shift, near, far), LANES - shift, 1)


def scatter(grad_ref, c, spot, width, lane, used, update):
    row, block, shift = spot
    turned = pltpu.roll(jnp.where(used, update, 0.0), shift, 1)
    near = lane >= shift
    grad_ref[c, block, pl.ds(row, width), :] += jnp.where(near, turned, 0.0)
    grad_ref[c, block + 1, pl.ds(row, width), :] += jnp.where(near, 0.0, turned)


def emit(grad_ref, own_ref, down_ref, upper_ref, lower_ref, diag_ref, width):
    tile_px = own_ref.shape[1]
    blocks = tile_px // LANES
    for c in range(2):
        for b in range(blocks):
            lanes = slice(b * LANES, (b + 1) * LANES)
            own_ref[c, :, lanes] = grad_ref[c, b, :tile_px, :]
            down_ref[c, :, lanes] = grad_ref[c, b, tile_px:, :]
        upper_ref[c] = grad_ref[c, blocks, :width, :]
        lower_ref[c] = grad_ref[c, blocks, width:tile_px, :]
        diag_ref[c] = grad_ref[c, blocks, tile_px:, :]


def lanes_of(width):
    return lax.broadcasted_iota(jnp.int32, (width, LANES), 1)


LAG = 1


def groups_of(spots):
    return [range(j, min(j + 2, spots)) for j in range(0, spots, 2)]


def forward_steps(group, enter_ref, leave_ref, cos_ref, sin_ref, table_ref, width):
    half = right_side([(enter_ref[j, 0], enter_ref[j, 1]) for j in group], table_ref)
    yield True
    pairs = left_side(half, table_ref, width)
    yield True
    half = right_side([
        (cos_ref[...] * real - sin_ref[...] * imag, -(cos_ref[...] * imag + sin_ref[...] * real))
        for real, imag in pairs
    ], table_ref)
    yield True
    pairs = left_side(half, table_ref, width)
    yield True
    for j, (real, negative) in zip(group, pairs):
        leave_ref[j, 0] = real
        leave_ref[j, 1] = -negative


def residual_steps(group, moved_ref, win_ref, measured_of, finish, table_ref, width):
    half = right_side([
        (
            moved_ref[j, 0] * win_ref[j, 0] - moved_ref[j, 1] * win_ref[j, 1],
            moved_ref[j, 0] * win_ref[j, 1] + moved_ref[j, 1] * win_ref[j, 0],
        )
        for j in group
    ], table_ref)
    yield True
    pairs = left_side(half, table_ref, width)
    yield True
    residuals = []
    for j, (real, imag) in zip(group, pairs):
        power = jnp.maximum(real * real + imag * imag, floor_amp * floor_amp)
        factor = 1.0 - measured_of(j) * lax.rsqrt(power)
        residuals.append((real * factor, -(imag * factor)))
    half = right_side(residuals, table_ref)
    yield True
    pairs = left_side(half, table_ref, width)
    yield True
    for j, (real, negative) in zip(group, pairs):
        finish(j, real, -negative)


def joined(*parts):
    for part in parts:
        yield from part


def whole_pieces(refs, s, tile_px, width):
    tile_ref, below_ref, upper_ref, lower_ref, corner_ref = refs
    both = pl.ds(2 * s, 2)
    return [
        (0, 0, tile_ref.at[s]),
        (tile_px, 0, below_ref.at[both]),
        (0, tile_px, upper_ref.at[both]),
        (width, tile_px, lower_ref.at[both]),
        (tile_px, tile_px, corner_ref.at[both]),
    ]


def slice_pieces(refs, s, tile_px, width):
    rest_ref, quad_ref, below_left_ref, below_right_ref, upper_ref, lower_ref, corner_ref = refs
    both = pl.ds(2 * s, 2)
    across = tile_px - width
    return [
        (width, 0, rest_ref.at[:, pl.ds(width, across), :]),
        (0, width, rest_ref.at[:, pl.ds(0, width), pl.ds(width, across)]),
        (0, 0, quad_ref),
        (tile_px, 0, below_left_ref.at[both]),
        (tile_px, width, below_right_ref.at[both]),
        (0, tile_px, upper_ref),
        (width, tile_px, lower_ref),
        (tile_px, tile_px, corner_ref),
    ]


def take_windows(ext_ref, spot_list, win_ref, width, lane):
    for j, spot in enumerate(spot_list):
        win_ref[j, 0] = window(ext_ref, 0, spot, width, lane)
        win_ref[j, 1] = window(ext_ref, 1, spot, width, lane)


def light(ext_ref, spot_list, probe_ref, enter_ref, width, lane):
    for j, spot in enumerate(spot_list):
        real = window(ext_ref, 0, spot, width, lane)
        imag = window(ext_ref, 1, spot, width, lane)
        enter_ref[j, 0] = probe_ref[0] * real - probe_ref[1] * imag
        enter_ref[j, 1] = probe_ref[0] * imag + probe_ref[1] * real


def residual_end(scalar_ref, spots, spot_list, ext_ref, moved_ref, win_ref, back_ref, width, lane):
    total = scalar_ref[2 * spots]

    def finish(j, real, imag):
        used = j < total
        scatter(ext_ref, 0, spot_list[j], width, lane, used, moved_ref[j, 0] * real + moved_ref[j, 1] * imag)
        scatter(ext_ref, 1, spot_list[j], width, lane, used, moved_ref[j, 0] * imag - moved_ref[j, 1] * real)
        back_ref[j, 0] = win_ref[j, 0] * real + win_ref[j, 1] * imag
        back_ref[j, 1] = win_ref[j, 0] * imag - win_ref[j, 1] * real

    return finish


def wave_kernel(
    scalar_ref, tile_ref, below_ref, upper_ref, lower_ref, corner_ref,
    cos_ref, sin_ref, probe_ref, amp_ref, table_ref,
    own_ref, down_ref, up_out_ref, low_out_ref, diag_ref, back_ref,
    ext_ref, win_ref, moved_ref, *, spots, width,
):
    lane = lanes_of(width)
    tile_px = own_ref.shape[1]
    spot_list = [place(scalar_ref, j) for j in range(spots)]
    halo = (tile_ref, below_ref, upper_ref, lower_ref, corner_ref)
    fill_ext(ext_ref, whole_pieces(halo, 0, tile_px, width))
    light(ext_ref, spot_list, probe_ref, back_ref, width, lane)
    fill_ext(ext_ref, whole_pieces(halo, 1, tile_px, width))
    take_windows(ext_ref, spot_list, win_ref, width, lane)
    ext_ref[...] = jnp.zeros(ext_ref.shape, jnp.float32)
    finish = residual_end(scalar_ref, spots, spot_list, ext_ref, moved_ref, win_ref, back_ref, width, lane)
    interleave([
        joined(
            forward_steps(group, back_ref, moved_ref, cos_ref, sin_ref, table_ref, width),
            residual_steps(
                group, moved_ref, win_ref, lambda j: amp_ref[scalar_ref[2 * spots + 1 + j]],
                finish, table_ref, width,
            ),
        )
        for group in groups_of(spots)
    ], LAG)
    emit(ext_ref, own_ref, down_ref, up_out_ref, low_out_ref, diag_ref, width)


def forward_kernel(
    scalar_ref, rest_ref, quad_ref, left_ref, right_ref, upper_ref, lower_ref, corner_ref,
    cos_ref, sin_ref, probe_ref, table_ref, moved_ref, ext_ref, enter_ref, *, spots, width,
):
    lane = lanes_of(width)
    spot_list = [place(scalar_ref, j) for j in range(spots)]
    halo = (rest_ref, quad_ref, left_ref, right_ref, upper_ref, lower_ref, corner_ref)
    fill_ext(ext_ref, slice_pieces(halo, 0, rest_ref.shape[1], width))
    light(ext_ref, spot_list, probe_ref, enter_ref, width, lane)
    interleave([
        forward_steps(group, enter_ref, moved_ref, cos_ref, sin_ref, table_ref, width)
        for group in groups_of(spots)
    ], LAG)


def residual_kernel(
    scalar_ref, rest_ref, quad_ref, left_ref, right_ref, upper_ref, lower_ref, corner_ref,
    moved_ref, amp_ref, table_ref,
    own_ref, down_ref, up_out_ref, low_out_ref, diag_ref, back_ref,
    ext_ref, win_ref, *, spots, width,
):
    lane = lanes_of(width)
    spot_list = [place(scalar_ref, j) for j in range(spots)]
    halo = (rest_ref, quad_ref, left_ref, right_ref, upper_ref, lower_ref, corner_ref)
    fill_ext(ext_ref, slice_pieces(halo, 1, rest_ref.shape[1], width))
    take_windows(ext_ref, spot_list, win_ref, width, lane)
    ext_ref[...] = jnp.zeros(ext_ref.shape, jnp.float32)
    finish = residual_end(scalar_ref, spots, spot_list, ext_ref, moved_ref, win_ref, back_ref, width, lane)
    interleave([
        residual_steps(
            group, moved_ref, win_ref, lambda j: amp_ref[scalar_ref[2 * spots + 1 + j]],
            finish, table_ref, width,
        )
        for group in groups_of(spots)
    ], LAG)
    emit(ext_ref, own_ref, down_ref, up_out_ref, low_out_ref, diag_ref, width)


def backward_kernel(
    scalar_ref, back_ref, cos_ref, sin_ref, probe_ref, table_ref,
    own_ref, down_ref, up_out_ref, low_out_ref, diag_ref, ext_ref, *, spots, width,
):
    lane = lanes_of(width)
    total = scalar_ref[2 * spots]
    ext_ref[...] = jnp.zeros(ext_ref.shape, jnp.float32)

    def chain(group):
        half = right_side([(back_ref[j, 0], back_ref[j, 1]) for j in group], table_ref)
        yield True
        pairs = left_side(half, table_ref, width)
        yield True
        half = right_side([
            (cos_ref[...] * real + sin_ref[...] * imag, -(cos_ref[...] * imag - sin_ref[...] * real))
            for real, imag in pairs
        ], table_ref)
        yield True
        pairs = left_side(half, table_ref, width)
        yield True
        for j, (real, negative) in zip(group, pairs):
            imag = -negative
            spot = place(scalar_ref, j)
            used = j < total
            scatter(ext_ref, 0, spot, width, lane, used, probe_ref[0] * real + probe_ref[1] * imag)
            scatter(ext_ref, 1, spot, width, lane, used, probe_ref[0] * imag - probe_ref[1] * real)

    interleave([chain(group) for group in groups_of(spots)], LAG)
    emit(ext_ref, own_ref, down_ref, up_out_ref, low_out_ref, diag_ref, width)


def step(value, gradient):
    return value - step_size * gradient


def rest_values(tile_ref, own_ref, above_ref, lower_ref, c, width):
    tile_px = own_ref.shape[1]
    top, low = slice(0, width), slice(width, tile_px)
    left, right = slice(0, width), slice(width, tile_px)
    yield top, right, step(tile_ref[c, top, right], own_ref[c, top, right] + above_ref[c, :, right])
    yield low, left, step(tile_ref[c, low, left], own_ref[c, low, left] + lower_ref[c])
    yield low, right, step(tile_ref[c, low, right], own_ref[c, low, right])


def quad_value(quad_ref, own_ref, above_ref, upper_ref, c, width):
    top, left = slice(0, width), slice(0, width)
    return step(quad_ref[c, top, left], own_ref[c, top, left] + above_ref[c, :, left] + upper_ref[c])


def update_second_kernel(
    tile_ref, own_ref, above_ref, low_ref, rest_ref, left_ref, right_ref, *, width,
):
    for c in range(2):
        pieces = list(rest_values(tile_ref.at[1], own_ref, above_ref, low_ref, c, width))
        for rows, lanes, value in pieces:
            rest_ref[c, rows, lanes] = value
        right_ref[c] = pieces[0][2]
        left_ref[c] = pieces[1][2]


def update_first_kernel(
    tile_ref, own_ref, above_ref, low_ref, second_ref, rest_ref, left_ref, right_ref, *, width,
):
    for c in range(2):
        pieces = list(rest_values(tile_ref.at[0], own_ref, above_ref, low_ref, c, width))
        for rows, lanes, value in pieces:
            rest_ref[c, rows, lanes] = value
        right_ref[c] = pieces[0][2]
        right_ref[2 + c] = second_ref[c]
        left_ref[c] = pieces[1][2]


def update_quad_kernel(
    tile_ref, own_one, own_two, above_one, above_two, up_one, up_two,
    quad_one, quad_two, left_ref, *, width,
):
    parts = ((own_one, above_one, up_one, quad_one), (own_two, above_two, up_two, quad_two))
    for s, (own_ref, above_ref, up_ref, quad_ref) in enumerate(parts):
        for c in range(2):
            value = quad_value(tile_ref.at[s], own_ref, above_ref, up_ref, c, width)
            quad_ref[c] = value
            left_ref[2 * s + c] = value


def finish_rest_kernel(rest_ref, own_ref, above_ref, low_ref, *refs, width, part):
    out_ref, tile_ref, sem = refs[-3:]
    for c in range(2):
        for rows, lanes, value in rest_values(rest_ref, own_ref, above_ref, low_ref, c, width):
            tile_ref[c, rows, lanes] = value
        tile_ref[c, :width, :width] = jnp.zeros((width, width), jnp.float32)
    copy = pltpu.make_async_copy(tile_ref, out_ref.at[part], sem)
    copy.start()
    copy.wait()


def finish_quad_kernel(
    quad_one, quad_two, own_one, own_two, above_one, above_two, up_one, up_two, part_ref, out_ref,
    quads_ref, sem, *, width,
):
    del part_ref
    parts = ((quad_one, own_one, above_one, up_one), (quad_two, own_two, above_two, up_two))
    for s, refs in enumerate(parts):
        for c in range(2):
            quads_ref[s, c] = quad_value(*refs, c, width)
    copy = pltpu.make_async_copy(quads_ref, out_ref.at[:, :, pl.ds(0, width), pl.ds(0, width)], sem)
    copy.start()
    copy.wait()


def stage_kernel(*refs):
    sems = refs[-1]
    count = (len(refs) - 1) // 2
    copies = [pltpu.make_async_copy(refs[k], refs[count + k], sems.at[k]) for k in range(count)]
    for copy in copies:
        copy.start()
    for copy in copies:
        copy.wait()


F32 = functools.partial(jax.ShapeDtypeStruct, dtype=jnp.float32)
SMEM = pl.BlockSpec(memory_space=pltpu.SMEM)
VMEM = pl.BlockSpec(memory_space=pltpu.VMEM)
LIMIT = pltpu.CompilerParams(vmem_limit_bytes=16 * 1024 * 1024)


FAR = pl.BlockSpec(memory_space=pltpu.MemorySpace.HBM)


def call(kernel, scalars, arrays, outs, scratch, **static):
    return pl.pallas_call(
        functools.partial(kernel, **static),
        in_specs=[SMEM] * len(scalars) + [VMEM] * len(arrays),
        out_specs=[VMEM] * len(outs),
        out_shape=outs,
        scratch_shapes=scratch,
        compiler_params=LIMIT,
    )(*scalars, *arrays)


def pack_kernel(whole_ref, up_ref, low_ref, top_ref, sems, *, width):
    tile_px = whole_ref.shape[2]
    left = pl.ds(0, width)
    copies = []
    for s in range(2):
        both = pl.ds(2 * s, 2)
        copies.append((whole_ref.at[s, :, pl.ds(0, width), left], up_ref.at[both]))
        copies.append((whole_ref.at[s, :, pl.ds(width, tile_px - width), left], low_ref.at[both]))
        copies.append((whole_ref.at[s, :, pl.ds(0, width), :], top_ref.at[both]))
    copies = [pltpu.make_async_copy(a, b, sems.at[k]) for k, (a, b) in enumerate(copies)]
    for copy in copies:
        copy.start()
    for copy in copies:
        copy.wait()


def in_hbm(array):
    return pltpu.with_memory_space_constraint(array, pltpu.MemorySpace.HBM)


def body(
    specimen_slices,
    illumination_probe,
    propagation_phase,
    amplitudes,
    positions,
    counts,
    measurement_index,
):
    tile_px = specimen_slices.shape[2]
    width = illumination_probe.shape[1]
    spots = positions.shape[2]
    ext = tile_px + width
    across = tile_px - width
    cos, sin = jnp.cos(propagation_phase), jnp.sin(propagation_phase)
    scalars = (jnp.concatenate([positions.reshape(-1), counts.reshape(-1), measurement_index.reshape(-1)]),)
    static = dict(spots=spots, width=width)
    ext_space = pltpu.VMEM((2, ext // LANES, ext, LANES), jnp.float32)
    wave_space = pltpu.VMEM((spots, 2, width, width), jnp.float32)
    wave = F32((spots, 2, width, width))
    square = F32((2, width, width))
    squares = F32((4, width, width))
    whole = F32((2, tile_px, tile_px))
    strip = F32((2, width, tile_px))
    gradient = [whole, strip, square, square, square]

    left_up, left_low, top = pl.pallas_call(
        functools.partial(pack_kernel, width=width),
        in_specs=[FAR],
        out_specs=[VMEM] * 3,
        out_shape=[squares, squares, F32((4, width, tile_px))],
        scratch_shapes=[pltpu.SemaphoreType.DMA((6,))],
        compiler_params=LIMIT,
        name="pack",
    )(in_hbm(specimen_slices))
    upper = from_behind(left_up, "col", -1)
    lower = from_behind(left_low, "col", -1)
    below = from_behind(top, "row", -1)
    far = (specimen_slices, illumination_probe, amplitudes[0, 0], jnp.asarray(dft_operands(width)))
    tile, probe, measured, table = pl.pallas_call(
        stage_kernel,
        in_specs=[FAR] * len(far),
        out_specs=[VMEM] * len(far),
        out_shape=[jax.ShapeDtypeStruct(x.shape, x.dtype) for x in far],
        scratch_shapes=[pltpu.SemaphoreType.DMA((len(far),))],
        compiler_params=LIMIT,
        name="stage",
    )(*[in_hbm(x) for x in far])
    corner = from_behind(upper, "row", -1)
    for i in range(ITERS):
        if i == 0:
            own_two, down_two, up_two, low_two, diag_two, back = call(
                wave_kernel, scalars,
                (tile, below, upper, lower, corner, cos, sin, probe, measured, table),
                [*gradient, wave], [ext_space, wave_space, wave_space], **static,
            )
        else:
            (moved,) = call(
                forward_kernel, scalars, (*halo[0], cos, sin, probe, table),
                [wave], [ext_space, wave_space], **static,
            )
            own_two, down_two, up_two, low_two, diag_two, back = call(
                residual_kernel, scalars, (*halo[1], moved, measured, table),
                [*gradient, wave], [ext_space, wave_space], **static,
            )
        low_two = from_behind(low_two, "col", 1)
        corner_two = from_behind(diag_two, "row", 1)
        above_two = from_behind(down_two, "row", 1)
        own_one, down_one, up_one, low_one, diag_one = call(
            backward_kernel, scalars, (back, cos, sin, probe, table),
            gradient, [ext_space], **static,
        )
        low_one = from_behind(low_one, "col", 1)
        corner_one = from_behind(diag_one, "row", 1)
        above_one = from_behind(down_one, "row", 1)
        up_two = up_two + corner_two
        up_one = up_one + corner_one
        up_two = from_behind(up_two, "col", 1)
        up_one = from_behind(up_one, "col", 1)
        if i + 1 < ITERS:
            rest_two, left_two, right = call(
                update_second_kernel, (), (tile, own_two, above_two, low_two),
                [whole, square, F32((2, width, across))], [], width=width,
            )
            rest_one, left_one, right = call(
                update_first_kernel, (), (tile, own_one, above_one, low_one, right),
                [whole, square, F32((4, width, across))], [], width=width,
            )
            lower_one = from_behind(left_one, "col", -1)
            below_right = from_behind(right, "row", -1)
            quad_one, quad_two, left = call(
                update_quad_kernel, (),
                (tile, own_one, own_two, above_one, above_two, up_one, up_two),
                [square, square, squares], [], width=width,
            )
            upper_one = from_behind(quad_one, "col", -1)
            upper_two = from_behind(quad_two, "col", -1)
            below_left = from_behind(left, "row", -1)
            lower_two = from_behind(left_two, "col", -1)
            corner_one = from_behind(upper_one, "row", -1)
            corner_two = from_behind(upper_two, "row", -1)
            halo = (
                (rest_one, quad_one, below_left, below_right, upper_one, lower_one, corner_one),
                (rest_two, quad_two, below_left, below_right, upper_two, lower_two, corner_two),
            )
        else:
            part = []
            for slice_at, operands in (
                (1, (rest_two, own_two, above_two, low_two)), (0, (rest_one, own_one, above_one, low_one))
            ):
                part = [pl.pallas_call(
                    functools.partial(finish_rest_kernel, width=width, part=slice_at),
                    in_specs=[VMEM] * 4 + [FAR] * len(part),
                    out_specs=FAR,
                    out_shape=F32(specimen_slices.shape),
                    input_output_aliases={4: 0} if part else {},
                    scratch_shapes=[
                        pltpu.VMEM((2, tile_px, tile_px), jnp.float32), pltpu.SemaphoreType.DMA(()),
                    ],
                    compiler_params=LIMIT,
                    name="finish_rest",
                )(*operands, *map(in_hbm, part))]
            updated = pl.pallas_call(
                functools.partial(finish_quad_kernel, width=width),
                in_specs=[VMEM] * 8 + [FAR],
                out_specs=FAR,
                out_shape=F32(specimen_slices.shape),
                input_output_aliases={8: 0},
                scratch_shapes=[
                    pltpu.VMEM((2, 2, width, width), jnp.float32), pltpu.SemaphoreType.DMA(()),
                ],
                compiler_params=LIMIT,
                name="finish_quad",
            )(quad_one, quad_two, own_one, own_two, above_one, above_two, up_one, up_two, in_hbm(part[0]))
    return updated


def solution(mesh):
    placed = (
        P(None, None, "row", "col"),
        P(),
        P(),
        P("row", "col", None, None, None),
        P("row", "col", None, None),
        P("row", "col"),
        P("row", "col", None),
    )

    return jax.shard_map(body, mesh=mesh, in_specs=placed, out_specs=P(None, None, "row", "col"), check_vma=False)
```

```python
import functools
import math

import jax
import jax.numpy as jnp
import ml_dtypes
import numpy as np
from jax import lax
from jax.experimental import pallas as pl
from jax.experimental.pallas import tpu as pltpu
from jax.sharding import PartitionSpec as P


ITERS = 2
LANES = 128

step_size = 0.02
floor_amp = 0.5


def from_behind(block, axis, distance):
    devices = range(lax.axis_size(axis))
    route = [((i - distance) % len(devices), i) for i in devices]
    return lax.ppermute(block, axis, route)


def two_parts(value):
    high = value.astype(ml_dtypes.bfloat16)
    low = (value - high.astype(np.float64)).astype(ml_dtypes.bfloat16)
    return high, low


def dft_operands(width):
    index = np.arange(width)
    angle = (index[:, None] * index[None, :] % width) * (2.0 * math.pi / width)
    real = np.cos(angle) / math.sqrt(width)
    imag = -np.sin(angle) / math.sqrt(width)
    right = np.block([[real, imag], [-imag, real]])
    right_high, right_low = two_parts(right)
    left_high, left_low = two_parts(right.T)
    return np.stack([right_high, right_low, left_high, left_low])


def split(value):
    high = value.astype(jnp.bfloat16)
    low = (value - high.astype(jnp.float32)).astype(jnp.bfloat16)
    return high, low


def rows_of(j, width):
    return slice(j * width, (j + 1) * width)


def product(left, right):
    return jnp.dot(left, right, preferred_element_type=jnp.float32)


def right_side(pairs, table_ref):
    high, low = split(jnp.concatenate([jnp.concatenate(pair, 1) for pair in pairs], 0))
    return product(high, table_ref[0]) + product(low, table_ref[0]) + product(high, table_ref[1])


def left_side(half, table_ref, width):
    count = half.shape[0] // width
    parts = [half[rows_of(k, width)] for k in range(count)]
    tall = [jnp.concatenate([part[:, :width], part[:, width:]], 0) for part in parts]
    high, low = split(jnp.concatenate(tall, 1))
    full = product(table_ref[2], high) + product(table_ref[2], low) + product(table_ref[3], high)
    return [(full[:width, rows_of(k, width)], full[width:, rows_of(k, width)]) for k in range(count)]


def interleave(chains, lag):
    waiting = [(n * lag, chain) for n, chain in enumerate(chains)]
    while waiting:
        after = []
        for delay, chain in waiting:
            if delay:
                after.append((delay - 1, chain))
            elif next(chain, None) is not None:
                after.append((0, chain))
        waiting = after


def fill_ext(ext_ref, pieces):
    for row, col, source in pieces:
        height, across = source.shape[1:]
        for c in range(2):
            for b in range(across // LANES):
                ext_ref[c, col // LANES + b, row:row + height, :] = source[c, :, b * LANES:(b + 1) * LANES]


def place(scalar_ref, j):
    col = scalar_ref[0, 2 * j + 1]
    return scalar_ref[0, 2 * j], col // LANES, col % LANES


def window(ext_ref, c, spot, width, lane):
    row, block, shift = spot
    near = ext_ref[c, block, pl.ds(row, width), :]
    far = ext_ref[c, block + 1, pl.ds(row, width), :]
    return pltpu.roll(jnp.where(lane >= shift, near, far), LANES - shift, 1)


def scatter(grad_ref, c, spot, width, lane, used, update):
    row, block, shift = spot
    turned = pltpu.roll(jnp.where(used, update, 0.0), shift, 1)
    near = lane >= shift
    grad_ref[c, block, pl.ds(row, width), :] += jnp.where(near, turned, 0.0)
    grad_ref[c, block + 1, pl.ds(row, width), :] += jnp.where(near, 0.0, turned)


def emit(grad_ref, own_ref, down_ref, upper_ref, lower_ref, diag_ref, width):
    tile_px = own_ref.shape[1]
    blocks = tile_px // LANES
    for c in range(2):
        for b in range(blocks):
            lanes = slice(b * LANES, (b + 1) * LANES)
            own_ref[c, :, lanes] = grad_ref[c, b, :tile_px, :]
            down_ref[c, :, lanes] = grad_ref[c, b, tile_px:, :]
        upper_ref[c] = grad_ref[c, blocks, :width, :]
        lower_ref[c] = grad_ref[c, blocks, width:tile_px, :]
        diag_ref[c] = grad_ref[c, blocks, tile_px:, :]


def lanes_of(width):
    return lax.broadcasted_iota(jnp.int32, (width, LANES), 1)


LAG = 1


def groups_of(spots):
    return [range(j, min(j + 2, spots)) for j in range(0, spots, 2)]


def forward_steps(group, enter_ref, leave_ref, cos_ref, sin_ref, table_ref, width):
    half = right_side([(enter_ref[j, 0], enter_ref[j, 1]) for j in group], table_ref)
    yield True
    pairs = left_side(half, table_ref, width)
    yield True
    half = right_side([
        (cos_ref[...] * real - sin_ref[...] * imag, -(cos_ref[...] * imag + sin_ref[...] * real))
        for real, imag in pairs
    ], table_ref)
    yield True
    pairs = left_side(half, table_ref, width)
    yield True
    for j, (real, negative) in zip(group, pairs):
        leave_ref[j, 0] = real
        leave_ref[j, 1] = -negative


def residual_steps(group, moved_ref, win_ref, measured_of, finish, table_ref, width):
    half = right_side([
        (
            moved_ref[j, 0] * win_ref[j, 0] - moved_ref[j, 1] * win_ref[j, 1],
            moved_ref[j, 0] * win_ref[j, 1] + moved_ref[j, 1] * win_ref[j, 0],
        )
        for j in group
    ], table_ref)
    yield True
    pairs = left_side(half, table_ref, width)
    yield True
    residuals = []
    for j, (real, imag) in zip(group, pairs):
        power = jnp.maximum(real * real + imag * imag, floor_amp * floor_amp)
        factor = 1.0 - measured_of(j) * lax.rsqrt(power)
        residuals.append((real * factor, -(imag * factor)))
    half = right_side(residuals, table_ref)
    yield True
    pairs = left_side(half, table_ref, width)
    yield True
    for j, (real, negative) in zip(group, pairs):
        finish(j, real, -negative)


def joined(*parts):
    for part in parts:
        yield from part


def whole_pieces(refs, s, tile_px, width):
    tile_ref, below_ref, upper_ref, lower_ref, corner_ref = refs
    both = pl.ds(2 * s, 2)
    return [
        (0, 0, tile_ref.at[s]),
        (tile_px, 0, below_ref.at[both]),
        (0, tile_px, upper_ref.at[both]),
        (width, tile_px, lower_ref.at[both]),
        (tile_px, tile_px, corner_ref.at[both]),
    ]


def slice_pieces(refs, s, tile_px, width):
    rest_ref, quad_ref, below_left_ref, below_right_ref, upper_ref, lower_ref, corner_ref = refs
    both = pl.ds(2 * s, 2)
    across = tile_px - width
    return [
        (width, 0, rest_ref.at[:, pl.ds(width, across), :]),
        (0, width, rest_ref.at[:, pl.ds(0, width), pl.ds(width, across)]),
        (0, 0, quad_ref),
        (tile_px, 0, below_left_ref.at[both]),
        (tile_px, width, below_right_ref.at[both]),
        (0, tile_px, upper_ref),
        (width, tile_px, lower_ref),
        (tile_px, tile_px, corner_ref),
    ]


def take_windows(ext_ref, spot_list, win_ref, width, lane):
    for j, spot in enumerate(spot_list):
        win_ref[j, 0] = window(ext_ref, 0, spot, width, lane)
        win_ref[j, 1] = window(ext_ref, 1, spot, width, lane)


def light(ext_ref, spot_list, probe_ref, enter_ref, width, lane):
    for j, spot in enumerate(spot_list):
        real = window(ext_ref, 0, spot, width, lane)
        imag = window(ext_ref, 1, spot, width, lane)
        enter_ref[j, 0] = probe_ref[0] * real - probe_ref[1] * imag
        enter_ref[j, 1] = probe_ref[0] * imag + probe_ref[1] * real


def residual_end(scalar_ref, spots, spot_list, ext_ref, moved_ref, win_ref, back_ref, width, lane):
    total = scalar_ref[0, 2 * spots]

    def finish(j, real, imag):
        used = j < total
        scatter(ext_ref, 0, spot_list[j], width, lane, used, moved_ref[j, 0] * real + moved_ref[j, 1] * imag)
        scatter(ext_ref, 1, spot_list[j], width, lane, used, moved_ref[j, 0] * imag - moved_ref[j, 1] * real)
        back_ref[j, 0] = win_ref[j, 0] * real + win_ref[j, 1] * imag
        back_ref[j, 1] = win_ref[j, 0] * imag - win_ref[j, 1] * real

    return finish


def wave_kernel(
    numbers_ref, tile_ref, below_ref, upper_ref, lower_ref, corner_ref,
    cos_ref, sin_ref, probe_ref, amp_ref, table_ref,
    own_ref, down_ref, up_out_ref, low_out_ref, diag_ref, back_ref,
    ext_ref, other_ref, grad_ref, win_ref, moved_ref, scalar_ref, scalar_sem, *, spots, width,
):
    fetched = pltpu.make_async_copy(numbers_ref, scalar_ref, scalar_sem)
    fetched.start()
    lane = lanes_of(width)
    tile_px = own_ref.shape[1]
    halo = (tile_ref, below_ref, upper_ref, lower_ref, corner_ref)
    fill_ext(ext_ref, whole_pieces(halo, 0, tile_px, width))
    fill_ext(other_ref, whole_pieces(halo, 1, tile_px, width))
    grad_ref[...] = jnp.zeros(grad_ref.shape, jnp.float32)
    fetched.wait()
    spot_list = [place(scalar_ref, j) for j in range(spots)]
    light(ext_ref, spot_list, probe_ref, back_ref, width, lane)
    take_windows(other_ref, spot_list, win_ref, width, lane)
    finish = residual_end(scalar_ref, spots, spot_list, grad_ref, moved_ref, win_ref, back_ref, width, lane)
    interleave([
        joined(
            forward_steps(group, back_ref, moved_ref, cos_ref, sin_ref, table_ref, width),
            residual_steps(
                group, moved_ref, win_ref, lambda j: amp_ref[scalar_ref[0, 2 * spots + 1 + j]],
                finish, table_ref, width,
            ),
        )
        for group in groups_of(spots)
    ], LAG)
    emit(grad_ref, own_ref, down_ref, up_out_ref, low_out_ref, diag_ref, width)


def forward_kernel(
    numbers_ref, rest_ref, quad_ref, left_ref, right_ref, upper_ref, lower_ref, corner_ref,
    cos_ref, sin_ref, probe_ref, table_ref, moved_ref, ext_ref, enter_ref, scalar_ref, scalar_sem, *, spots, width,
):
    fetched = pltpu.make_async_copy(numbers_ref, scalar_ref, scalar_sem)
    fetched.start()
    lane = lanes_of(width)
    halo = (rest_ref, quad_ref, left_ref, right_ref, upper_ref, lower_ref, corner_ref)
    fill_ext(ext_ref, slice_pieces(halo, 0, rest_ref.shape[1], width))
    fetched.wait()
    spot_list = [place(scalar_ref, j) for j in range(spots)]
    light(ext_ref, spot_list, probe_ref, enter_ref, width, lane)
    interleave([
        forward_steps(group, enter_ref, moved_ref, cos_ref, sin_ref, table_ref, width)
        for group in groups_of(spots)
    ], LAG)


def residual_kernel(
    numbers_ref, rest_ref, quad_ref, left_ref, right_ref, upper_ref, lower_ref, corner_ref,
    moved_ref, amp_ref, table_ref,
    own_ref, down_ref, up_out_ref, low_out_ref, diag_ref, back_ref,
    ext_ref, grad_ref, win_ref, scalar_ref, scalar_sem, *, spots, width,
):
    fetched = pltpu.make_async_copy(numbers_ref, scalar_ref, scalar_sem)
    fetched.start()
    lane = lanes_of(width)
    halo = (rest_ref, quad_ref, left_ref, right_ref, upper_ref, lower_ref, corner_ref)
    fill_ext(ext_ref, slice_pieces(halo, 1, rest_ref.shape[1], width))
    grad_ref[...] = jnp.zeros(grad_ref.shape, jnp.float32)
    fetched.wait()
    spot_list = [place(scalar_ref, j) for j in range(spots)]
    take_windows(ext_ref, spot_list, win_ref, width, lane)
    finish = residual_end(scalar_ref, spots, spot_list, grad_ref, moved_ref, win_ref, back_ref, width, lane)
    interleave([
        residual_steps(
            group, moved_ref, win_ref, lambda j: amp_ref[scalar_ref[0, 2 * spots + 1 + j]],
            finish, table_ref, width,
        )
        for group in groups_of(spots)
    ], LAG)
    emit(grad_ref, own_ref, down_ref, up_out_ref, low_out_ref, diag_ref, width)


def backward_kernel(
    numbers_ref, back_ref, other_down_ref, cos_ref, sin_ref, probe_ref, table_ref,
    own_ref, down_ref, up_out_ref, low_out_ref, diag_ref, ext_ref, scalar_ref, scalar_sem, *, spots, width,
):
    fetched = pltpu.make_async_copy(numbers_ref, scalar_ref, scalar_sem)
    fetched.start()
    lane = lanes_of(width)
    down_ref[2:] = other_down_ref[...]
    waiting = [fetched]
    ext_ref[...] = jnp.zeros(ext_ref.shape, jnp.float32)

    def chain(group):
        half = right_side([(back_ref[j, 0], back_ref[j, 1]) for j in group], table_ref)
        yield True
        pairs = left_side(half, table_ref, width)
        yield True
        half = right_side([
            (cos_ref[...] * real + sin_ref[...] * imag, -(cos_ref[...] * imag - sin_ref[...] * real))
            for real, imag in pairs
        ], table_ref)
        yield True
        pairs = left_side(half, table_ref, width)
        yield True
        while waiting:
            waiting.pop().wait()
        total = scalar_ref[0, 2 * spots]
        for j, (real, negative) in zip(group, pairs):
            imag = -negative
            spot = place(scalar_ref, j)
            used = j < total
            scatter(ext_ref, 0, spot, width, lane, used, probe_ref[0] * real + probe_ref[1] * imag)
            scatter(ext_ref, 1, spot, width, lane, used, probe_ref[0] * imag - probe_ref[1] * real)

    interleave([chain(group) for group in groups_of(spots)], LAG)
    emit(ext_ref, own_ref, down_ref, up_out_ref, low_out_ref, diag_ref, width)


def step(value, gradient):
    return value - step_size * gradient


def rest_values(tile_ref, own_ref, above_ref, lower_ref, c, width):
    tile_px = own_ref.shape[1]
    top, low = slice(0, width), slice(width, tile_px)
    left, right = slice(0, width), slice(width, tile_px)
    yield top, right, step(tile_ref[c, top, right], own_ref[c, top, right] + above_ref[c, :, right])
    yield low, left, step(tile_ref[c, low, left], own_ref[c, low, left] + lower_ref[c])
    yield low, right, step(tile_ref[c, low, right], own_ref[c, low, right])


def quad_value(quad_ref, own_ref, above_ref, upper_ref, c, width):
    top, left = slice(0, width), slice(0, width)
    return step(quad_ref[c, top, left], own_ref[c, top, left] + above_ref[c, :, left] + upper_ref[c])


def update_low_kernel(tile_ref, own_one, own_two, low_one, low_two, left_one, left_two, *, width):
    tile_px = own_one.shape[1]
    low, left = slice(width, tile_px), slice(0, width)
    for s, (own_ref, low_ref, left_ref) in enumerate(((own_one, low_one, left_one), (own_two, low_two, left_two))):
        for c in range(2):
            left_ref[c] = step(tile_ref[s, c, low, left], own_ref[c, low, left] + low_ref[c])


def update_rest_kernel(
    tile_ref, own_one, own_two, above_ref, low_one, low_two, rest_one, rest_two, right_ref, *, width,
):
    parts = ((own_one, low_one, rest_one), (own_two, low_two, rest_two))
    for s, (own_ref, low_ref, rest_ref) in enumerate(parts):
        above = above_ref.at[pl.ds(2 * s, 2)]
        for c in range(2):
            pieces = list(rest_values(tile_ref.at[s], own_ref, above, low_ref, c, width))
            for rows, lanes, value in pieces:
                rest_ref[c, rows, lanes] = value
            right_ref[2 * s + c] = pieces[0][2]


def update_quad_kernel(
    tile_ref, own_one, own_two, above_ref, up_one, up_two, quad_one, quad_two, left_ref, *, width,
):
    parts = ((own_one, up_one, quad_one), (own_two, up_two, quad_two))
    for s, (own_ref, up_ref, quad_ref) in enumerate(parts):
        above = above_ref.at[pl.ds(2 * s, 2)]
        for c in range(2):
            value = quad_value(tile_ref.at[s], own_ref, above, up_ref, c, width)
            quad_ref[c] = value
            left_ref[2 * s + c] = value


def finish_rest_kernel(
    rest_one, rest_two, own_one, own_two, above_ref, low_one, low_two, out_ref, tile_ref, sem, *, width,
):
    parts = ((rest_one, own_one, low_one), (rest_two, own_two, low_two))
    for s, (rest_ref, own_ref, low_ref) in enumerate(parts):
        above = above_ref.at[pl.ds(2 * s, 2)]
        for c in range(2):
            for rows, lanes, value in rest_values(rest_ref, own_ref, above, low_ref, c, width):
                tile_ref[s, c, rows, lanes] = value
            tile_ref[s, c, :width, :width] = jnp.zeros((width, width), jnp.float32)
    copy = pltpu.make_async_copy(tile_ref, out_ref, sem)
    copy.start()
    copy.wait()


def finish_quad_kernel(
    quad_one, quad_two, own_one, own_two, above_ref, up_one, up_two, part_ref, out_ref, quads_ref, sem, *, width,
):
    del part_ref
    parts = ((quad_one, own_one, up_one), (quad_two, own_two, up_two))
    for s, (quad_ref, own_ref, up_ref) in enumerate(parts):
        above = above_ref.at[pl.ds(2 * s, 2)]
        for c in range(2):
            quads_ref[s, c] = quad_value(quad_ref, own_ref, above, up_ref, c, width)
    copy = pltpu.make_async_copy(quads_ref, out_ref.at[:, :, pl.ds(0, width), pl.ds(0, width)], sem)
    copy.start()
    copy.wait()


def stage_kernel(*refs):
    sems = refs[-1]
    count = (len(refs) - 1) // 2
    copies = [pltpu.make_async_copy(refs[k], refs[count + k], sems.at[k]) for k in range(count)]
    for copy in copies:
        copy.start()
    for copy in copies:
        copy.wait()


F32 = functools.partial(jax.ShapeDtypeStruct, dtype=jnp.float32)
SMEM = pl.BlockSpec(memory_space=pltpu.SMEM)
VMEM = pl.BlockSpec(memory_space=pltpu.VMEM)
SCALAR_SPACE = (pltpu.SMEM((1, LANES), jnp.int32), pltpu.SemaphoreType.DMA(()))
LIMIT = pltpu.CompilerParams(vmem_limit_bytes=16 * 1024 * 1024)


FAR = pl.BlockSpec(memory_space=pltpu.MemorySpace.HBM)


def call(kernel, scalars, arrays, outs, scratch, **static):
    return pl.pallas_call(
        functools.partial(kernel, **static),
        in_specs=[VMEM] * (len(scalars) + len(arrays)),
        out_specs=[VMEM] * len(outs),
        out_shape=outs,
        scratch_shapes=[*scratch, *(SCALAR_SPACE if scalars else ())],
        compiler_params=LIMIT,
    )(*scalars, *arrays)


def pack_kernel(whole_ref, up_ref, low_ref, top_ref, sems, *, width):
    tile_px = whole_ref.shape[2]
    left = pl.ds(0, width)
    copies = []
    for s in range(2):
        both = pl.ds(2 * s, 2)
        copies.append((whole_ref.at[s, :, pl.ds(0, width), left], up_ref.at[both]))
        copies.append((whole_ref.at[s, :, pl.ds(width, tile_px - width), left], low_ref.at[both]))
        copies.append((whole_ref.at[s, :, pl.ds(0, width), :], top_ref.at[both]))
    copies = [pltpu.make_async_copy(a, b, sems.at[k]) for k, (a, b) in enumerate(copies)]
    for copy in copies:
        copy.start()
    for copy in copies:
        copy.wait()


def in_hbm(array):
    return pltpu.with_memory_space_constraint(array, pltpu.MemorySpace.HBM)


def body(
    specimen_slices,
    illumination_probe,
    propagation_phase,
    amplitudes,
    positions,
    counts,
    measurement_index,
):
    tile_px = specimen_slices.shape[2]
    width = illumination_probe.shape[1]
    spots = positions.shape[2]
    ext = tile_px + width
    across = tile_px - width
    cos, sin = jnp.cos(propagation_phase), jnp.sin(propagation_phase)
    numbers = jnp.concatenate([positions.reshape(-1), counts.reshape(-1), measurement_index.reshape(-1)])
    numbers = jnp.pad(numbers, (0, LANES - numbers.shape[0])).reshape(1, LANES)
    scalars = (numbers,)
    static = dict(spots=spots, width=width)
    ext_space = pltpu.VMEM((2, ext // LANES, ext, LANES), jnp.float32)
    wave_space = pltpu.VMEM((spots, 2, width, width), jnp.float32)
    wave = F32((spots, 2, width, width))
    square = F32((2, width, width))
    squares = F32((4, width, width))
    whole = F32((2, tile_px, tile_px))
    strip = F32((2, width, tile_px))
    gradient = [whole, strip, square, square, square]

    left_up, left_low, top = pl.pallas_call(
        functools.partial(pack_kernel, width=width),
        in_specs=[FAR],
        out_specs=[VMEM] * 3,
        out_shape=[squares, squares, F32((4, width, tile_px))],
        scratch_shapes=[pltpu.SemaphoreType.DMA((6,))],
        compiler_params=LIMIT,
        name="pack",
    )(in_hbm(specimen_slices))
    upper = from_behind(left_up, "col", -1)
    lower = from_behind(left_low, "col", -1)
    below = from_behind(top, "row", -1)
    far = (specimen_slices, illumination_probe, amplitudes[0, 0], jnp.asarray(dft_operands(width)))
    tile, probe, measured, table = pl.pallas_call(
        stage_kernel,
        in_specs=[FAR] * len(far),
        out_specs=[VMEM] * len(far),
        out_shape=[jax.ShapeDtypeStruct(x.shape, x.dtype) for x in far],
        scratch_shapes=[pltpu.SemaphoreType.DMA((len(far),))],
        compiler_params=LIMIT,
        name="stage",
    )(*[in_hbm(x) for x in far])
    corner = from_behind(upper, "row", -1)
    for i in range(ITERS):
        if i == 0:
            own_two, down_two, up_two, low_two, diag_two, back = call(
                wave_kernel, scalars,
                (tile, below, upper, lower, corner, cos, sin, probe, measured, table),
                [*gradient, wave], [ext_space, ext_space, ext_space, wave_space, wave_space], **static,
            )
        else:
            (moved,) = call(
                forward_kernel, scalars, (*halo[0], cos, sin, probe, table),
                [wave], [ext_space, wave_space], **static,
            )
            own_two, down_two, up_two, low_two, diag_two, back = call(
                residual_kernel, scalars, (*halo[1], moved, measured, table),
                [*gradient, wave], [ext_space, ext_space, wave_space], **static,
            )
        low_two = from_behind(low_two, "col", 1)
        corner_two = from_behind(diag_two, "row", 1)
        own_one, down, up_one, low_one, diag_one = call(
            backward_kernel, scalars, (back, down_two, cos, sin, probe, table),
            [whole, F32((4, width, tile_px)), square, square, square], [ext_space], **static,
        )
        low_one = from_behind(low_one, "col", 1)
        corner_one = from_behind(diag_one, "row", 1)
        above = from_behind(down, "row", 1)
        up_two = up_two + corner_two
        up_one = up_one + corner_one
        up_two = from_behind(up_two, "col", 1)
        up_one = from_behind(up_one, "col", 1)
        if i + 1 < ITERS:
            left_one, left_two = call(
                update_low_kernel, (), (tile, own_one, own_two, low_one, low_two),
                [F32((2, across, width))] * 2, [], width=width,
            )
            lower_one = from_behind(left_one, "col", -1)
            rest_one, rest_two, right = call(
                update_rest_kernel, (), (tile, own_one, own_two, above, low_one, low_two),
                [whole, whole, F32((4, width, across))], [], width=width,
            )
            below_right = from_behind(right, "row", -1)
            quad_one, quad_two, left = call(
                update_quad_kernel, (),
                (tile, own_one, own_two, above, up_one, up_two),
                [square, square, squares], [], width=width,
            )
            upper_one = from_behind(quad_one, "col", -1)
            upper_two = from_behind(quad_two, "col", -1)
            below_left = from_behind(left, "row", -1)
            lower_two = from_behind(left_two, "col", -1)
            corner_one = from_behind(upper_one, "row", -1)
            corner_two = from_behind(upper_two, "row", -1)
            halo = (
                (rest_one, quad_one, below_left, below_right, upper_one, lower_one, corner_one),
                (rest_two, quad_two, below_left, below_right, upper_two, lower_two, corner_two),
            )
        else:
            part = pl.pallas_call(
                functools.partial(finish_rest_kernel, width=width),
                in_specs=[VMEM] * 7,
                out_specs=FAR,
                out_shape=F32(specimen_slices.shape),
                scratch_shapes=[
                    pltpu.VMEM(specimen_slices.shape, jnp.float32), pltpu.SemaphoreType.DMA(()),
                ],
                compiler_params=LIMIT,
                name="finish_rest",
            )(rest_one, rest_two, own_one, own_two, above, low_one, low_two)
            updated = pl.pallas_call(
                functools.partial(finish_quad_kernel, width=width),
                in_specs=[VMEM] * 7 + [FAR],
                out_specs=FAR,
                out_shape=F32(specimen_slices.shape),
                input_output_aliases={7: 0},
                scratch_shapes=[
                    pltpu.VMEM((2, 2, width, width), jnp.float32), pltpu.SemaphoreType.DMA(()),
                ],
                compiler_params=LIMIT,
                name="finish_quad",
            )(quad_one, quad_two, own_one, own_two, above, up_one, up_two, in_hbm(part))
    return updated


def solution(mesh):
    placed = (
        P(None, None, "row", "col"),
        P(),
        P(),
        P("row", "col", None, None, None),
        P("row", "col", None, None),
        P("row", "col"),
        P("row", "col", None),
    )

    return jax.shard_map(body, mesh=mesh, in_specs=placed, out_specs=P(None, None, "row", "col"), check_vma=False)
```

```python
import functools
import math

import jax
import jax.numpy as jnp
import ml_dtypes
import numpy as np
from jax import lax
from jax.experimental import pallas as pl
from jax.experimental.pallas import tpu as pltpu
from jax.sharding import PartitionSpec as P


ITERS = 2
LANES = 128

step_size = 0.02
floor_amp = 0.5


def from_behind(block, axis, distance):
    devices = range(lax.axis_size(axis))
    route = [((i - distance) % len(devices), i) for i in devices]
    return lax.ppermute(block, axis, route)


def two_parts(value):
    high = value.astype(ml_dtypes.bfloat16)
    low = (value - high.astype(np.float64)).astype(ml_dtypes.bfloat16)
    return high, low


def dft_operands(width):
    index = np.arange(width)
    angle = (index[:, None] * index[None, :] % width) * (2.0 * math.pi / width)
    real = np.cos(angle) / math.sqrt(width)
    imag = -np.sin(angle) / math.sqrt(width)
    right = np.block([[real, imag], [-imag, real]])
    right_high, right_low = two_parts(right)
    left_high, left_low = two_parts(right.T)
    return np.stack([right_high, right_low, left_high, left_low])


def split(value):
    high = value.astype(jnp.bfloat16)
    low = (value - high.astype(jnp.float32)).astype(jnp.bfloat16)
    return high, low


def rows_of(j, width):
    return slice(j * width, (j + 1) * width)


def product(left, right):
    return jnp.dot(left, right, preferred_element_type=jnp.float32)


def right_side(pairs, table_ref):
    high, low = split(jnp.concatenate([jnp.concatenate(pair, 1) for pair in pairs], 0))
    return product(high, table_ref[0]) + product(low, table_ref[0]) + product(high, table_ref[1])


def left_side(half, table_ref, width):
    count = half.shape[0] // width
    parts = [half[rows_of(k, width)] for k in range(count)]
    tall = [jnp.concatenate([part[:, :width], part[:, width:]], 0) for part in parts]
    high, low = split(jnp.concatenate(tall, 1))
    full = product(table_ref[2], high) + product(table_ref[2], low) + product(table_ref[3], high)
    return [(full[:width, rows_of(k, width)], full[width:, rows_of(k, width)]) for k in range(count)]


def interleave(chains, lag):
    waiting = [(n * lag, chain) for n, chain in enumerate(chains)]
    while waiting:
        after = []
        for delay, chain in waiting:
            if delay:
                after.append((delay - 1, chain))
            elif next(chain, None) is not None:
                after.append((0, chain))
        waiting = after


def fill_ext(ext_ref, pieces):
    for row, col, source in pieces:
        height, across = source.shape[1:]
        for c in range(2):
            for b in range(across // LANES):
                ext_ref[c, col // LANES + b, row:row + height, :] = source[c, :, b * LANES:(b + 1) * LANES]


def pick(numbers_ref, k):
    values = numbers_ref[...].astype(jnp.float32)
    lane = lax.broadcasted_iota(jnp.int32, values.shape, 1)
    return jnp.sum(jnp.where(lane == k, values, 0.0)).astype(jnp.int32)


def places(numbers_ref, spots):
    spot_list = []
    for j in range(spots):
        row, col = pick(numbers_ref, 2 * j), pick(numbers_ref, 2 * j + 1)
        spot_list.append((row, col // LANES, col % LANES))
    return spot_list


def window(ext_ref, c, spot, width, lane):
    row, block, shift = spot
    near = ext_ref[c, block, pl.ds(row, width), :]
    far = ext_ref[c, block + 1, pl.ds(row, width), :]
    return pltpu.roll(jnp.where(lane >= shift, near, far), LANES - shift, 1)


def scatter(grad_ref, c, spot, width, lane, used, update):
    row, block, shift = spot
    turned = pltpu.roll(jnp.where(used, update, 0.0), shift, 1)
    near = lane >= shift
    grad_ref[c, block, pl.ds(row, width), :] += jnp.where(near, turned, 0.0)
    grad_ref[c, block + 1, pl.ds(row, width), :] += jnp.where(near, 0.0, turned)


def emit(grad_ref, own_ref, down_ref, upper_ref, lower_ref, diag_ref, width):
    tile_px = own_ref.shape[1]
    blocks = tile_px // LANES
    for c in range(2):
        for b in range(blocks):
            lanes = slice(b * LANES, (b + 1) * LANES)
            own_ref[c, :, lanes] = grad_ref[c, b, :tile_px, :]
            down_ref[c, :, lanes] = grad_ref[c, b, tile_px:, :]
        upper_ref[c] = grad_ref[c, blocks, :width, :]
        lower_ref[c] = grad_ref[c, blocks, width:tile_px, :]
        diag_ref[c] = grad_ref[c, blocks, tile_px:, :]


def lanes_of(width):
    return lax.broadcasted_iota(jnp.int32, (width, LANES), 1)


LAG = 1


def groups_of(spots):
    return [range(j, min(j + 2, spots)) for j in range(0, spots, 2)]


def forward_steps(group, enter_ref, leave_ref, cos_ref, sin_ref, table_ref, width):
    half = right_side([(enter_ref[j, 0], enter_ref[j, 1]) for j in group], table_ref)
    yield True
    pairs = left_side(half, table_ref, width)
    yield True
    half = right_side([
        (cos_ref[...] * real - sin_ref[...] * imag, -(cos_ref[...] * imag + sin_ref[...] * real))
        for real, imag in pairs
    ], table_ref)
    yield True
    pairs = left_side(half, table_ref, width)
    yield True
    for j, (real, negative) in zip(group, pairs):
        leave_ref[j, 0] = real
        leave_ref[j, 1] = -negative


def residual_steps(group, moved_ref, win_ref, measured_of, finish, table_ref, width):
    half = right_side([
        (
            moved_ref[j, 0] * win_ref[j, 0] - moved_ref[j, 1] * win_ref[j, 1],
            moved_ref[j, 0] * win_ref[j, 1] + moved_ref[j, 1] * win_ref[j, 0],
        )
        for j in group
    ], table_ref)
    yield True
    pairs = left_side(half, table_ref, width)
    yield True
    residuals = []
    for j, (real, imag) in zip(group, pairs):
        power = jnp.maximum(real * real + imag * imag, floor_amp * floor_amp)
        factor = 1.0 - measured_of(j) * lax.rsqrt(power)
        residuals.append((real * factor, -(imag * factor)))
    half = right_side(residuals, table_ref)
    yield True
    pairs = left_side(half, table_ref, width)
    yield True
    for j, (real, negative) in zip(group, pairs):
        finish(j, real, -negative)


def joined(*parts):
    for part in parts:
        yield from part


def whole_pieces(refs, s, tile_px, width):
    tile_ref, below_ref, upper_ref, lower_ref, corner_ref = refs
    both = pl.ds(2 * s, 2)
    return [
        (0, 0, tile_ref.at[s]),
        (tile_px, 0, below_ref.at[both]),
        (0, tile_px, upper_ref.at[both]),
        (width, tile_px, lower_ref.at[both]),
        (tile_px, tile_px, corner_ref.at[both]),
    ]


def slice_pieces(refs, s, tile_px, width):
    rest_ref, quad_ref, below_left_ref, below_right_ref, upper_ref, lower_ref, corner_ref = refs
    both = pl.ds(2 * s, 2)
    across = tile_px - width
    return [
        (width, 0, rest_ref.at[:, pl.ds(width, across), :]),
        (0, width, rest_ref.at[:, pl.ds(0, width), pl.ds(width, across)]),
        (0, 0, quad_ref),
        (tile_px, 0, below_left_ref.at[both]),
        (tile_px, width, below_right_ref.at[both]),
        (0, tile_px, upper_ref),
        (width, tile_px, lower_ref),
        (tile_px, tile_px, corner_ref),
    ]


def take_windows(ext_ref, spot_list, win_ref, width, lane):
    for j, spot in enumerate(spot_list):
        win_ref[j, 0] = window(ext_ref, 0, spot, width, lane)
        win_ref[j, 1] = window(ext_ref, 1, spot, width, lane)


def light(ext_ref, spot_list, probe_ref, enter_ref, width, lane):
    for j, spot in enumerate(spot_list):
        real = window(ext_ref, 0, spot, width, lane)
        imag = window(ext_ref, 1, spot, width, lane)
        enter_ref[j, 0] = probe_ref[0] * real - probe_ref[1] * imag
        enter_ref[j, 1] = probe_ref[0] * imag + probe_ref[1] * real


def residual_end(numbers_ref, spots, spot_list, ext_ref, moved_ref, win_ref, back_ref, width, lane):
    total = pick(numbers_ref, 2 * spots)

    def finish(j, real, imag):
        used = j < total
        scatter(ext_ref, 0, spot_list[j], width, lane, used, moved_ref[j, 0] * real + moved_ref[j, 1] * imag)
        scatter(ext_ref, 1, spot_list[j], width, lane, used, moved_ref[j, 0] * imag - moved_ref[j, 1] * real)
        back_ref[j, 0] = win_ref[j, 0] * real + win_ref[j, 1] * imag
        back_ref[j, 1] = win_ref[j, 0] * imag - win_ref[j, 1] * real

    return finish


def wave_kernel(
    numbers_ref, tile_ref, below_ref, upper_ref, lower_ref, corner_ref,
    cos_ref, sin_ref, probe_ref, amp_ref, table_ref,
    own_ref, down_ref, up_out_ref, low_out_ref, diag_ref, back_ref,
    ext_ref, other_ref, grad_ref, win_ref, moved_ref, *, spots, width,
):
    lane = lanes_of(width)
    tile_px = own_ref.shape[1]
    halo = (tile_ref, below_ref, upper_ref, lower_ref, corner_ref)
    fill_ext(ext_ref, whole_pieces(halo, 0, tile_px, width))
    fill_ext(other_ref, whole_pieces(halo, 1, tile_px, width))
    grad_ref[...] = jnp.zeros(grad_ref.shape, jnp.float32)
    spot_list = places(numbers_ref, spots)
    light(ext_ref, spot_list, probe_ref, back_ref, width, lane)
    take_windows(other_ref, spot_list, win_ref, width, lane)
    finish = residual_end(numbers_ref, spots, spot_list, grad_ref, moved_ref, win_ref, back_ref, width, lane)
    interleave([
        joined(
            forward_steps(group, back_ref, moved_ref, cos_ref, sin_ref, table_ref, width),
            residual_steps(
                group, moved_ref, win_ref, lambda j: amp_ref[pick(numbers_ref, 2 * spots + 1 + j)],
                finish, table_ref, width,
            ),
        )
        for group in groups_of(spots)
    ], LAG)
    emit(grad_ref, own_ref, down_ref, up_out_ref, low_out_ref, diag_ref, width)


def forward_kernel(
    numbers_ref, rest_ref, quad_ref, left_ref, right_ref, upper_ref, lower_ref, corner_ref,
    cos_ref, sin_ref, probe_ref, table_ref, moved_ref, ext_ref, enter_ref, *, spots, width,
):
    lane = lanes_of(width)
    halo = (rest_ref, quad_ref, left_ref, right_ref, upper_ref, lower_ref, corner_ref)
    fill_ext(ext_ref, slice_pieces(halo, 0, rest_ref.shape[1], width))
    spot_list = places(numbers_ref, spots)
    light(ext_ref, spot_list, probe_ref, enter_ref, width, lane)
    interleave([
        forward_steps(group, enter_ref, moved_ref, cos_ref, sin_ref, table_ref, width)
        for group in groups_of(spots)
    ], LAG)


def residual_kernel(
    numbers_ref, rest_ref, quad_ref, left_ref, right_ref, upper_ref, lower_ref, corner_ref,
    moved_ref, amp_ref, table_ref,
    own_ref, down_ref, up_out_ref, low_out_ref, diag_ref, back_ref,
    ext_ref, grad_ref, win_ref, *, spots, width,
):
    lane = lanes_of(width)
    halo = (rest_ref, quad_ref, left_ref, right_ref, upper_ref, lower_ref, corner_ref)
    fill_ext(ext_ref, slice_pieces(halo, 1, rest_ref.shape[1], width))
    grad_ref[...] = jnp.zeros(grad_ref.shape, jnp.float32)
    spot_list = places(numbers_ref, spots)
    take_windows(ext_ref, spot_list, win_ref, width, lane)
    finish = residual_end(numbers_ref, spots, spot_list, grad_ref, moved_ref, win_ref, back_ref, width, lane)
    interleave([
        residual_steps(
            group, moved_ref, win_ref, lambda j: amp_ref[pick(numbers_ref, 2 * spots + 1 + j)],
            finish, table_ref, width,
        )
        for group in groups_of(spots)
    ], LAG)
    emit(grad_ref, own_ref, down_ref, up_out_ref, low_out_ref, diag_ref, width)


def backward_kernel(
    numbers_ref, back_ref, other_down_ref, cos_ref, sin_ref, probe_ref, table_ref,
    own_ref, down_ref, up_out_ref, low_out_ref, diag_ref, ext_ref, *, spots, width,
):
    lane = lanes_of(width)
    down_ref[2:] = other_down_ref[...]
    spot_list = places(numbers_ref, spots)
    total = pick(numbers_ref, 2 * spots)
    ext_ref[...] = jnp.zeros(ext_ref.shape, jnp.float32)

    def chain(group):
        half = right_side([(back_ref[j, 0], back_ref[j, 1]) for j in group], table_ref)
        yield True
        pairs = left_side(half, table_ref, width)
        yield True
        half = right_side([
            (cos_ref[...] * real + sin_ref[...] * imag, -(cos_ref[...] * imag - sin_ref[...] * real))
            for real, imag in pairs
        ], table_ref)
        yield True
        pairs = left_side(half, table_ref, width)
        yield True
        for j, (real, negative) in zip(group, pairs):
            imag = -negative
            spot = spot_list[j]
            used = j < total
            scatter(ext_ref, 0, spot, width, lane, used, probe_ref[0] * real + probe_ref[1] * imag)
            scatter(ext_ref, 1, spot, width, lane, used, probe_ref[0] * imag - probe_ref[1] * real)

    interleave([chain(group) for group in groups_of(spots)], LAG)
    emit(ext_ref, own_ref, down_ref, up_out_ref, low_out_ref, diag_ref, width)


def step(value, gradient):
    return value - step_size * gradient


def rest_values(tile_ref, own_ref, above_ref, lower_ref, c, width):
    tile_px = own_ref.shape[1]
    top, low = slice(0, width), slice(width, tile_px)
    left, right = slice(0, width), slice(width, tile_px)
    yield top, right, step(tile_ref[c, top, right], own_ref[c, top, right] + above_ref[c, :, right])
    yield low, left, step(tile_ref[c, low, left], own_ref[c, low, left] + lower_ref[c])
    yield low, right, step(tile_ref[c, low, right], own_ref[c, low, right])


def quad_value(quad_ref, own_ref, above_ref, upper_ref, c, width):
    top, left = slice(0, width), slice(0, width)
    return step(quad_ref[c, top, left], own_ref[c, top, left] + above_ref[c, :, left] + upper_ref[c])


def update_low_kernel(tile_ref, own_one, own_two, low_one, low_two, left_one, left_two, *, width):
    tile_px = own_one.shape[1]
    low, left = slice(width, tile_px), slice(0, width)
    for s, (own_ref, low_ref, left_ref) in enumerate(((own_one, low_one, left_one), (own_two, low_two, left_two))):
        for c in range(2):
            left_ref[c] = step(tile_ref[s, c, low, left], own_ref[c, low, left] + low_ref[c])


def update_rest_kernel(
    tile_ref, own_one, own_two, above_ref, low_one, low_two, rest_one, rest_two, right_ref, *, width,
):
    parts = ((own_one, low_one, rest_one), (own_two, low_two, rest_two))
    for s, (own_ref, low_ref, rest_ref) in enumerate(parts):
        above = above_ref.at[pl.ds(2 * s, 2)]
        for c in range(2):
            pieces = list(rest_values(tile_ref.at[s], own_ref, above, low_ref, c, width))
            for rows, lanes, value in pieces:
                rest_ref[c, rows, lanes] = value
            right_ref[2 * s + c] = pieces[0][2]


def update_quad_kernel(
    tile_ref, own_one, own_two, above_ref, up_one, up_two, quad_one, quad_two, left_ref, *, width,
):
    parts = ((own_one, up_one, quad_one), (own_two, up_two, quad_two))
    for s, (own_ref, up_ref, quad_ref) in enumerate(parts):
        above = above_ref.at[pl.ds(2 * s, 2)]
        for c in range(2):
            value = quad_value(tile_ref.at[s], own_ref, above, up_ref, c, width)
            quad_ref[c] = value
            left_ref[2 * s + c] = value


def finish_kernel(
    rest_one, rest_two, quad_one, quad_two, own_one, own_two, above_ref, low_one, low_two, up_one, up_two,
    out_ref, tile_ref, sems, *, width,
):
    parts = ((rest_one, quad_one, own_one, low_one, up_one), (rest_two, quad_two, own_two, low_two, up_two))
    copies = []
    for s in (1, 0):
        rest_ref, quad_ref, own_ref, low_ref, up_ref = parts[s]
        above = above_ref.at[pl.ds(2 * s, 2)]
        for c in range(2):
            for rows, lanes, value in rest_values(rest_ref, own_ref, above, low_ref, c, width):
                tile_ref[s, c, rows, lanes] = value
            tile_ref[s, c, :width, :width] = quad_value(quad_ref, own_ref, above, up_ref, c, width)
            copies.append(pltpu.make_async_copy(tile_ref.at[s, c], out_ref.at[s, c], sems.at[len(copies)]))
            copies[-1].start()
    for copy in copies:
        copy.wait()


def stage_kernel(*refs):
    sems = refs[-1]
    count = (len(refs) - 1) // 2
    copies = [pltpu.make_async_copy(refs[k], refs[count + k], sems.at[k]) for k in range(count)]
    for copy in copies:
        copy.start()
    for copy in copies:
        copy.wait()


F32 = functools.partial(jax.ShapeDtypeStruct, dtype=jnp.float32)
VMEM = pl.BlockSpec(memory_space=pltpu.VMEM)
LIMIT = pltpu.CompilerParams(vmem_limit_bytes=16 * 1024 * 1024)


FAR = pl.BlockSpec(memory_space=pltpu.MemorySpace.HBM)


def call(kernel, scalars, arrays, outs, scratch, **static):
    return pl.pallas_call(
        functools.partial(kernel, **static),
        in_specs=[VMEM] * (len(scalars) + len(arrays)),
        out_specs=[VMEM] * len(outs),
        out_shape=outs,
        scratch_shapes=scratch,
        compiler_params=LIMIT,
    )(*scalars, *arrays)


def pack_kernel(whole_ref, *refs, boxes):
    outs, sems = refs[:-1], refs[-1]
    copies = []
    for (rows, lanes), out_ref in zip(boxes, outs):
        for s in range(2):
            source = whole_ref.at[s, :, pl.ds(*rows), pl.ds(*lanes)]
            copies.append(pltpu.make_async_copy(source, out_ref.at[pl.ds(2 * s, 2)], sems.at[len(copies)]))
    for copy in copies:
        copy.start()
    for copy in copies:
        copy.wait()


def pack(whole, boxes):
    return pl.pallas_call(
        functools.partial(pack_kernel, boxes=boxes),
        in_specs=[FAR],
        out_specs=[VMEM] * len(boxes),
        out_shape=[F32((4, rows[1], lanes[1])) for rows, lanes in boxes],
        scratch_shapes=[pltpu.SemaphoreType.DMA((2 * len(boxes),))],
        compiler_params=LIMIT,
    )(in_hbm(whole))


def in_hbm(array):
    return pltpu.with_memory_space_constraint(array, pltpu.MemorySpace.HBM)


def body(
    specimen_slices,
    illumination_probe,
    propagation_phase,
    amplitudes,
    positions,
    counts,
    measurement_index,
):
    tile_px = specimen_slices.shape[2]
    width = illumination_probe.shape[1]
    spots = positions.shape[2]
    ext = tile_px + width
    across = tile_px - width
    cos, sin = jnp.cos(propagation_phase), jnp.sin(propagation_phase)
    numbers = jnp.concatenate([positions.reshape(-1), counts.reshape(-1), measurement_index.reshape(-1)])
    numbers = jnp.pad(numbers, (0, LANES - numbers.shape[0])).reshape(1, LANES)
    scalars = (numbers,)
    static = dict(spots=spots, width=width)
    ext_space = pltpu.VMEM((2, ext // LANES, ext, LANES), jnp.float32)
    wave_space = pltpu.VMEM((spots, 2, width, width), jnp.float32)
    wave = F32((spots, 2, width, width))
    square = F32((2, width, width))
    squares = F32((4, width, width))
    whole = F32((2, tile_px, tile_px))
    strip = F32((2, width, tile_px))
    gradient = [whole, strip, square, square, square]

    (left_up,) = pack(specimen_slices, [((0, width), (0, width))])
    upper = from_behind(left_up, "col", -1)
    left_low, top = pack(specimen_slices, [((width, across), (0, width)), ((0, width), (0, tile_px))])
    lower = from_behind(left_low, "col", -1)
    below = from_behind(top, "row", -1)
    far = (specimen_slices, illumination_probe, amplitudes[0, 0], jnp.asarray(dft_operands(width)))
    tile, probe, measured, table = pl.pallas_call(
        stage_kernel,
        in_specs=[FAR] * len(far),
        out_specs=[VMEM] * len(far),
        out_shape=[jax.ShapeDtypeStruct(x.shape, x.dtype) for x in far],
        scratch_shapes=[pltpu.SemaphoreType.DMA((len(far),))],
        compiler_params=LIMIT,
        name="stage",
    )(*[in_hbm(x) for x in far])
    corner = from_behind(upper, "row", -1)
    for i in range(ITERS):
        if i == 0:
            own_two, down_two, up_two, low_two, diag_two, back = call(
                wave_kernel, scalars,
                (tile, below, upper, lower, corner, cos, sin, probe, measured, table),
                [*gradient, wave], [ext_space, ext_space, ext_space, wave_space, wave_space], **static,
            )
        else:
            (moved,) = call(
                forward_kernel, scalars, (*halo[0], cos, sin, probe, table),
                [wave], [ext_space, wave_space], **static,
            )
            own_two, down_two, up_two, low_two, diag_two, back = call(
                residual_kernel, scalars, (*halo[1], moved, measured, table),
                [*gradient, wave], [ext_space, ext_space, wave_space], **static,
            )
        low_two = from_behind(low_two, "col", 1)
        corner_two = from_behind(diag_two, "row", 1)
        own_one, down, up_one, low_one, diag_one = call(
            backward_kernel, scalars, (back, down_two, cos, sin, probe, table),
            [whole, F32((4, width, tile_px)), square, square, square], [ext_space], **static,
        )
        low_one = from_behind(low_one, "col", 1)
        corner_one = from_behind(diag_one, "row", 1)
        above = from_behind(down, "row", 1)
        up_two = up_two + corner_two
        up_one = up_one + corner_one
        up_two = from_behind(up_two, "col", 1)
        up_one = from_behind(up_one, "col", 1)
        if i + 1 < ITERS:
            left_one, left_two = call(
                update_low_kernel, (), (tile, own_one, own_two, low_one, low_two),
                [F32((2, across, width))] * 2, [], width=width,
            )
            lower_one = from_behind(left_one, "col", -1)
            rest_one, rest_two, right = call(
                update_rest_kernel, (), (tile, own_one, own_two, above, low_one, low_two),
                [whole, whole, F32((4, width, across))], [], width=width,
            )
            below_right = from_behind(right, "row", -1)
            quad_one, quad_two, left = call(
                update_quad_kernel, (),
                (tile, own_one, own_two, above, up_one, up_two),
                [square, square, squares], [], width=width,
            )
            upper_one = from_behind(quad_one, "col", -1)
            upper_two = from_behind(quad_two, "col", -1)
            below_left = from_behind(left, "row", -1)
            lower_two = from_behind(left_two, "col", -1)
            corner_one = from_behind(upper_one, "row", -1)
            corner_two = from_behind(upper_two, "row", -1)
            halo = (
                (rest_one, quad_one, below_left, below_right, upper_one, lower_one, corner_one),
                (rest_two, quad_two, below_left, below_right, upper_two, lower_two, corner_two),
            )
        else:
            updated = pl.pallas_call(
                functools.partial(finish_kernel, width=width),
                in_specs=[VMEM] * 11,
                out_specs=FAR,
                out_shape=F32(specimen_slices.shape),
                scratch_shapes=[
                    pltpu.VMEM(specimen_slices.shape, jnp.float32), pltpu.SemaphoreType.DMA((4,)),
                ],
                compiler_params=LIMIT,
                name="finish",
            )(
                rest_one, rest_two, quad_one, quad_two, own_one, own_two, above,
                low_one, low_two, up_one, up_two,
            )
    return updated


def solution(mesh):
    placed = (
        P(None, None, "row", "col"),
        P(),
        P(),
        P("row", "col", None, None, None),
        P("row", "col", None, None),
        P("row", "col"),
        P("row", "col", None),
    )

    return jax.shard_map(body, mesh=mesh, in_specs=placed, out_specs=P(None, None, "row", "col"), check_vma=False)
```

```python
import functools
import math

import jax
import jax.numpy as jnp
import ml_dtypes
import numpy as np
from jax import lax
from jax.experimental import pallas as pl
from jax.experimental.pallas import tpu as pltpu
from jax.sharding import PartitionSpec as P


ITERS = 2
LANES = 128

step_size = 0.02
floor_amp = 0.5


def from_behind(block, axis, distance):
    devices = range(lax.axis_size(axis))
    route = [((i - distance) % len(devices), i) for i in devices]
    return lax.ppermute(block, axis, route)


def two_parts(value):
    high = value.astype(ml_dtypes.bfloat16)
    low = (value - high.astype(np.float64)).astype(ml_dtypes.bfloat16)
    return high, low


def dft_operands(width):
    index = np.arange(width)
    angle = (index[:, None] * index[None, :] % width) * (2.0 * math.pi / width)
    real = np.cos(angle) / math.sqrt(width)
    imag = -np.sin(angle) / math.sqrt(width)
    right = np.block([[real, imag], [-imag, real]])
    right_high, right_low = two_parts(right)
    left_high, left_low = two_parts(right.T)
    return np.stack([right_high, right_low, left_high, left_low])


def split(value):
    high = value.astype(jnp.bfloat16)
    low = (value - high.astype(jnp.float32)).astype(jnp.bfloat16)
    return high, low


def rows_of(j, width):
    return slice(j * width, (j + 1) * width)


def product(left, right):
    return jnp.dot(left, right, preferred_element_type=jnp.float32)


def right_side(pairs, table_ref):
    high, low = split(jnp.concatenate([jnp.concatenate(pair, 1) for pair in pairs], 0))
    return product(high, table_ref[0]) + product(low, table_ref[0]) + product(high, table_ref[1])


def left_side(half, table_ref, width):
    count = half.shape[0] // width
    parts = [half[rows_of(k, width)] for k in range(count)]
    tall = [jnp.concatenate([part[:, :width], part[:, width:]], 0) for part in parts]
    high, low = split(jnp.concatenate(tall, 1))
    full = product(table_ref[2], high) + product(table_ref[2], low) + product(table_ref[3], high)
    return [(full[:width, rows_of(k, width)], full[width:, rows_of(k, width)]) for k in range(count)]


def interleave(chains, lag):
    waiting = [(n * lag, chain) for n, chain in enumerate(chains)]
    while waiting:
        after = []
        for delay, chain in waiting:
            if delay:
                after.append((delay - 1, chain))
            elif next(chain, None) is not None:
                after.append((0, chain))
        waiting = after


def fill_ext(ext_ref, pieces):
    for row, col, source in pieces:
        height, across = source.shape[1:]
        for c in range(2):
            for b in range(across // LANES):
                ext_ref[c, col // LANES + b, row:row + height, :] = source[c, :, b * LANES:(b + 1) * LANES]


def pick(numbers_ref, k):
    values = numbers_ref[...].astype(jnp.float32)
    lane = lax.broadcasted_iota(jnp.int32, values.shape, 1)
    return jnp.sum(jnp.where(lane == k, values, 0.0)).astype(jnp.int32)


def places(numbers_ref, spots):
    spot_list = []
    for j in range(spots):
        row, col = pick(numbers_ref, 2 * j), pick(numbers_ref, 2 * j + 1)
        spot_list.append((row, col // LANES, col % LANES))
    return spot_list


def window(ext_ref, c, spot, width, lane):
    row, block, shift = spot
    near = ext_ref[c, block, pl.ds(row, width), :]
    far = ext_ref[c, block + 1, pl.ds(row, width), :]
    return pltpu.roll(jnp.where(lane >= shift, near, far), LANES - shift, 1)


def scatter(grad_ref, c, spot, width, lane, used, update):
    row, block, shift = spot
    turned = pltpu.roll(jnp.where(used, update, 0.0), shift, 1)
    near = lane >= shift
    grad_ref[c, block, pl.ds(row, width), :] += jnp.where(near, turned, 0.0)
    grad_ref[c, block + 1, pl.ds(row, width), :] += jnp.where(near, 0.0, turned)


def emit(grad_ref, own_ref, down_ref, upper_ref, lower_ref, diag_ref, width):
    tile_px = own_ref.shape[1]
    blocks = tile_px // LANES
    for c in range(2):
        for b in range(blocks):
            lanes = slice(b * LANES, (b + 1) * LANES)
            own_ref[c, :, lanes] = grad_ref[c, b, :tile_px, :]
            down_ref[c, :, lanes] = grad_ref[c, b, tile_px:, :]
        upper_ref[c] = grad_ref[c, blocks, :width, :]
        lower_ref[c] = grad_ref[c, blocks, width:tile_px, :]
        diag_ref[c] = grad_ref[c, blocks, tile_px:, :]


def lanes_of(width):
    return lax.broadcasted_iota(jnp.int32, (width, LANES), 1)


LAG = 1


def groups_of(spots):
    return [range(j, min(j + 2, spots)) for j in range(0, spots, 2)]


def forward_steps(group, enter_ref, leave_ref, cos_ref, sin_ref, table_ref, width):
    half = right_side([(enter_ref[j, 0], enter_ref[j, 1]) for j in group], table_ref)
    yield True
    pairs = left_side(half, table_ref, width)
    yield True
    half = right_side([
        (cos_ref[...] * real - sin_ref[...] * imag, -(cos_ref[...] * imag + sin_ref[...] * real))
        for real, imag in pairs
    ], table_ref)
    yield True
    pairs = left_side(half, table_ref, width)
    yield True
    for j, (real, negative) in zip(group, pairs):
        leave_ref[j, 0] = real
        leave_ref[j, 1] = -negative


def residual_steps(group, moved_ref, win_ref, measured_of, finish, table_ref, width):
    half = right_side([
        (
            moved_ref[j, 0] * win_ref[j, 0] - moved_ref[j, 1] * win_ref[j, 1],
            moved_ref[j, 0] * win_ref[j, 1] + moved_ref[j, 1] * win_ref[j, 0],
        )
        for j in group
    ], table_ref)
    yield True
    pairs = left_side(half, table_ref, width)
    yield True
    residuals = []
    for j, (real, imag) in zip(group, pairs):
        power = jnp.maximum(real * real + imag * imag, floor_amp * floor_amp)
        factor = 1.0 - measured_of(j) * lax.rsqrt(power)
        residuals.append((real * factor, -(imag * factor)))
    half = right_side(residuals, table_ref)
    yield True
    pairs = left_side(half, table_ref, width)
    yield True
    for j, (real, negative) in zip(group, pairs):
        finish(j, real, -negative)


def joined(*parts):
    for part in parts:
        yield from part


def whole_pieces(refs, s, tile_px, width):
    tile_ref, below_ref, upper_ref, lower_ref, corner_ref = refs
    both = pl.ds(2 * s, 2)
    return [
        (0, 0, tile_ref.at[s]),
        (tile_px, 0, below_ref.at[both]),
        (0, tile_px, upper_ref),
        (width, tile_px, lower_ref.at[both]),
        (tile_px, tile_px, corner_ref),
    ]


def slice_pieces(refs, s, tile_px, width):
    rest_ref, quad_ref, below_left_ref, below_right_ref, upper_ref, lower_ref, corner_ref = refs
    both = pl.ds(2 * s, 2)
    across = tile_px - width
    return [
        (width, 0, rest_ref.at[:, pl.ds(width, across), :]),
        (0, width, rest_ref.at[:, pl.ds(0, width), pl.ds(width, across)]),
        (0, 0, quad_ref),
        (tile_px, 0, below_left_ref.at[both]),
        (tile_px, width, below_right_ref.at[both]),
        (0, tile_px, upper_ref),
        (width, tile_px, lower_ref),
        (tile_px, tile_px, corner_ref),
    ]


def take_windows(ext_ref, spot_list, win_ref, width, lane):
    for j, spot in enumerate(spot_list):
        win_ref[j, 0] = window(ext_ref, 0, spot, width, lane)
        win_ref[j, 1] = window(ext_ref, 1, spot, width, lane)


def light(ext_ref, spot_list, probe_ref, enter_ref, width, lane):
    for j, spot in enumerate(spot_list):
        real = window(ext_ref, 0, spot, width, lane)
        imag = window(ext_ref, 1, spot, width, lane)
        enter_ref[j, 0] = probe_ref[0] * real - probe_ref[1] * imag
        enter_ref[j, 1] = probe_ref[0] * imag + probe_ref[1] * real


def residual_end(numbers_ref, spots, spot_list, ext_ref, moved_ref, win_ref, back_ref, width, lane):
    total = pick(numbers_ref, 2 * spots)

    def finish(j, real, imag):
        used = j < total
        scatter(ext_ref, 0, spot_list[j], width, lane, used, moved_ref[j, 0] * real + moved_ref[j, 1] * imag)
        scatter(ext_ref, 1, spot_list[j], width, lane, used, moved_ref[j, 0] * imag - moved_ref[j, 1] * real)
        back_ref[j, 0] = win_ref[j, 0] * real + win_ref[j, 1] * imag
        back_ref[j, 1] = win_ref[j, 0] * imag - win_ref[j, 1] * real

    return finish


def wave_kernel(
    numbers_ref, tile_ref, below_ref, upper_one, upper_two, lower_ref, corner_one, corner_two,
    cos_ref, sin_ref, probe_ref, amp_ref, table_ref,
    own_ref, down_ref, up_out_ref, low_out_ref, diag_ref, back_ref,
    ext_ref, other_ref, grad_ref, win_ref, moved_ref, *, spots, width,
):
    lane = lanes_of(width)
    tile_px = own_ref.shape[1]
    first = (tile_ref, below_ref, upper_one, lower_ref, corner_one)
    second = (tile_ref, below_ref, upper_two, lower_ref, corner_two)
    fill_ext(ext_ref, whole_pieces(first, 0, tile_px, width))
    fill_ext(other_ref, whole_pieces(second, 1, tile_px, width))
    grad_ref[...] = jnp.zeros(grad_ref.shape, jnp.float32)
    spot_list = places(numbers_ref, spots)
    light(ext_ref, spot_list, probe_ref, back_ref, width, lane)
    take_windows(other_ref, spot_list, win_ref, width, lane)
    finish = residual_end(numbers_ref, spots, spot_list, grad_ref, moved_ref, win_ref, back_ref, width, lane)
    interleave([
        joined(
            forward_steps(group, back_ref, moved_ref, cos_ref, sin_ref, table_ref, width),
            residual_steps(
                group, moved_ref, win_ref, lambda j: amp_ref[pick(numbers_ref, 2 * spots + 1 + j)],
                finish, table_ref, width,
            ),
        )
        for group in groups_of(spots)
    ], LAG)
    emit(grad_ref, own_ref, down_ref, up_out_ref, low_out_ref, diag_ref, width)


def forward_kernel(
    numbers_ref, rest_ref, quad_ref, left_ref, right_ref, upper_ref, lower_ref, corner_ref,
    cos_ref, sin_ref, probe_ref, table_ref, moved_ref, ext_ref, enter_ref, *, spots, width,
):
    lane = lanes_of(width)
    halo = (rest_ref, quad_ref, left_ref, right_ref, upper_ref, lower_ref, corner_ref)
    fill_ext(ext_ref, slice_pieces(halo, 0, rest_ref.shape[1], width))
    spot_list = places(numbers_ref, spots)
    light(ext_ref, spot_list, probe_ref, enter_ref, width, lane)
    interleave([
        forward_steps(group, enter_ref, moved_ref, cos_ref, sin_ref, table_ref, width)
        for group in groups_of(spots)
    ], LAG)


def residual_kernel(
    numbers_ref, rest_ref, quad_ref, left_ref, right_ref, upper_ref, lower_ref, corner_ref,
    moved_ref, amp_ref, table_ref,
    own_ref, down_ref, up_out_ref, low_out_ref, diag_ref, back_ref,
    ext_ref, grad_ref, win_ref, *, spots, width,
):
    lane = lanes_of(width)
    halo = (rest_ref, quad_ref, left_ref, right_ref, upper_ref, lower_ref, corner_ref)
    fill_ext(ext_ref, slice_pieces(halo, 1, rest_ref.shape[1], width))
    grad_ref[...] = jnp.zeros(grad_ref.shape, jnp.float32)
    spot_list = places(numbers_ref, spots)
    take_windows(ext_ref, spot_list, win_ref, width, lane)
    finish = residual_end(numbers_ref, spots, spot_list, grad_ref, moved_ref, win_ref, back_ref, width, lane)
    interleave([
        residual_steps(
            group, moved_ref, win_ref, lambda j: amp_ref[pick(numbers_ref, 2 * spots + 1 + j)],
            finish, table_ref, width,
        )
        for group in groups_of(spots)
    ], LAG)
    emit(grad_ref, own_ref, down_ref, up_out_ref, low_out_ref, diag_ref, width)


def backward_kernel(
    numbers_ref, back_ref, other_down_ref, cos_ref, sin_ref, probe_ref, table_ref,
    own_ref, down_ref, up_out_ref, low_out_ref, diag_ref, ext_ref, *, spots, width,
):
    lane = lanes_of(width)
    down_ref[2:] = other_down_ref[...]
    spot_list = places(numbers_ref, spots)
    total = pick(numbers_ref, 2 * spots)
    ext_ref[...] = jnp.zeros(ext_ref.shape, jnp.float32)

    def chain(group):
        half = right_side([(back_ref[j, 0], back_ref[j, 1]) for j in group], table_ref)
        yield True
        pairs = left_side(half, table_ref, width)
        yield True
        half = right_side([
            (cos_ref[...] * real + sin_ref[...] * imag, -(cos_ref[...] * imag - sin_ref[...] * real))
            for real, imag in pairs
        ], table_ref)
        yield True
        pairs = left_side(half, table_ref, width)
        yield True
        for j, (real, negative) in zip(group, pairs):
            imag = -negative
            spot = spot_list[j]
            used = j < total
            scatter(ext_ref, 0, spot, width, lane, used, probe_ref[0] * real + probe_ref[1] * imag)
            scatter(ext_ref, 1, spot, width, lane, used, probe_ref[0] * imag - probe_ref[1] * real)

    interleave([chain(group) for group in groups_of(spots)], LAG)
    emit(ext_ref, own_ref, down_ref, up_out_ref, low_out_ref, diag_ref, width)


def step(value, gradient):
    return value - step_size * gradient


def rest_values(tile_ref, own_ref, above_ref, lower_ref, c, width):
    top, right = slice(0, width), slice(width, own_ref.shape[1])
    yield top, right, step(tile_ref[c, top, right], own_ref[c, top, right] + above_ref[c, :, right])
    yield from low_values(tile_ref, own_ref, lower_ref, c, width)


def low_values(tile_ref, own_ref, lower_ref, c, width):
    tile_px = own_ref.shape[1]
    low, left, right = slice(width, tile_px), slice(0, width), slice(width, tile_px)
    yield low, left, step(tile_ref[c, low, left], own_ref[c, low, left] + lower_ref[c])
    yield low, right, step(tile_ref[c, low, right], own_ref[c, low, right])


def quad_value(quad_ref, own_ref, above_ref, upper_ref, c, width):
    top, left = slice(0, width), slice(0, width)
    return step(quad_ref[c, top, left], own_ref[c, top, left] + above_ref[c, :, left] + upper_ref[c])


def update_low_kernel(tile_ref, own_one, own_two, low_one, low_two, left_one, left_two, *, width):
    tile_px = own_one.shape[1]
    low, left = slice(width, tile_px), slice(0, width)
    for s, (own_ref, low_ref, left_ref) in enumerate(((own_one, low_one, left_one), (own_two, low_two, left_two))):
        for c in range(2):
            left_ref[c] = step(tile_ref[s, c, low, left], own_ref[c, low, left] + low_ref[c])


def update_rest_kernel(
    tile_ref, own_one, own_two, above_ref, low_one, low_two, rest_one, rest_two, right_ref, *, width,
):
    parts = ((own_one, low_one, rest_one), (own_two, low_two, rest_two))
    for s, (own_ref, low_ref, rest_ref) in enumerate(parts):
        above = above_ref.at[pl.ds(2 * s, 2)]
        for c in range(2):
            pieces = list(rest_values(tile_ref.at[s], own_ref, above, low_ref, c, width))
            for rows, lanes, value in pieces:
                rest_ref[c, rows, lanes] = value
            right_ref[2 * s + c] = pieces[0][2]


def update_quad_kernel(
    tile_ref, own_one, own_two, above_ref, up_one, up_two, quad_one, quad_two, left_ref, *, width,
):
    parts = ((own_one, up_one, quad_one), (own_two, up_two, quad_two))
    for s, (own_ref, up_ref, quad_ref) in enumerate(parts):
        above = above_ref.at[pl.ds(2 * s, 2)]
        for c in range(2):
            value = quad_value(tile_ref.at[s], own_ref, above, up_ref, c, width)
            quad_ref[c] = value
            left_ref[2 * s + c] = value


def finish_low_kernel(
    rest_one, rest_two, own_one, own_two, low_one, low_two, out_ref, rows_ref, sem, *, width,
):
    tile_px = own_one.shape[1]
    for s, (rest_ref, own_ref, low_ref) in enumerate(((rest_one, own_one, low_one), (rest_two, own_two, low_two))):
        for c in range(2):
            for _, lanes, value in low_values(rest_ref, own_ref, low_ref, c, width):
                rows_ref[s, c, :, lanes] = value
    copy = pltpu.make_async_copy(rows_ref, out_ref.at[:, :, pl.ds(width, tile_px - width), :], sem)
    copy.start()
    copy.wait()


def finish_top_kernel(
    rest_one, rest_two, quad_one, quad_two, own_one, own_two, above_ref, up_one, up_two, part_ref,
    out_ref, rows_ref, sem, *, width,
):
    del part_ref
    tile_px = own_one.shape[1]
    parts = ((rest_one, quad_one, own_one, up_one), (rest_two, quad_two, own_two, up_two))
    for s, (rest_ref, quad_ref, own_ref, up_ref) in enumerate(parts):
        above = above_ref.at[pl.ds(2 * s, 2)]
        for c in range(2):
            top, right = slice(0, width), slice(width, tile_px)
            rows_ref[s, c, :, :width] = quad_value(quad_ref, own_ref, above, up_ref, c, width)
            rows_ref[s, c, :, width:] = step(rest_ref[c, top, right], own_ref[c, top, right] + above[c, :, right])
    copy = pltpu.make_async_copy(rows_ref, out_ref.at[:, :, pl.ds(0, width), :], sem)
    copy.start()
    copy.wait()


def stage_kernel(*refs):
    sems = refs[-1]
    count = (len(refs) - 1) // 2
    copies = [pltpu.make_async_copy(refs[k], refs[count + k], sems.at[k]) for k in range(count)]
    for copy in copies:
        copy.start()
    for copy in copies:
        copy.wait()


F32 = functools.partial(jax.ShapeDtypeStruct, dtype=jnp.float32)
VMEM = pl.BlockSpec(memory_space=pltpu.VMEM)
LIMIT = pltpu.CompilerParams(vmem_limit_bytes=16 * 1024 * 1024)


FAR = pl.BlockSpec(memory_space=pltpu.MemorySpace.HBM)


def call(kernel, scalars, arrays, outs, scratch, **static):
    return pl.pallas_call(
        functools.partial(kernel, **static),
        in_specs=[VMEM] * (len(scalars) + len(arrays)),
        out_specs=[VMEM] * len(outs),
        out_shape=outs,
        scratch_shapes=scratch,
        compiler_params=LIMIT,
    )(*scalars, *arrays)


def pack_kernel(whole_ref, *refs, boxes):
    outs, sems = refs[:-1], refs[-1]
    copies = []
    for (slices, rows, lanes), out_ref in zip(boxes, outs):
        for k, s in enumerate(slices):
            source = whole_ref.at[s, :, pl.ds(*rows), pl.ds(*lanes)]
            copies.append(pltpu.make_async_copy(source, out_ref.at[pl.ds(2 * k, 2)], sems.at[len(copies)]))
    for copy in copies:
        copy.start()
    for copy in copies:
        copy.wait()


def pack(whole, boxes):
    count = sum(len(slices) for slices, _, _ in boxes)
    return pl.pallas_call(
        functools.partial(pack_kernel, boxes=boxes),
        in_specs=[FAR],
        out_specs=[VMEM] * len(boxes),
        out_shape=[F32((2 * len(slices), rows[1], lanes[1])) for slices, rows, lanes in boxes],
        scratch_shapes=[pltpu.SemaphoreType.DMA((count,))],
        compiler_params=LIMIT,
    )(in_hbm(whole))


def in_hbm(array):
    return pltpu.with_memory_space_constraint(array, pltpu.MemorySpace.HBM)


def body(
    specimen_slices,
    illumination_probe,
    propagation_phase,
    amplitudes,
    positions,
    counts,
    measurement_index,
):
    tile_px = specimen_slices.shape[2]
    width = illumination_probe.shape[1]
    spots = positions.shape[2]
    ext = tile_px + width
    across = tile_px - width
    cos, sin = jnp.cos(propagation_phase), jnp.sin(propagation_phase)
    numbers = jnp.concatenate([positions.reshape(-1), counts.reshape(-1), measurement_index.reshape(-1)])
    numbers = jnp.pad(numbers, (0, LANES - numbers.shape[0])).reshape(1, LANES)
    scalars = (numbers,)
    static = dict(spots=spots, width=width)
    ext_space = pltpu.VMEM((2, ext // LANES, ext, LANES), jnp.float32)
    wave_space = pltpu.VMEM((spots, 2, width, width), jnp.float32)
    wave = F32((spots, 2, width, width))
    square = F32((2, width, width))
    squares = F32((4, width, width))
    whole = F32((2, tile_px, tile_px))
    strip = F32((2, width, tile_px))
    gradient = [whole, strip, square, square, square]

    left, low, full = (0, width), (width, across), (0, tile_px)
    up_one, up_two = pack(specimen_slices, [((0,), left, left), ((1,), left, left)])
    upper_one = from_behind(up_one, "col", -1)
    upper_two = from_behind(up_two, "col", -1)
    left_low, top = pack(specimen_slices, [((0, 1), low, left), ((0, 1), left, full)])
    lower = from_behind(left_low, "col", -1)
    below = from_behind(top, "row", -1)
    far = (specimen_slices, illumination_probe, amplitudes[0, 0], jnp.asarray(dft_operands(width)))
    tile, probe, measured, table = pl.pallas_call(
        stage_kernel,
        in_specs=[FAR] * len(far),
        out_specs=[VMEM] * len(far),
        out_shape=[jax.ShapeDtypeStruct(x.shape, x.dtype) for x in far],
        scratch_shapes=[pltpu.SemaphoreType.DMA((len(far),))],
        compiler_params=LIMIT,
        name="stage",
    )(*[in_hbm(x) for x in far])
    corner_one = from_behind(upper_one, "row", -1)
    corner_two = from_behind(upper_two, "row", -1)
    for i in range(ITERS):
        if i == 0:
            own_two, down_two, up_two, low_two, diag_two, back = call(
                wave_kernel, scalars,
                (tile, below, upper_one, upper_two, lower, corner_one, corner_two, cos, sin, probe, measured, table),
                [*gradient, wave], [ext_space, ext_space, ext_space, wave_space, wave_space], **static,
            )
        else:
            (moved,) = call(
                forward_kernel, scalars, (*halo[0], cos, sin, probe, table),
                [wave], [ext_space, wave_space], **static,
            )
            own_two, down_two, up_two, low_two, diag_two, back = call(
                residual_kernel, scalars, (*halo[1], moved, measured, table),
                [*gradient, wave], [ext_space, ext_space, wave_space], **static,
            )
        low_two = from_behind(low_two, "col", 1)
        corner_two = from_behind(diag_two, "row", 1)
        own_one, down, up_one, low_one, diag_one = call(
            backward_kernel, scalars, (back, down_two, cos, sin, probe, table),
            [whole, F32((4, width, tile_px)), square, square, square], [ext_space], **static,
        )
        low_one = from_behind(low_one, "col", 1)
        corner_one = from_behind(diag_one, "row", 1)
        above = from_behind(down, "row", 1)
        up_two = up_two + corner_two
        up_one = up_one + corner_one
        up_two = from_behind(up_two, "col", 1)
        up_one = from_behind(up_one, "col", 1)
        if i + 1 < ITERS:
            left_one, left_two = call(
                update_low_kernel, (), (tile, own_one, own_two, low_one, low_two),
                [F32((2, across, width))] * 2, [], width=width,
            )
            lower_one = from_behind(left_one, "col", -1)
            rest_one, rest_two, right = call(
                update_rest_kernel, (), (tile, own_one, own_two, above, low_one, low_two),
                [whole, whole, F32((4, width, across))], [], width=width,
            )
            below_right = from_behind(right, "row", -1)
            quad_one, quad_two, left = call(
                update_quad_kernel, (),
                (tile, own_one, own_two, above, up_one, up_two),
                [square, square, squares], [], width=width,
            )
            upper_one = from_behind(quad_one, "col", -1)
            upper_two = from_behind(quad_two, "col", -1)
            below_left = from_behind(left, "row", -1)
            lower_two = from_behind(left_two, "col", -1)
            corner_one = from_behind(upper_one, "row", -1)
            corner_two = from_behind(upper_two, "row", -1)
            halo = (
                (rest_one, quad_one, below_left, below_right, upper_one, lower_one, corner_one),
                (rest_two, quad_two, below_left, below_right, upper_two, lower_two, corner_two),
            )
        else:
            end = dict(
                out_specs=FAR,
                out_shape=F32(specimen_slices.shape),
                compiler_params=LIMIT,
            )
            part = pl.pallas_call(
                functools.partial(finish_low_kernel, width=width),
                in_specs=[VMEM] * 6,
                scratch_shapes=[
                    pltpu.VMEM((2, 2, across, tile_px), jnp.float32), pltpu.SemaphoreType.DMA(()),
                ],
                name="finish_low",
                **end,
            )(rest_one, rest_two, own_one, own_two, low_one, low_two)
            updated = pl.pallas_call(
                functools.partial(finish_top_kernel, width=width),
                in_specs=[VMEM] * 9 + [FAR],
                input_output_aliases={9: 0},
                scratch_shapes=[
                    pltpu.VMEM((2, 2, width, tile_px), jnp.float32), pltpu.SemaphoreType.DMA(()),
                ],
                name="finish_top",
                **end,
            )(
                rest_one, rest_two, quad_one, quad_two, own_one, own_two, above, up_one, up_two, in_hbm(part),
            )
    return updated


def solution(mesh):
    placed = (
        P(None, None, "row", "col"),
        P(),
        P(),
        P("row", "col", None, None, None),
        P("row", "col", None, None),
        P("row", "col"),
        P("row", "col", None),
    )

    return jax.shard_map(body, mesh=mesh, in_specs=placed, out_specs=P(None, None, "row", "col"), check_vma=False)
```

```python
import functools
import math

import jax
import jax.numpy as jnp
import ml_dtypes
import numpy as np
from jax import lax
from jax.experimental import pallas as pl
from jax.experimental.pallas import tpu as pltpu
from jax.sharding import PartitionSpec as P


ITERS = 2
LANES = 128

step_size = 0.02
floor_amp = 0.5


def from_behind(block, axis, distance):
    devices = range(lax.axis_size(axis))
    route = [((i - distance) % len(devices), i) for i in devices]
    return lax.ppermute(block, axis, route)


def two_parts(value):
    high = value.astype(ml_dtypes.bfloat16)
    low = (value - high.astype(np.float64)).astype(ml_dtypes.bfloat16)
    return high, low


def dft_operands(width):
    index = np.arange(width)
    angle = (index[:, None] * index[None, :] % width) * (2.0 * math.pi / width)
    real = np.cos(angle) / math.sqrt(width)
    imag = -np.sin(angle) / math.sqrt(width)
    right = np.block([[real, imag], [-imag, real]])
    right_high, right_low = two_parts(right)
    left_high, left_low = two_parts(right.T)
    return np.stack([right_high, right_low, left_high, left_low])


def split(value):
    high = value.astype(jnp.bfloat16)
    low = (value - high.astype(jnp.float32)).astype(jnp.bfloat16)
    return high, low


def rows_of(j, width):
    return slice(j * width, (j + 1) * width)


def product(left, right):
    return jnp.dot(left, right, preferred_element_type=jnp.float32)


def right_side(pairs, table_ref):
    high, low = split(jnp.concatenate([jnp.concatenate(pair, 1) for pair in pairs], 0))
    return product(high, table_ref[0]) + product(low, table_ref[0]) + product(high, table_ref[1])


def left_side(half, table_ref, width):
    count = half.shape[0] // width
    parts = [half[rows_of(k, width)] for k in range(count)]
    tall = [jnp.concatenate([part[:, :width], part[:, width:]], 0) for part in parts]
    high, low = split(jnp.concatenate(tall, 1))
    full = product(table_ref[2], high) + product(table_ref[2], low) + product(table_ref[3], high)
    return [(full[:width, rows_of(k, width)], full[width:, rows_of(k, width)]) for k in range(count)]


def interleave(chains, lag):
    waiting = [(n * lag, chain) for n, chain in enumerate(chains)]
    while waiting:
        after = []
        for delay, chain in waiting:
            if delay:
                after.append((delay - 1, chain))
            elif next(chain, None) is not None:
                after.append((0, chain))
        waiting = after


def fill_ext(ext_ref, pieces):
    for row, col, source in pieces:
        height, across = source.shape[1:]
        for c in range(2):
            for b in range(across // LANES):
                ext_ref[c, col // LANES + b, row:row + height, :] = source[c, :, b * LANES:(b + 1) * LANES]


def pick(numbers_ref, k):
    values = numbers_ref[...].astype(jnp.float32)
    lane = lax.broadcasted_iota(jnp.int32, values.shape, 1)
    return jnp.sum(jnp.where(lane == k, values, 0.0)).astype(jnp.int32)


def places(numbers_ref, spots):
    spot_list = []
    for j in range(spots):
        row, col = pick(numbers_ref, 2 * j), pick(numbers_ref, 2 * j + 1)
        spot_list.append((row, col // LANES, col % LANES))
    return spot_list


def window(ext_ref, c, spot, width, lane):
    row, block, shift = spot
    near = ext_ref[c, block, pl.ds(row, width), :]
    far = ext_ref[c, block + 1, pl.ds(row, width), :]
    return pltpu.roll(jnp.where(lane >= shift, near, far), LANES - shift, 1)


def scatter(grad_ref, c, spot, width, lane, used, update):
    row, block, shift = spot
    turned = pltpu.roll(jnp.where(used, update, 0.0), shift, 1)
    near = lane >= shift
    grad_ref[c, block, pl.ds(row, width), :] += jnp.where(near, turned, 0.0)
    grad_ref[c, block + 1, pl.ds(row, width), :] += jnp.where(near, 0.0, turned)


def emit(grad_ref, own_ref, down_ref, upper_ref, lower_ref, diag_ref, width):
    tile_px = own_ref.shape[1]
    blocks = tile_px // LANES
    for c in range(2):
        for b in range(blocks):
            lanes = slice(b * LANES, (b + 1) * LANES)
            own_ref[c, :, lanes] = grad_ref[c, b, :tile_px, :]
            down_ref[c, :, lanes] = grad_ref[c, b, tile_px:, :]
        upper_ref[c] = grad_ref[c, blocks, :width, :]
        lower_ref[c] = grad_ref[c, blocks, width:tile_px, :]
        diag_ref[c] = grad_ref[c, blocks, tile_px:, :]


def lanes_of(width):
    return lax.broadcasted_iota(jnp.int32, (width, LANES), 1)


LAG = 1


def groups_of(spots):
    return [range(j, min(j + 2, spots)) for j in range(0, spots, 2)]


def forward_steps(group, enter_ref, leave_ref, cos_ref, sin_ref, table_ref, width):
    half = right_side([(enter_ref[j, 0], enter_ref[j, 1]) for j in group], table_ref)
    yield True
    pairs = left_side(half, table_ref, width)
    yield True
    half = right_side([
        (cos_ref[...] * real - sin_ref[...] * imag, -(cos_ref[...] * imag + sin_ref[...] * real))
        for real, imag in pairs
    ], table_ref)
    yield True
    pairs = left_side(half, table_ref, width)
    yield True
    for j, (real, negative) in zip(group, pairs):
        leave_ref[j, 0] = real
        leave_ref[j, 1] = -negative


def residual_steps(group, moved_ref, win_ref, measured_of, finish, table_ref, width):
    half = right_side([
        (
            moved_ref[j, 0] * win_ref[j, 0] - moved_ref[j, 1] * win_ref[j, 1],
            moved_ref[j, 0] * win_ref[j, 1] + moved_ref[j, 1] * win_ref[j, 0],
        )
        for j in group
    ], table_ref)
    yield True
    pairs = left_side(half, table_ref, width)
    yield True
    residuals = []
    for j, (real, imag) in zip(group, pairs):
        power = jnp.maximum(real * real + imag * imag, floor_amp * floor_amp)
        factor = 1.0 - measured_of(j) * lax.rsqrt(power)
        residuals.append((real * factor, -(imag * factor)))
    half = right_side(residuals, table_ref)
    yield True
    pairs = left_side(half, table_ref, width)
    yield True
    for j, (real, negative) in zip(group, pairs):
        finish(j, real, -negative)


def joined(*parts):
    for part in parts:
        yield from part


def whole_pieces(refs, s, tile_px, width):
    tile_ref, below_ref, upper_ref, lower_ref, corner_ref = refs
    both = pl.ds(2 * s, 2)
    return [
        (0, 0, tile_ref.at[s]),
        (tile_px, 0, below_ref.at[both]),
        (0, tile_px, upper_ref),
        (width, tile_px, lower_ref.at[both]),
        (tile_px, tile_px, corner_ref),
    ]


def slice_pieces(refs, s, tile_px, width):
    rest_ref, quad_ref, below_left_ref, below_right_ref, upper_ref, lower_ref, corner_ref = refs
    both = pl.ds(2 * s, 2)
    across = tile_px - width
    return [
        (width, 0, rest_ref.at[:, pl.ds(width, across), :]),
        (0, width, rest_ref.at[:, pl.ds(0, width), pl.ds(width, across)]),
        (0, 0, quad_ref),
        (tile_px, 0, below_left_ref.at[both]),
        (tile_px, width, below_right_ref.at[both]),
        (0, tile_px, upper_ref),
        (width, tile_px, lower_ref),
        (tile_px, tile_px, corner_ref),
    ]


def take_windows(ext_ref, spot_list, win_ref, width, lane):
    for j, spot in enumerate(spot_list):
        win_ref[j, 0] = window(ext_ref, 0, spot, width, lane)
        win_ref[j, 1] = window(ext_ref, 1, spot, width, lane)


def light(ext_ref, spot_list, probe_ref, enter_ref, width, lane):
    for j, spot in enumerate(spot_list):
        real = window(ext_ref, 0, spot, width, lane)
        imag = window(ext_ref, 1, spot, width, lane)
        enter_ref[j, 0] = probe_ref[0] * real - probe_ref[1] * imag
        enter_ref[j, 1] = probe_ref[0] * imag + probe_ref[1] * real


def residual_end(numbers_ref, spots, spot_list, ext_ref, moved_ref, win_ref, back_ref, width, lane):
    total = pick(numbers_ref, 2 * spots)

    def finish(j, real, imag):
        used = j < total
        scatter(ext_ref, 0, spot_list[j], width, lane, used, moved_ref[j, 0] * real + moved_ref[j, 1] * imag)
        scatter(ext_ref, 1, spot_list[j], width, lane, used, moved_ref[j, 0] * imag - moved_ref[j, 1] * real)
        back_ref[j, 0] = win_ref[j, 0] * real + win_ref[j, 1] * imag
        back_ref[j, 1] = win_ref[j, 0] * imag - win_ref[j, 1] * real

    return finish


def wave_kernel(
    numbers_ref, tile_ref, below_ref, upper_one, upper_two, lower_ref, corner_one, corner_two,
    cos_ref, sin_ref, probe_ref, amp_ref, table_ref,
    own_ref, down_ref, up_out_ref, low_out_ref, diag_ref, back_ref,
    ext_ref, other_ref, grad_ref, win_ref, moved_ref, *, spots, width,
):
    lane = lanes_of(width)
    tile_px = own_ref.shape[1]
    first = (tile_ref, below_ref, upper_one, lower_ref, corner_one)
    second = (tile_ref, below_ref, upper_two, lower_ref, corner_two)
    fill_ext(ext_ref, whole_pieces(first, 0, tile_px, width))
    fill_ext(other_ref, whole_pieces(second, 1, tile_px, width))
    grad_ref[...] = jnp.zeros(grad_ref.shape, jnp.float32)
    spot_list = places(numbers_ref, spots)
    light(ext_ref, spot_list, probe_ref, back_ref, width, lane)
    take_windows(other_ref, spot_list, win_ref, width, lane)
    finish = residual_end(numbers_ref, spots, spot_list, grad_ref, moved_ref, win_ref, back_ref, width, lane)
    interleave([
        joined(
            forward_steps(group, back_ref, moved_ref, cos_ref, sin_ref, table_ref, width),
            residual_steps(
                group, moved_ref, win_ref, lambda j: amp_ref[pick(numbers_ref, 2 * spots + 1 + j)],
                finish, table_ref, width,
            ),
        )
        for group in groups_of(spots)
    ], LAG)
    emit(grad_ref, own_ref, down_ref, up_out_ref, low_out_ref, diag_ref, width)


def forward_kernel(
    numbers_ref, rest_ref, quad_ref, left_ref, right_ref, upper_ref, lower_ref, corner_ref,
    cos_ref, sin_ref, probe_ref, table_ref, moved_ref, ext_ref, enter_ref, *, spots, width,
):
    lane = lanes_of(width)
    halo = (rest_ref, quad_ref, left_ref, right_ref, upper_ref, lower_ref, corner_ref)
    fill_ext(ext_ref, slice_pieces(halo, 0, rest_ref.shape[1], width))
    spot_list = places(numbers_ref, spots)
    light(ext_ref, spot_list, probe_ref, enter_ref, width, lane)
    interleave([
        forward_steps(group, enter_ref, moved_ref, cos_ref, sin_ref, table_ref, width)
        for group in groups_of(spots)
    ], LAG)


def residual_kernel(
    numbers_ref, rest_ref, quad_ref, left_ref, right_ref, upper_ref, lower_ref, corner_ref,
    moved_ref, amp_ref, table_ref,
    own_ref, down_ref, up_out_ref, low_out_ref, diag_ref, back_ref,
    ext_ref, grad_ref, win_ref, *, spots, width,
):
    lane = lanes_of(width)
    halo = (rest_ref, quad_ref, left_ref, right_ref, upper_ref, lower_ref, corner_ref)
    fill_ext(ext_ref, slice_pieces(halo, 1, rest_ref.shape[1], width))
    grad_ref[...] = jnp.zeros(grad_ref.shape, jnp.float32)
    spot_list = places(numbers_ref, spots)
    take_windows(ext_ref, spot_list, win_ref, width, lane)
    finish = residual_end(numbers_ref, spots, spot_list, grad_ref, moved_ref, win_ref, back_ref, width, lane)
    interleave([
        residual_steps(
            group, moved_ref, win_ref, lambda j: amp_ref[pick(numbers_ref, 2 * spots + 1 + j)],
            finish, table_ref, width,
        )
        for group in groups_of(spots)
    ], LAG)
    emit(grad_ref, own_ref, down_ref, up_out_ref, low_out_ref, diag_ref, width)


def backward_kernel(
    numbers_ref, back_ref, other_down_ref, cos_ref, sin_ref, probe_ref, table_ref,
    own_ref, down_ref, up_out_ref, low_out_ref, diag_ref, ext_ref, *, spots, width,
):
    lane = lanes_of(width)
    down_ref[2:] = other_down_ref[...]
    spot_list = places(numbers_ref, spots)
    total = pick(numbers_ref, 2 * spots)
    ext_ref[...] = jnp.zeros(ext_ref.shape, jnp.float32)

    def chain(group):
        half = right_side([(back_ref[j, 0], back_ref[j, 1]) for j in group], table_ref)
        yield True
        pairs = left_side(half, table_ref, width)
        yield True
        half = right_side([
            (cos_ref[...] * real + sin_ref[...] * imag, -(cos_ref[...] * imag - sin_ref[...] * real))
            for real, imag in pairs
        ], table_ref)
        yield True
        pairs = left_side(half, table_ref, width)
        yield True
        for j, (real, negative) in zip(group, pairs):
            imag = -negative
            spot = spot_list[j]
            used = j < total
            scatter(ext_ref, 0, spot, width, lane, used, probe_ref[0] * real + probe_ref[1] * imag)
            scatter(ext_ref, 1, spot, width, lane, used, probe_ref[0] * imag - probe_ref[1] * real)

    interleave([chain(group) for group in groups_of(spots)], LAG)
    emit(ext_ref, own_ref, down_ref, up_out_ref, low_out_ref, diag_ref, width)


def step(value, gradient):
    return value - step_size * gradient


def rest_values(tile_ref, own_ref, above_ref, lower_ref, c, width):
    top, right = slice(0, width), slice(width, own_ref.shape[1])
    yield top, right, step(tile_ref[c, top, right], own_ref[c, top, right] + above_ref[c, :, right])
    yield from low_values(tile_ref, own_ref, lower_ref, c, width)


def low_values(tile_ref, own_ref, lower_ref, c, width):
    tile_px = own_ref.shape[1]
    low, left, right = slice(width, tile_px), slice(0, width), slice(width, tile_px)
    yield low, left, step(tile_ref[c, low, left], own_ref[c, low, left] + lower_ref[c])
    yield low, right, step(tile_ref[c, low, right], own_ref[c, low, right])


def quad_value(quad_ref, own_ref, above_ref, upper_ref, c, width):
    top, left = slice(0, width), slice(0, width)
    return step(quad_ref[c, top, left], own_ref[c, top, left] + above_ref[c, :, left] + upper_ref[c])


def update_low_kernel(tile_ref, own_one, own_two, low_one, low_two, left_one, left_two, *, width):
    tile_px = own_one.shape[1]
    low, left = slice(width, tile_px), slice(0, width)
    for s, (own_ref, low_ref, left_ref) in enumerate(((own_one, low_one, left_one), (own_two, low_two, left_two))):
        for c in range(2):
            left_ref[c] = step(tile_ref[s, c, low, left], own_ref[c, low, left] + low_ref[c])


def update_rest_kernel(
    tile_ref, own_one, own_two, above_ref, low_one, low_two, rest_one, rest_two, right_ref, *, width,
):
    parts = ((own_one, low_one, rest_one), (own_two, low_two, rest_two))
    for s, (own_ref, low_ref, rest_ref) in enumerate(parts):
        above = above_ref.at[pl.ds(2 * s, 2)]
        for c in range(2):
            pieces = list(rest_values(tile_ref.at[s], own_ref, above, low_ref, c, width))
            for rows, lanes, value in pieces:
                rest_ref[c, rows, lanes] = value
            right_ref[2 * s + c] = pieces[0][2]


def update_quad_kernel(
    tile_ref, own_one, own_two, above_ref, up_one, up_two, quad_one, quad_two, left_ref, *, width,
):
    parts = ((own_one, up_one, quad_one), (own_two, up_two, quad_two))
    for s, (own_ref, up_ref, quad_ref) in enumerate(parts):
        above = above_ref.at[pl.ds(2 * s, 2)]
        for c in range(2):
            value = quad_value(tile_ref.at[s], own_ref, above, up_ref, c, width)
            quad_ref[c] = value
            left_ref[2 * s + c] = value


def finish_low_kernel(
    rest_one, rest_two, own_one, own_two, low_one, low_two, out_ref, rows_ref, sem, *, width,
):
    tile_px = own_one.shape[1]
    for s, (rest_ref, own_ref, low_ref) in enumerate(((rest_one, own_one, low_one), (rest_two, own_two, low_two))):
        for c in range(2):
            for _, lanes, value in low_values(rest_ref, own_ref, low_ref, c, width):
                rows_ref[s, c, :, lanes] = value
    copy = pltpu.make_async_copy(rows_ref, out_ref.at[:, :, pl.ds(width, tile_px - width), :], sem)
    copy.start()
    copy.wait()


def finish_top_kernel(
    rest_one, rest_two, quad_one, quad_two, own_one, own_two, above_ref, up_one, up_two, part_ref,
    out_ref, rows_ref, sem, *, width,
):
    del part_ref
    tile_px = own_one.shape[1]
    parts = ((rest_one, quad_one, own_one, up_one), (rest_two, quad_two, own_two, up_two))
    for s, (rest_ref, quad_ref, own_ref, up_ref) in enumerate(parts):
        above = above_ref.at[pl.ds(2 * s, 2)]
        for c in range(2):
            top, right = slice(0, width), slice(width, tile_px)
            rows_ref[s, c, :, :width] = quad_value(quad_ref, own_ref, above, up_ref, c, width)
            rows_ref[s, c, :, width:] = step(rest_ref[c, top, right], own_ref[c, top, right] + above[c, :, right])
    copy = pltpu.make_async_copy(rows_ref, out_ref.at[:, :, pl.ds(0, width), :], sem)
    copy.start()
    copy.wait()


def stage_kernel(*refs):
    sems = refs[-1]
    count = (len(refs) - 1) // 2
    copies = [pltpu.make_async_copy(refs[k], refs[count + k], sems.at[k]) for k in range(count)]
    for copy in copies:
        copy.start()
    for copy in copies:
        copy.wait()


F32 = functools.partial(jax.ShapeDtypeStruct, dtype=jnp.float32)
VMEM = pl.BlockSpec(memory_space=pltpu.VMEM)
LIMIT = pltpu.CompilerParams(vmem_limit_bytes=16 * 1024 * 1024)


FAR = pl.BlockSpec(memory_space=pltpu.MemorySpace.HBM)


def call(kernel, scalars, arrays, outs, scratch, **static):
    return pl.pallas_call(
        functools.partial(kernel, **static),
        in_specs=[VMEM] * (len(scalars) + len(arrays)),
        out_specs=[VMEM] * len(outs),
        out_shape=outs,
        scratch_shapes=scratch,
        compiler_params=LIMIT,
    )(*scalars, *arrays)


def pack_kernel(whole_ref, *refs, boxes):
    outs, sems = refs[:-1], refs[-1]
    copies = []
    for (slices, rows, lanes), out_ref in zip(boxes, outs):
        for k, s in enumerate(slices):
            source = whole_ref.at[s, :, pl.ds(*rows), pl.ds(*lanes)]
            copies.append(pltpu.make_async_copy(source, out_ref.at[pl.ds(2 * k, 2)], sems.at[len(copies)]))
    for copy in copies:
        copy.start()
    for copy in copies:
        copy.wait()


def pack(whole, boxes):
    count = sum(len(slices) for slices, _, _ in boxes)
    return pl.pallas_call(
        functools.partial(pack_kernel, boxes=boxes),
        in_specs=[FAR],
        out_specs=[VMEM] * len(boxes),
        out_shape=[F32((2 * len(slices), rows[1], lanes[1])) for slices, rows, lanes in boxes],
        scratch_shapes=[pltpu.SemaphoreType.DMA((count,))],
        compiler_params=LIMIT,
    )(in_hbm(whole))


def in_hbm(array):
    return pltpu.with_memory_space_constraint(array, pltpu.MemorySpace.HBM)


def body(
    specimen_slices,
    illumination_probe,
    propagation_phase,
    amplitudes,
    positions,
    counts,
    measurement_index,
):
    tile_px = specimen_slices.shape[2]
    width = illumination_probe.shape[1]
    spots = positions.shape[2]
    ext = tile_px + width
    across = tile_px - width
    cos, sin = jnp.cos(propagation_phase), jnp.sin(propagation_phase)
    numbers = jnp.concatenate([positions.reshape(-1), counts.reshape(-1), measurement_index.reshape(-1)])
    numbers = jnp.pad(numbers, (0, LANES - numbers.shape[0])).reshape(1, LANES)
    scalars = (numbers,)
    static = dict(spots=spots, width=width)
    ext_space = pltpu.VMEM((2, ext // LANES, ext, LANES), jnp.float32)
    wave_space = pltpu.VMEM((spots, 2, width, width), jnp.float32)
    wave = F32((spots, 2, width, width))
    square = F32((2, width, width))
    squares = F32((4, width, width))
    whole = F32((2, tile_px, tile_px))
    strip = F32((2, width, tile_px))
    gradient = [whole, strip, square, square, square]

    left, low, full = (0, width), (width, across), (0, tile_px)
    up_one, up_two, left_low, top = pack(
        specimen_slices, [((0,), left, left), ((1,), left, left), ((0, 1), low, left), ((0, 1), left, full)]
    )
    upper_one = from_behind(up_one, "col", -1)
    upper_two = from_behind(up_two, "col", -1)
    lower = from_behind(left_low, "col", -1)
    below = from_behind(top, "row", -1)
    far = (specimen_slices, illumination_probe, amplitudes[0, 0], jnp.asarray(dft_operands(width)))
    tile, probe, measured, table = pl.pallas_call(
        stage_kernel,
        in_specs=[FAR] * len(far),
        out_specs=[VMEM] * len(far),
        out_shape=[jax.ShapeDtypeStruct(x.shape, x.dtype) for x in far],
        scratch_shapes=[pltpu.SemaphoreType.DMA((len(far),))],
        compiler_params=LIMIT,
        name="stage",
    )(*[in_hbm(x) for x in far])
    corner_one = from_behind(upper_one, "row", -1)
    corner_two = from_behind(upper_two, "row", -1)
    for i in range(ITERS):
        if i == 0:
            own_two, down_two, up_two, low_two, diag_two, back = call(
                wave_kernel, scalars,
                (tile, below, upper_one, upper_two, lower, corner_one, corner_two, cos, sin, probe, measured, table),
                [*gradient, wave], [ext_space, ext_space, ext_space, wave_space, wave_space], **static,
            )
        else:
            (moved,) = call(
                forward_kernel, scalars, (*halo[0], cos, sin, probe, table),
                [wave], [ext_space, wave_space], **static,
            )
            own_two, down_two, up_two, low_two, diag_two, back = call(
                residual_kernel, scalars, (*halo[1], moved, measured, table),
                [*gradient, wave], [ext_space, ext_space, wave_space], **static,
            )
        low_two = from_behind(low_two, "col", 1)
        corner_two = from_behind(diag_two, "row", 1)
        own_one, down, up_one, low_one, diag_one = call(
            backward_kernel, scalars, (back, down_two, cos, sin, probe, table),
            [whole, F32((4, width, tile_px)), square, square, square], [ext_space], **static,
        )
        low_one = from_behind(low_one, "col", 1)
        corner_one = from_behind(diag_one, "row", 1)
        above = from_behind(down, "row", 1)
        up_two = up_two + corner_two
        up_one = up_one + corner_one
        up_two = from_behind(up_two, "col", 1)
        up_one = from_behind(up_one, "col", 1)
        if i + 1 < ITERS:
            left_one, left_two = call(
                update_low_kernel, (), (tile, own_one, own_two, low_one, low_two),
                [F32((2, across, width))] * 2, [], width=width,
            )
            lower_one = from_behind(left_one, "col", -1)
            rest_one, rest_two, right = call(
                update_rest_kernel, (), (tile, own_one, own_two, above, low_one, low_two),
                [whole, whole, F32((4, width, across))], [], width=width,
            )
            below_right = from_behind(right, "row", -1)
            quad_one, quad_two, left = call(
                update_quad_kernel, (),
                (tile, own_one, own_two, above, up_one, up_two),
                [square, square, squares], [], width=width,
            )
            upper_one = from_behind(quad_one, "col", -1)
            upper_two = from_behind(quad_two, "col", -1)
            below_left = from_behind(left, "row", -1)
            lower_two = from_behind(left_two, "col", -1)
            corner_one = from_behind(upper_one, "row", -1)
            corner_two = from_behind(upper_two, "row", -1)
            halo = (
                (rest_one, quad_one, below_left, below_right, upper_one, lower_one, corner_one),
                (rest_two, quad_two, below_left, below_right, upper_two, lower_two, corner_two),
            )
        else:
            end = dict(
                out_specs=FAR,
                out_shape=F32(specimen_slices.shape),
                compiler_params=LIMIT,
            )
            part = pl.pallas_call(
                functools.partial(finish_low_kernel, width=width),
                in_specs=[VMEM] * 6,
                scratch_shapes=[
                    pltpu.VMEM((2, 2, across, tile_px), jnp.float32), pltpu.SemaphoreType.DMA(()),
                ],
                name="finish_low",
                **end,
            )(rest_one, rest_two, own_one, own_two, low_one, low_two)
            updated = pl.pallas_call(
                functools.partial(finish_top_kernel, width=width),
                in_specs=[VMEM] * 9 + [FAR],
                input_output_aliases={9: 0},
                scratch_shapes=[
                    pltpu.VMEM((2, 2, width, tile_px), jnp.float32), pltpu.SemaphoreType.DMA(()),
                ],
                name="finish_top",
                **end,
            )(
                rest_one, rest_two, quad_one, quad_two, own_one, own_two, above, up_one, up_two, in_hbm(part),
            )
    return updated


def solution(mesh):
    placed = (
        P(None, None, "row", "col"),
        P(),
        P(),
        P("row", "col", None, None, None),
        P("row", "col", None, None),
        P("row", "col"),
        P("row", "col", None),
    )

    return jax.shard_map(body, mesh=mesh, in_specs=placed, out_specs=P(None, None, "row", "col"), check_vma=False)
```

```python
import functools
import math

import jax
import jax.numpy as jnp
import ml_dtypes
import numpy as np
from jax import lax
from jax.experimental import pallas as pl
from jax.experimental.pallas import tpu as pltpu
from jax.sharding import PartitionSpec as P


ITERS = 2
LANES = 128

step_size = 0.02
floor_amp = 0.5


def from_behind(block, axis, distance):
    devices = range(lax.axis_size(axis))
    route = [((i - distance) % len(devices), i) for i in devices]
    return lax.ppermute(block, axis, route)


def two_parts(value):
    high = value.astype(ml_dtypes.bfloat16)
    low = (value - high.astype(np.float64)).astype(ml_dtypes.bfloat16)
    return high, low


def dft_operands(width):
    index = np.arange(width)
    angle = (index[:, None] * index[None, :] % width) * (2.0 * math.pi / width)
    real = np.cos(angle) / math.sqrt(width)
    imag = -np.sin(angle) / math.sqrt(width)
    right = np.block([[real, imag], [-imag, real]])
    right_high, right_low = two_parts(right)
    left_high, left_low = two_parts(right.T)
    return np.stack([right_high, right_low, left_high, left_low])


def split(value):
    high = value.astype(jnp.bfloat16)
    low = (value - high.astype(jnp.float32)).astype(jnp.bfloat16)
    return high, low


def rows_of(j, width):
    return slice(j * width, (j + 1) * width)


def product(left, right):
    return jnp.dot(left, right, preferred_element_type=jnp.float32)


def right_side(pairs, table_ref):
    high, low = split(jnp.concatenate([jnp.concatenate(pair, 1) for pair in pairs], 0))
    return product(high, table_ref[0]) + product(low, table_ref[0]) + product(high, table_ref[1])


def left_side(half, table_ref, width):
    count = half.shape[0] // width
    parts = [half[rows_of(k, width)] for k in range(count)]
    tall = [jnp.concatenate([part[:, :width], part[:, width:]], 0) for part in parts]
    high, low = split(jnp.concatenate(tall, 1))
    both = product(table_ref[2], jnp.concatenate([high, low], 1))
    full = both[:, :high.shape[1]] + both[:, high.shape[1]:] + product(table_ref[3], high)
    return [(full[:width, rows_of(k, width)], full[width:, rows_of(k, width)]) for k in range(count)]


def interleave(chains, lag):
    waiting = [(n * lag, chain) for n, chain in enumerate(chains)]
    while waiting:
        after = []
        for delay, chain in waiting:
            if delay:
                after.append((delay - 1, chain))
            elif next(chain, None) is not None:
                after.append((0, chain))
        waiting = after


def fill_ext(ext_ref, pieces):
    for row, col, source in pieces:
        height, across = source.shape[1:]
        for c in range(2):
            for b in range(across // LANES):
                ext_ref[c, col // LANES + b, row:row + height, :] = source[c, :, b * LANES:(b + 1) * LANES]


def pick(numbers_ref, k):
    values = numbers_ref[...].astype(jnp.float32)
    lane = lax.broadcasted_iota(jnp.int32, values.shape, 1)
    return jnp.sum(jnp.where(lane == k, values, 0.0)).astype(jnp.int32)


def places(numbers_ref, spots):
    spot_list = []
    for j in range(spots):
        row, col = pick(numbers_ref, 2 * j), pick(numbers_ref, 2 * j + 1)
        spot_list.append((row, col // LANES, col % LANES))
    return spot_list


def window(ext_ref, c, spot, width, lane):
    row, block, shift = spot
    near = ext_ref[c, block, pl.ds(row, width), :]
    far = ext_ref[c, block + 1, pl.ds(row, width), :]
    return pltpu.roll(jnp.where(lane >= shift, near, far), LANES - shift, 1)


def scatter(grad_ref, c, spot, width, lane, used, update):
    row, block, shift = spot
    turned = pltpu.roll(jnp.where(used, update, 0.0), shift, 1)
    near = lane >= shift
    grad_ref[c, block, pl.ds(row, width), :] += jnp.where(near, turned, 0.0)
    grad_ref[c, block + 1, pl.ds(row, width), :] += jnp.where(near, 0.0, turned)


def emit(grad_ref, own_ref, down_ref, upper_ref, lower_ref, diag_ref, width):
    tile_px = own_ref.shape[1]
    blocks = tile_px // LANES
    for c in range(2):
        for b in range(blocks):
            lanes = slice(b * LANES, (b + 1) * LANES)
            own_ref[c, :, lanes] = grad_ref[c, b, :tile_px, :]
            down_ref[c, :, lanes] = grad_ref[c, b, tile_px:, :]
        upper_ref[c] = grad_ref[c, blocks, :width, :]
        lower_ref[c] = grad_ref[c, blocks, width:tile_px, :]
        diag_ref[c] = grad_ref[c, blocks, tile_px:, :]


def lanes_of(width):
    return lax.broadcasted_iota(jnp.int32, (width, LANES), 1)


LAG = 0


def groups_of(spots):
    return [range(j, j + 1) for j in range(spots)]


def forward_steps(group, enter_ref, leave_ref, cos_ref, sin_ref, table_ref, width):
    half = right_side([(enter_ref[j, 0], enter_ref[j, 1]) for j in group], table_ref)
    yield True
    pairs = left_side(half, table_ref, width)
    yield True
    half = right_side([
        (cos_ref[...] * real - sin_ref[...] * imag, -(cos_ref[...] * imag + sin_ref[...] * real))
        for real, imag in pairs
    ], table_ref)
    yield True
    pairs = left_side(half, table_ref, width)
    yield True
    for j, (real, negative) in zip(group, pairs):
        leave_ref[j, 0] = real
        leave_ref[j, 1] = -negative


def residual_steps(group, moved_ref, win_ref, measured_of, finish, table_ref, width):
    half = right_side([
        (
            moved_ref[j, 0] * win_ref[j, 0] - moved_ref[j, 1] * win_ref[j, 1],
            moved_ref[j, 0] * win_ref[j, 1] + moved_ref[j, 1] * win_ref[j, 0],
        )
        for j in group
    ], table_ref)
    yield True
    pairs = left_side(half, table_ref, width)
    yield True
    residuals = []
    for j, (real, imag) in zip(group, pairs):
        power = jnp.maximum(real * real + imag * imag, floor_amp * floor_amp)
        factor = 1.0 - measured_of(j) * lax.rsqrt(power)
        residuals.append((real * factor, -(imag * factor)))
    half = right_side(residuals, table_ref)
    yield True
    pairs = left_side(half, table_ref, width)
    yield True
    for j, (real, negative) in zip(group, pairs):
        finish(j, real, -negative)


def by_count(total, spots, run):
    groups = groups_of(spots)
    first = (len(groups) + 1) // 2
    if first == len(groups):
        run(groups)
        return

    @pl.when(total > first)
    def _():
        run(groups)

    @pl.when(total <= first)
    def _():
        run(groups[:first])


def joined(*parts):
    for part in parts:
        yield from part


def whole_pieces(refs, s, tile_px, width):
    tile_ref, below_ref, upper_ref, lower_ref, corner_ref = refs
    both = pl.ds(2 * s, 2)
    return [
        (0, 0, tile_ref.at[s]),
        (tile_px, 0, below_ref.at[both]),
        (0, tile_px, upper_ref),
        (width, tile_px, lower_ref.at[both]),
        (tile_px, tile_px, corner_ref),
    ]


def slice_pieces(refs, s, tile_px, width):
    rest_ref, quad_ref, below_left_ref, below_right_ref, upper_ref, lower_ref, corner_ref = refs
    both = pl.ds(2 * s, 2)
    across = tile_px - width
    return [
        (width, 0, rest_ref.at[:, pl.ds(width, across), :]),
        (0, width, rest_ref.at[:, pl.ds(0, width), pl.ds(width, across)]),
        (0, 0, quad_ref),
        (tile_px, 0, below_left_ref.at[both]),
        (tile_px, width, below_right_ref.at[both]),
        (0, tile_px, upper_ref),
        (width, tile_px, lower_ref),
        (tile_px, tile_px, corner_ref),
    ]


def take_windows(ext_ref, spot_list, probes, win_ref, width, lane):
    for j in probes:
        spot = spot_list[j]
        win_ref[j, 0] = window(ext_ref, 0, spot, width, lane)
        win_ref[j, 1] = window(ext_ref, 1, spot, width, lane)


def light(ext_ref, spot_list, probes, probe_ref, enter_ref, width, lane):
    for j in probes:
        spot = spot_list[j]
        real = window(ext_ref, 0, spot, width, lane)
        imag = window(ext_ref, 1, spot, width, lane)
        enter_ref[j, 0] = probe_ref[0] * real - probe_ref[1] * imag
        enter_ref[j, 1] = probe_ref[0] * imag + probe_ref[1] * real


def residual_end(total, spot_list, ext_ref, moved_ref, win_ref, back_ref, width, lane):
    def finish(j, real, imag):
        used = j < total
        scatter(ext_ref, 0, spot_list[j], width, lane, used, moved_ref[j, 0] * real + moved_ref[j, 1] * imag)
        scatter(ext_ref, 1, spot_list[j], width, lane, used, moved_ref[j, 0] * imag - moved_ref[j, 1] * real)
        back_ref[j, 0] = win_ref[j, 0] * real + win_ref[j, 1] * imag
        back_ref[j, 1] = win_ref[j, 0] * imag - win_ref[j, 1] * real

    return finish


def wave_kernel(
    numbers_ref, tile_ref, below_ref, upper_one, upper_two, lower_ref, corner_one, corner_two,
    cos_ref, sin_ref, probe_ref, amp_ref, table_ref,
    own_ref, down_ref, up_out_ref, low_out_ref, diag_ref, back_ref,
    ext_ref, other_ref, grad_ref, win_ref, moved_ref, *, spots, width,
):
    lane = lanes_of(width)
    tile_px = own_ref.shape[1]
    first = (tile_ref, below_ref, upper_one, lower_ref, corner_one)
    second = (tile_ref, below_ref, upper_two, lower_ref, corner_two)
    fill_ext(ext_ref, whole_pieces(first, 0, tile_px, width))
    fill_ext(other_ref, whole_pieces(second, 1, tile_px, width))
    grad_ref[...] = jnp.zeros(grad_ref.shape, jnp.float32)
    spot_list = places(numbers_ref, spots)
    total = pick(numbers_ref, 2 * spots)
    finish = residual_end(total, spot_list, grad_ref, moved_ref, win_ref, back_ref, width, lane)
    measured_of = lambda j: amp_ref[pick(numbers_ref, 2 * spots + 1 + j)]

    def run(groups):
        probes = [j for group in groups for j in group]
        light(ext_ref, spot_list, probes, probe_ref, back_ref, width, lane)
        take_windows(other_ref, spot_list, probes, win_ref, width, lane)
        interleave([
            joined(
                forward_steps(group, back_ref, moved_ref, cos_ref, sin_ref, table_ref, width),
                residual_steps(group, moved_ref, win_ref, measured_of, finish, table_ref, width),
            )
            for group in groups
        ], LAG)

    by_count(total, spots, run)
    emit(grad_ref, own_ref, down_ref, up_out_ref, low_out_ref, diag_ref, width)


def forward_kernel(
    numbers_ref, rest_ref, quad_ref, left_ref, right_ref, upper_ref, lower_ref, corner_ref,
    cos_ref, sin_ref, probe_ref, table_ref, moved_ref, ext_ref, enter_ref, *, spots, width,
):
    lane = lanes_of(width)
    halo = (rest_ref, quad_ref, left_ref, right_ref, upper_ref, lower_ref, corner_ref)
    fill_ext(ext_ref, slice_pieces(halo, 0, rest_ref.shape[1], width))
    spot_list = places(numbers_ref, spots)

    def run(groups):
        light(ext_ref, spot_list, [j for group in groups for j in group], probe_ref, enter_ref, width, lane)
        interleave([
            forward_steps(group, enter_ref, moved_ref, cos_ref, sin_ref, table_ref, width) for group in groups
        ], LAG)

    by_count(pick(numbers_ref, 2 * spots), spots, run)


def residual_kernel(
    numbers_ref, rest_ref, quad_ref, left_ref, right_ref, upper_ref, lower_ref, corner_ref,
    moved_ref, amp_ref, table_ref,
    own_ref, down_ref, up_out_ref, low_out_ref, diag_ref, back_ref,
    ext_ref, grad_ref, win_ref, *, spots, width,
):
    lane = lanes_of(width)
    halo = (rest_ref, quad_ref, left_ref, right_ref, upper_ref, lower_ref, corner_ref)
    fill_ext(ext_ref, slice_pieces(halo, 1, rest_ref.shape[1], width))
    grad_ref[...] = jnp.zeros(grad_ref.shape, jnp.float32)
    spot_list = places(numbers_ref, spots)
    total = pick(numbers_ref, 2 * spots)
    finish = residual_end(total, spot_list, grad_ref, moved_ref, win_ref, back_ref, width, lane)
    measured_of = lambda j: amp_ref[pick(numbers_ref, 2 * spots + 1 + j)]

    def run(groups):
        take_windows(ext_ref, spot_list, [j for group in groups for j in group], win_ref, width, lane)
        interleave([
            residual_steps(group, moved_ref, win_ref, measured_of, finish, table_ref, width) for group in groups
        ], LAG)

    by_count(total, spots, run)
    emit(grad_ref, own_ref, down_ref, up_out_ref, low_out_ref, diag_ref, width)


def backward_kernel(
    numbers_ref, back_ref, other_down_ref, cos_ref, sin_ref, probe_ref, table_ref,
    own_ref, down_ref, up_out_ref, low_out_ref, diag_ref, ext_ref, *, spots, width,
):
    lane = lanes_of(width)
    down_ref[2:] = other_down_ref[...]
    spot_list = places(numbers_ref, spots)
    total = pick(numbers_ref, 2 * spots)
    ext_ref[...] = jnp.zeros(ext_ref.shape, jnp.float32)

    def chain(group):
        half = right_side([(back_ref[j, 0], back_ref[j, 1]) for j in group], table_ref)
        yield True
        pairs = left_side(half, table_ref, width)
        yield True
        half = right_side([
            (cos_ref[...] * real + sin_ref[...] * imag, -(cos_ref[...] * imag - sin_ref[...] * real))
            for real, imag in pairs
        ], table_ref)
        yield True
        pairs = left_side(half, table_ref, width)
        yield True
        for j, (real, negative) in zip(group, pairs):
            imag = -negative
            spot = spot_list[j]
            used = j < total
            scatter(ext_ref, 0, spot, width, lane, used, probe_ref[0] * real + probe_ref[1] * imag)
            scatter(ext_ref, 1, spot, width, lane, used, probe_ref[0] * imag - probe_ref[1] * real)

    by_count(total, spots, lambda groups: interleave([chain(group) for group in groups], LAG))
    emit(ext_ref, own_ref, down_ref, up_out_ref, low_out_ref, diag_ref, width)


def step(value, gradient):
    return value - step_size * gradient


def rest_values(tile_ref, own_ref, above_ref, lower_ref, c, width):
    top, right = slice(0, width), slice(width, own_ref.shape[1])
    yield top, right, step(tile_ref[c, top, right], own_ref[c, top, right] + above_ref[c, :, right])
    yield from low_values(tile_ref, own_ref, lower_ref, c, width)


def low_values(tile_ref, own_ref, lower_ref, c, width):
    tile_px = own_ref.shape[1]
    low, left, right = slice(width, tile_px), slice(0, width), slice(width, tile_px)
    yield low, left, step(tile_ref[c, low, left], own_ref[c, low, left] + lower_ref[c])
    yield low, right, step(tile_ref[c, low, right], own_ref[c, low, right])


def quad_value(quad_ref, own_ref, above_ref, upper_ref, c, width):
    top, left = slice(0, width), slice(0, width)
    return step(quad_ref[c, top, left], own_ref[c, top, left] + above_ref[c, :, left] + upper_ref[c])


def update_low_kernel(tile_ref, own_one, own_two, low_one, low_two, left_one, left_two, *, width):
    tile_px = own_one.shape[1]
    low, left = slice(width, tile_px), slice(0, width)
    for s, (own_ref, low_ref, left_ref) in enumerate(((own_one, low_one, left_one), (own_two, low_two, left_two))):
        for c in range(2):
            left_ref[c] = step(tile_ref[s, c, low, left], own_ref[c, low, left] + low_ref[c])


def update_rest_kernel(
    tile_ref, own_one, own_two, above_ref, low_one, low_two, rest_one, rest_two, right_ref, *, width,
):
    parts = ((own_one, low_one, rest_one), (own_two, low_two, rest_two))
    for s, (own_ref, low_ref, rest_ref) in enumerate(parts):
        above = above_ref.at[pl.ds(2 * s, 2)]
        for c in range(2):
            pieces = list(rest_values(tile_ref.at[s], own_ref, above, low_ref, c, width))
            for rows, lanes, value in pieces:
                rest_ref[c, rows, lanes] = value
            right_ref[2 * s + c] = pieces[0][2]


def update_quad_kernel(
    tile_ref, own_one, own_two, above_ref, up_one, up_two, quad_one, quad_two, left_ref, *, width,
):
    parts = ((own_one, up_one, quad_one), (own_two, up_two, quad_two))
    for s, (own_ref, up_ref, quad_ref) in enumerate(parts):
        above = above_ref.at[pl.ds(2 * s, 2)]
        for c in range(2):
            value = quad_value(tile_ref.at[s], own_ref, above, up_ref, c, width)
            quad_ref[c] = value
            left_ref[2 * s + c] = value


def finish_low_kernel(
    rest_one, rest_two, own_one, own_two, low_one, low_two, out_ref, rows_ref, sem, *, width,
):
    tile_px = own_one.shape[1]
    for s, (rest_ref, own_ref, low_ref) in enumerate(((rest_one, own_one, low_one), (rest_two, own_two, low_two))):
        for c in range(2):
            for _, lanes, value in low_values(rest_ref, own_ref, low_ref, c, width):
                rows_ref[s, c, :, lanes] = value
    copy = pltpu.make_async_copy(rows_ref, out_ref.at[:, :, pl.ds(width, tile_px - width), :], sem)
    copy.start()
    copy.wait()


def finish_top_kernel(
    rest_one, rest_two, quad_one, quad_two, own_one, own_two, above_ref, up_one, up_two, part_ref,
    out_ref, rows_ref, sem, *, width,
):
    del part_ref
    tile_px = own_one.shape[1]
    parts = ((rest_one, quad_one, own_one, up_one), (rest_two, quad_two, own_two, up_two))
    for s, (rest_ref, quad_ref, own_ref, up_ref) in enumerate(parts):
        above = above_ref.at[pl.ds(2 * s, 2)]
        for c in range(2):
            top, right = slice(0, width), slice(width, tile_px)
            rows_ref[s, c, :, :width] = quad_value(quad_ref, own_ref, above, up_ref, c, width)
            rows_ref[s, c, :, width:] = step(rest_ref[c, top, right], own_ref[c, top, right] + above[c, :, right])
    copy = pltpu.make_async_copy(rows_ref, out_ref.at[:, :, pl.ds(0, width), :], sem)
    copy.start()
    copy.wait()


def stage_kernel(*refs):
    sems = refs[-1]
    count = (len(refs) - 1) // 2
    copies = [pltpu.make_async_copy(refs[k], refs[count + k], sems.at[k]) for k in range(count)]
    for copy in copies:
        copy.start()
    for copy in copies:
        copy.wait()


F32 = functools.partial(jax.ShapeDtypeStruct, dtype=jnp.float32)
VMEM = pl.BlockSpec(memory_space=pltpu.VMEM)
LIMIT = pltpu.CompilerParams(vmem_limit_bytes=16 * 1024 * 1024)


FAR = pl.BlockSpec(memory_space=pltpu.MemorySpace.HBM)


def call(kernel, scalars, arrays, outs, scratch, **static):
    return pl.pallas_call(
        functools.partial(kernel, **static),
        in_specs=[VMEM] * (len(scalars) + len(arrays)),
        out_specs=[VMEM] * len(outs),
        out_shape=outs,
        scratch_shapes=scratch,
        compiler_params=LIMIT,
    )(*scalars, *arrays)


def pack_kernel(whole_ref, *refs, boxes):
    outs, sems = refs[:-1], refs[-1]
    copies = []
    for (slices, rows, lanes), out_ref in zip(boxes, outs):
        for k, s in enumerate(slices):
            source = whole_ref.at[s, :, pl.ds(*rows), pl.ds(*lanes)]
            copies.append(pltpu.make_async_copy(source, out_ref.at[pl.ds(2 * k, 2)], sems.at[len(copies)]))
    for copy in copies:
        copy.start()
    for copy in copies:
        copy.wait()


def pack(whole, boxes):
    count = sum(len(slices) for slices, _, _ in boxes)
    return pl.pallas_call(
        functools.partial(pack_kernel, boxes=boxes),
        in_specs=[FAR],
        out_specs=[VMEM] * len(boxes),
        out_shape=[F32((2 * len(slices), rows[1], lanes[1])) for slices, rows, lanes in boxes],
        scratch_shapes=[pltpu.SemaphoreType.DMA((count,))],
        compiler_params=LIMIT,
    )(in_hbm(whole))


def in_hbm(array):
    return pltpu.with_memory_space_constraint(array, pltpu.MemorySpace.HBM)


def body(
    specimen_slices,
    illumination_probe,
    propagation_phase,
    amplitudes,
    positions,
    counts,
    measurement_index,
):
    tile_px = specimen_slices.shape[2]
    width = illumination_probe.shape[1]
    spots = positions.shape[2]
    ext = tile_px + width
    across = tile_px - width
    cos, sin = jnp.cos(propagation_phase), jnp.sin(propagation_phase)
    numbers = jnp.concatenate([positions.reshape(-1), counts.reshape(-1), measurement_index.reshape(-1)])
    numbers = jnp.pad(numbers, (0, LANES - numbers.shape[0])).reshape(1, LANES)
    scalars = (numbers,)
    static = dict(spots=spots, width=width)
    ext_space = pltpu.VMEM((2, ext // LANES, ext, LANES), jnp.float32)
    wave_space = pltpu.VMEM((spots, 2, width, width), jnp.float32)
    wave = F32((spots, 2, width, width))
    square = F32((2, width, width))
    squares = F32((4, width, width))
    whole = F32((2, tile_px, tile_px))
    strip = F32((2, width, tile_px))
    gradient = [whole, strip, square, square, square]

    left, low, full = (0, width), (width, across), (0, tile_px)
    up_one, up_two, left_low, top = pack(
        specimen_slices, [((0,), left, left), ((1,), left, left), ((0, 1), low, left), ((0, 1), left, full)]
    )
    upper_one = from_behind(up_one, "col", -1)
    upper_two = from_behind(up_two, "col", -1)
    lower = from_behind(left_low, "col", -1)
    below = from_behind(top, "row", -1)
    far = (specimen_slices, illumination_probe, amplitudes[0, 0], jnp.asarray(dft_operands(width)))
    tile, probe, measured, table = pl.pallas_call(
        stage_kernel,
        in_specs=[FAR] * len(far),
        out_specs=[VMEM] * len(far),
        out_shape=[jax.ShapeDtypeStruct(x.shape, x.dtype) for x in far],
        scratch_shapes=[pltpu.SemaphoreType.DMA((len(far),))],
        compiler_params=LIMIT,
        name="stage",
    )(*[in_hbm(x) for x in far])
    corner_one = from_behind(upper_one, "row", -1)
    corner_two = from_behind(upper_two, "row", -1)
    for i in range(ITERS):
        if i == 0:
            own_two, down_two, up_two, low_two, diag_two, back = call(
                wave_kernel, scalars,
                (tile, below, upper_one, upper_two, lower, corner_one, corner_two, cos, sin, probe, measured, table),
                [*gradient, wave], [ext_space, ext_space, ext_space, wave_space, wave_space], **static,
            )
        else:
            (moved,) = call(
                forward_kernel, scalars, (*halo[0], cos, sin, probe, table),
                [wave], [ext_space, wave_space], **static,
            )
            own_two, down_two, up_two, low_two, diag_two, back = call(
                residual_kernel, scalars, (*halo[1], moved, measured, table),
                [*gradient, wave], [ext_space, ext_space, wave_space], **static,
            )
        low_two = from_behind(low_two, "col", 1)
        corner_two = from_behind(diag_two, "row", 1)
        own_one, down, up_one, low_one, diag_one = call(
            backward_kernel, scalars, (back, down_two, cos, sin, probe, table),
            [whole, F32((4, width, tile_px)), square, square, square], [ext_space], **static,
        )
        low_one = from_behind(low_one, "col", 1)
        corner_one = from_behind(diag_one, "row", 1)
        above = from_behind(down, "row", 1)
        up_two = up_two + corner_two
        up_one = up_one + corner_one
        up_two = from_behind(up_two, "col", 1)
        up_one = from_behind(up_one, "col", 1)
        if i + 1 < ITERS:
            left_one, left_two = call(
                update_low_kernel, (), (tile, own_one, own_two, low_one, low_two),
                [F32((2, across, width))] * 2, [], width=width,
            )
            lower_one = from_behind(left_one, "col", -1)
            rest_one, rest_two, right = call(
                update_rest_kernel, (), (tile, own_one, own_two, above, low_one, low_two),
                [whole, whole, F32((4, width, across))], [], width=width,
            )
            below_right = from_behind(right, "row", -1)
            quad_one, quad_two, left = call(
                update_quad_kernel, (),
                (tile, own_one, own_two, above, up_one, up_two),
                [square, square, squares], [], width=width,
            )
            upper_one = from_behind(quad_one, "col", -1)
            upper_two = from_behind(quad_two, "col", -1)
            below_left = from_behind(left, "row", -1)
            lower_two = from_behind(left_two, "col", -1)
            corner_one = from_behind(upper_one, "row", -1)
            corner_two = from_behind(upper_two, "row", -1)
            halo = (
                (rest_one, quad_one, below_left, below_right, upper_one, lower_one, corner_one),
                (rest_two, quad_two, below_left, below_right, upper_two, lower_two, corner_two),
            )
        else:
            end = dict(
                out_specs=FAR,
                out_shape=F32(specimen_slices.shape),
                compiler_params=LIMIT,
            )
            part = pl.pallas_call(
                functools.partial(finish_low_kernel, width=width),
                in_specs=[VMEM] * 6,
                scratch_shapes=[
                    pltpu.VMEM((2, 2, across, tile_px), jnp.float32), pltpu.SemaphoreType.DMA(()),
                ],
                name="finish_low",
                **end,
            )(rest_one, rest_two, own_one, own_two, low_one, low_two)
            updated = pl.pallas_call(
                functools.partial(finish_top_kernel, width=width),
                in_specs=[VMEM] * 9 + [FAR],
                input_output_aliases={9: 0},
                scratch_shapes=[
                    pltpu.VMEM((2, 2, width, tile_px), jnp.float32), pltpu.SemaphoreType.DMA(()),
                ],
                name="finish_top",
                **end,
            )(
                rest_one, rest_two, quad_one, quad_two, own_one, own_two, above, up_one, up_two, in_hbm(part),
            )
    return updated


def solution(mesh):
    placed = (
        P(None, None, "row", "col"),
        P(),
        P(),
        P("row", "col", None, None, None),
        P("row", "col", None, None),
        P("row", "col"),
        P("row", "col", None),
    )

    return jax.shard_map(body, mesh=mesh, in_specs=placed, out_specs=P(None, None, "row", "col"), check_vma=False)
```

```python
import functools
import math

import jax
import jax.numpy as jnp
import ml_dtypes
import numpy as np
from jax import lax
from jax.experimental import pallas as pl
from jax.experimental.pallas import tpu as pltpu
from jax.sharding import PartitionSpec as P


ITERS = 2
LANES = 128

step_size = 0.02
floor_amp = 0.5


def from_behind(block, axis, distance):
    devices = range(lax.axis_size(axis))
    route = [((i - distance) % len(devices), i) for i in devices]
    return lax.ppermute(block, axis, route)


def two_parts(value):
    high = value.astype(ml_dtypes.bfloat16)
    low = (value - high.astype(np.float64)).astype(ml_dtypes.bfloat16)
    return high, low


def dft_operands(width):
    index = np.arange(width)
    angle = (index[:, None] * index[None, :] % width) * (2.0 * math.pi / width)
    real = np.cos(angle) / math.sqrt(width)
    imag = -np.sin(angle) / math.sqrt(width)
    right = np.block([[real, imag], [-imag, real]])
    right_high, right_low = two_parts(right)
    left_high, left_low = two_parts(right.T)
    return np.stack([right_high, right_low, left_high, left_low])


def split(value):
    high = value.astype(jnp.bfloat16)
    low = (value - high.astype(jnp.float32)).astype(jnp.bfloat16)
    return high, low


def rows_of(j, width):
    return slice(j * width, (j + 1) * width)


def product(left, right):
    return jnp.dot(left, right, preferred_element_type=jnp.float32)


def right_side(pairs, table_ref):
    high, low = split(jnp.concatenate([jnp.concatenate(pair, 1) for pair in pairs], 0))
    return product(high, table_ref[0]) + product(low, table_ref[0]) + product(high, table_ref[1])


def left_side(half, table_ref, width):
    count = half.shape[0] // width
    parts = [half[rows_of(k, width)] for k in range(count)]
    tall = [jnp.concatenate([part[:, :width], part[:, width:]], 0) for part in parts]
    high, low = split(jnp.concatenate(tall, 1))
    both = product(table_ref[2], jnp.concatenate([high, low], 1))
    full = both[:, :high.shape[1]] + both[:, high.shape[1]:] + product(table_ref[3], high)
    return [(full[:width, rows_of(k, width)], full[width:, rows_of(k, width)]) for k in range(count)]


def interleave(chains, lag):
    waiting = [(n * lag, chain) for n, chain in enumerate(chains)]
    while waiting:
        after = []
        for delay, chain in waiting:
            if delay:
                after.append((delay - 1, chain))
            elif next(chain, None) is not None:
                after.append((0, chain))
        waiting = after


def fill_ext(ext_ref, pieces):
    for row, col, source in pieces:
        height, across = source.shape[1:]
        for c in range(2):
            for b in range(across // LANES):
                ext_ref[c, col // LANES + b, row:row + height, :] = source[c, :, b * LANES:(b + 1) * LANES]


def pick(numbers_ref, k):
    values = numbers_ref[...].astype(jnp.float32)
    lane = lax.broadcasted_iota(jnp.int32, values.shape, 1)
    return jnp.sum(jnp.where(lane == k, values, 0.0)).astype(jnp.int32)


def places(numbers_ref, spots):
    spot_list = []
    for j in range(spots):
        row, col = pick(numbers_ref, 2 * j), pick(numbers_ref, 2 * j + 1)
        spot_list.append((row, col // LANES, col % LANES))
    return spot_list


def window(ext_ref, c, spot, width, lane):
    row, block, shift = spot
    near = ext_ref[c, block, pl.ds(row, width), :]
    far = ext_ref[c, block + 1, pl.ds(row, width), :]
    return pltpu.roll(jnp.where(lane >= shift, near, far), LANES - shift, 1)


def scatter(grad_ref, c, spot, width, lane, used, update):
    row, block, shift = spot
    turned = pltpu.roll(jnp.where(used, update, 0.0), shift, 1)
    near = lane >= shift
    grad_ref[c, block, pl.ds(row, width), :] += jnp.where(near, turned, 0.0)
    grad_ref[c, block + 1, pl.ds(row, width), :] += jnp.where(near, 0.0, turned)


def emit(grad_ref, own_ref, down_ref, upper_ref, lower_ref, diag_ref, width):
    tile_px = own_ref.shape[1]
    blocks = tile_px // LANES
    for c in range(2):
        for b in range(blocks):
            lanes = slice(b * LANES, (b + 1) * LANES)
            own_ref[c, :, lanes] = grad_ref[c, b, :tile_px, :]
            down_ref[c, :, lanes] = grad_ref[c, b, tile_px:, :]
        upper_ref[c] = grad_ref[c, blocks, :width, :]
        lower_ref[c] = grad_ref[c, blocks, width:tile_px, :]
        diag_ref[c] = grad_ref[c, blocks, tile_px:, :]


def lanes_of(width):
    return lax.broadcasted_iota(jnp.int32, (width, LANES), 1)


LAG = 0


def groups_of(spots):
    return [range(j, j + 1) for j in range(spots)]


def forward_steps(group, enter_ref, leave_ref, cos_ref, sin_ref, table_ref, width):
    half = right_side([(enter_ref[j, 0], enter_ref[j, 1]) for j in group], table_ref)
    yield True
    pairs = left_side(half, table_ref, width)
    yield True
    half = right_side([
        (cos_ref[...] * real - sin_ref[...] * imag, -(cos_ref[...] * imag + sin_ref[...] * real))
        for real, imag in pairs
    ], table_ref)
    yield True
    pairs = left_side(half, table_ref, width)
    yield True
    for j, (real, negative) in zip(group, pairs):
        leave_ref[j, 0] = real
        leave_ref[j, 1] = -negative


def residual_steps(group, moved_ref, win_ref, measured_of, finish, table_ref, width):
    half = right_side([
        (
            moved_ref[j, 0] * win_ref[j, 0] - moved_ref[j, 1] * win_ref[j, 1],
            moved_ref[j, 0] * win_ref[j, 1] + moved_ref[j, 1] * win_ref[j, 0],
        )
        for j in group
    ], table_ref)
    yield True
    pairs = left_side(half, table_ref, width)
    yield True
    residuals = []
    for j, (real, imag) in zip(group, pairs):
        power = jnp.maximum(real * real + imag * imag, floor_amp * floor_amp)
        factor = 1.0 - measured_of(j) * lax.rsqrt(power)
        residuals.append((real * factor, -(imag * factor)))
    half = right_side(residuals, table_ref)
    yield True
    pairs = left_side(half, table_ref, width)
    yield True
    for j, (real, negative) in zip(group, pairs):
        finish(j, real, -negative)


def by_count(total, spots, run):
    groups = groups_of(spots)
    first = (len(groups) + 1) // 2
    if first == len(groups):
        run(groups)
        return

    @pl.when(total > first)
    def _():
        run(groups)

    @pl.when(total <= first)
    def _():
        run(groups[:first])


def joined(*parts):
    for part in parts:
        yield from part


def whole_pieces(refs, s, tile_px, width):
    tile_ref, below_ref, upper_ref, lower_ref, corner_ref = refs
    both = pl.ds(2 * s, 2)
    return [
        (0, 0, tile_ref.at[s]),
        (tile_px, 0, below_ref.at[both]),
        (0, tile_px, upper_ref),
        (width, tile_px, lower_ref.at[both]),
        (tile_px, tile_px, corner_ref),
    ]


def slice_pieces(refs, s, tile_px, width):
    rest_ref, quad_ref, below_left_ref, below_right_ref, upper_ref, lower_ref, corner_ref = refs
    both = pl.ds(2 * s, 2)
    across = tile_px - width
    return [
        (width, 0, rest_ref.at[:, pl.ds(width, across), :]),
        (0, width, rest_ref.at[:, pl.ds(0, width), pl.ds(width, across)]),
        (0, 0, quad_ref),
        (tile_px, 0, below_left_ref.at[both]),
        (tile_px, width, below_right_ref.at[both]),
        (0, tile_px, upper_ref),
        (width, tile_px, lower_ref),
        (tile_px, tile_px, corner_ref),
    ]


def take_windows(ext_ref, spot_list, probes, win_ref, width, lane):
    for j in probes:
        spot = spot_list[j]
        win_ref[j, 0] = window(ext_ref, 0, spot, width, lane)
        win_ref[j, 1] = window(ext_ref, 1, spot, width, lane)


def light(ext_ref, spot_list, probes, probe_ref, enter_ref, width, lane):
    for j in probes:
        spot = spot_list[j]
        real = window(ext_ref, 0, spot, width, lane)
        imag = window(ext_ref, 1, spot, width, lane)
        enter_ref[j, 0] = probe_ref[0] * real - probe_ref[1] * imag
        enter_ref[j, 1] = probe_ref[0] * imag + probe_ref[1] * real


def residual_end(total, spot_list, ext_ref, moved_ref, win_ref, back_ref, width, lane):
    def finish(j, real, imag):
        used = j < total
        scatter(ext_ref, 0, spot_list[j], width, lane, used, moved_ref[j, 0] * real + moved_ref[j, 1] * imag)
        scatter(ext_ref, 1, spot_list[j], width, lane, used, moved_ref[j, 0] * imag - moved_ref[j, 1] * real)
        back_ref[j, 0] = win_ref[j, 0] * real + win_ref[j, 1] * imag
        back_ref[j, 1] = win_ref[j, 0] * imag - win_ref[j, 1] * real

    return finish


def wave_kernel(
    numbers_ref, tile_ref, below_ref, upper_one, upper_two, lower_ref, corner_one, corner_two,
    cos_ref, sin_ref, probe_ref, amp_ref, table_ref,
    own_ref, down_ref, up_out_ref, low_out_ref, diag_ref, back_ref,
    ext_ref, other_ref, grad_ref, win_ref, moved_ref, *, spots, width,
):
    lane = lanes_of(width)
    tile_px = own_ref.shape[1]
    first = (tile_ref, below_ref, upper_one, lower_ref, corner_one)
    second = (tile_ref, below_ref, upper_two, lower_ref, corner_two)
    fill_ext(ext_ref, whole_pieces(first, 0, tile_px, width))
    fill_ext(other_ref, whole_pieces(second, 1, tile_px, width))
    grad_ref[...] = jnp.zeros(grad_ref.shape, jnp.float32)
    spot_list = places(numbers_ref, spots)
    total = pick(numbers_ref, 2 * spots)
    finish = residual_end(total, spot_list, grad_ref, moved_ref, win_ref, back_ref, width, lane)
    measured_of = lambda j: amp_ref[pick(numbers_ref, 2 * spots + 1 + j)]

    def run(groups):
        probes = [j for group in groups for j in group]
        light(ext_ref, spot_list, probes, probe_ref, back_ref, width, lane)
        take_windows(other_ref, spot_list, probes, win_ref, width, lane)
        interleave([
            joined(
                forward_steps(group, back_ref, moved_ref, cos_ref, sin_ref, table_ref, width),
                residual_steps(group, moved_ref, win_ref, measured_of, finish, table_ref, width),
            )
            for group in groups
        ], LAG)

    by_count(total, spots, run)
    emit(grad_ref, own_ref, down_ref, up_out_ref, low_out_ref, diag_ref, width)


def forward_kernel(
    numbers_ref, rest_ref, quad_ref, left_ref, right_ref, upper_ref, lower_ref, corner_ref,
    cos_ref, sin_ref, probe_ref, table_ref, moved_ref, ext_ref, enter_ref, *, spots, width,
):
    lane = lanes_of(width)
    halo = (rest_ref, quad_ref, left_ref, right_ref, upper_ref, lower_ref, corner_ref)
    fill_ext(ext_ref, slice_pieces(halo, 0, rest_ref.shape[1], width))
    spot_list = places(numbers_ref, spots)

    def run(groups):
        light(ext_ref, spot_list, [j for group in groups for j in group], probe_ref, enter_ref, width, lane)
        interleave([
            forward_steps(group, enter_ref, moved_ref, cos_ref, sin_ref, table_ref, width) for group in groups
        ], LAG)

    by_count(pick(numbers_ref, 2 * spots), spots, run)


def residual_kernel(
    numbers_ref, rest_ref, quad_ref, left_ref, right_ref, upper_ref, lower_ref, corner_ref,
    moved_ref, amp_ref, table_ref,
    own_ref, down_ref, up_out_ref, low_out_ref, diag_ref, back_ref,
    ext_ref, grad_ref, win_ref, *, spots, width,
):
    lane = lanes_of(width)
    halo = (rest_ref, quad_ref, left_ref, right_ref, upper_ref, lower_ref, corner_ref)
    fill_ext(ext_ref, slice_pieces(halo, 1, rest_ref.shape[1], width))
    grad_ref[...] = jnp.zeros(grad_ref.shape, jnp.float32)
    spot_list = places(numbers_ref, spots)
    total = pick(numbers_ref, 2 * spots)
    finish = residual_end(total, spot_list, grad_ref, moved_ref, win_ref, back_ref, width, lane)
    measured_of = lambda j: amp_ref[pick(numbers_ref, 2 * spots + 1 + j)]

    def run(groups):
        take_windows(ext_ref, spot_list, [j for group in groups for j in group], win_ref, width, lane)
        interleave([
            residual_steps(group, moved_ref, win_ref, measured_of, finish, table_ref, width) for group in groups
        ], LAG)

    by_count(total, spots, run)
    emit(grad_ref, own_ref, down_ref, up_out_ref, low_out_ref, diag_ref, width)


def backward_kernel(
    numbers_ref, back_ref, other_down_ref, cos_ref, sin_ref, probe_ref, table_ref,
    own_ref, down_ref, up_out_ref, low_out_ref, diag_ref, ext_ref, *, spots, width,
):
    lane = lanes_of(width)
    down_ref[2:] = other_down_ref[...]
    spot_list = places(numbers_ref, spots)
    total = pick(numbers_ref, 2 * spots)
    ext_ref[...] = jnp.zeros(ext_ref.shape, jnp.float32)

    def chain(group):
        half = right_side([(back_ref[j, 0], back_ref[j, 1]) for j in group], table_ref)
        yield True
        pairs = left_side(half, table_ref, width)
        yield True
        half = right_side([
            (cos_ref[...] * real + sin_ref[...] * imag, -(cos_ref[...] * imag - sin_ref[...] * real))
            for real, imag in pairs
        ], table_ref)
        yield True
        pairs = left_side(half, table_ref, width)
        yield True
        for j, (real, negative) in zip(group, pairs):
            imag = -negative
            spot = spot_list[j]
            used = j < total
            scatter(ext_ref, 0, spot, width, lane, used, probe_ref[0] * real + probe_ref[1] * imag)
            scatter(ext_ref, 1, spot, width, lane, used, probe_ref[0] * imag - probe_ref[1] * real)

    by_count(total, spots, lambda groups: interleave([chain(group) for group in groups], LAG))
    emit(ext_ref, own_ref, down_ref, up_out_ref, low_out_ref, diag_ref, width)


def step(value, gradient):
    return value - step_size * gradient


def rest_values(tile_ref, own_ref, above_ref, lower_ref, c, width):
    top, right = slice(0, width), slice(width, own_ref.shape[1])
    yield top, right, step(tile_ref[c, top, right], own_ref[c, top, right] + above_ref[c, :, right])
    yield from low_values(tile_ref, own_ref, lower_ref, c, width)


def low_values(tile_ref, own_ref, lower_ref, c, width):
    tile_px = own_ref.shape[1]
    low, left, right = slice(width, tile_px), slice(0, width), slice(width, tile_px)
    yield low, left, step(tile_ref[c, low, left], own_ref[c, low, left] + lower_ref[c])
    yield low, right, step(tile_ref[c, low, right], own_ref[c, low, right])


def quad_value(quad_ref, own_ref, above_ref, upper_ref, c, width):
    top, left = slice(0, width), slice(0, width)
    return step(quad_ref[c, top, left], own_ref[c, top, left] + above_ref[c, :, left] + upper_ref[c])


def update_low_kernel(tile_ref, own_one, own_two, low_one, low_two, left_one, left_two, *, width):
    tile_px = own_one.shape[1]
    low, left = slice(width, tile_px), slice(0, width)
    for s, (own_ref, low_ref, left_ref) in enumerate(((own_one, low_one, left_one), (own_two, low_two, left_two))):
        for c in range(2):
            left_ref[c] = step(tile_ref[s, c, low, left], own_ref[c, low, left] + low_ref[c])


def update_rest_kernel(
    tile_ref, own_one, own_two, above_ref, low_one, low_two, rest_one, rest_two, right_ref, *, width,
):
    parts = ((own_one, low_one, rest_one), (own_two, low_two, rest_two))
    for s, (own_ref, low_ref, rest_ref) in enumerate(parts):
        above = above_ref.at[pl.ds(2 * s, 2)]
        for c in range(2):
            pieces = list(rest_values(tile_ref.at[s], own_ref, above, low_ref, c, width))
            for rows, lanes, value in pieces:
                rest_ref[c, rows, lanes] = value
            right_ref[2 * s + c] = pieces[0][2]


def update_quad_kernel(
    tile_ref, own_one, own_two, above_ref, up_one, up_two, quad_one, quad_two, left_ref, *, width,
):
    parts = ((own_one, up_one, quad_one), (own_two, up_two, quad_two))
    for s, (own_ref, up_ref, quad_ref) in enumerate(parts):
        above = above_ref.at[pl.ds(2 * s, 2)]
        for c in range(2):
            value = quad_value(tile_ref.at[s], own_ref, above, up_ref, c, width)
            quad_ref[c] = value
            left_ref[2 * s + c] = value


def finish_low_kernel(
    rest_one, rest_two, own_one, own_two, low_one, low_two, out_ref, rows_ref, sem, *, width,
):
    tile_px = own_one.shape[1]
    for s, (rest_ref, own_ref, low_ref) in enumerate(((rest_one, own_one, low_one), (rest_two, own_two, low_two))):
        for c in range(2):
            for _, lanes, value in low_values(rest_ref, own_ref, low_ref, c, width):
                rows_ref[s, c, :, lanes] = value
    copy = pltpu.make_async_copy(rows_ref, out_ref.at[:, :, pl.ds(width, tile_px - width), :], sem)
    copy.start()
    copy.wait()


def finish_top_kernel(
    rest_one, rest_two, quad_one, quad_two, own_one, own_two, above_ref, up_one, up_two, part_ref,
    out_ref, rows_ref, sems, *, width,
):
    del part_ref
    tile_px = own_one.shape[1]
    copies = []
    parts = ((rest_one, quad_one, own_one, up_one), (rest_two, quad_two, own_two, up_two))
    for s, (rest_ref, quad_ref, own_ref, up_ref) in enumerate(parts):
        above = above_ref.at[pl.ds(2 * s, 2)]
        for c in range(2):
            top, right = slice(0, width), slice(width, tile_px)
            rows_ref[s, c, :, :width] = quad_value(quad_ref, own_ref, above, up_ref, c, width)
            rows_ref[s, c, :, width:] = step(rest_ref[c, top, right], own_ref[c, top, right] + above[c, :, right])
            copies.append(
                pltpu.make_async_copy(rows_ref.at[s, c], out_ref.at[s, c, pl.ds(0, width), :], sems.at[2 * s + c])
            )
            copies[-1].start()
    for copy in copies:
        copy.wait()


def stage_kernel(*refs):
    sems = refs[-1]
    count = (len(refs) - 1) // 2
    copies = [pltpu.make_async_copy(refs[k], refs[count + k], sems.at[k]) for k in range(count)]
    for copy in copies:
        copy.start()
    for copy in copies:
        copy.wait()


F32 = functools.partial(jax.ShapeDtypeStruct, dtype=jnp.float32)
VMEM = pl.BlockSpec(memory_space=pltpu.VMEM)
LIMIT = pltpu.CompilerParams(vmem_limit_bytes=16 * 1024 * 1024)


FAR = pl.BlockSpec(memory_space=pltpu.MemorySpace.HBM)


def call(kernel, scalars, arrays, outs, scratch, **static):
    return pl.pallas_call(
        functools.partial(kernel, **static),
        in_specs=[VMEM] * (len(scalars) + len(arrays)),
        out_specs=[VMEM] * len(outs),
        out_shape=outs,
        scratch_shapes=scratch,
        compiler_params=LIMIT,
    )(*scalars, *arrays)


def pack_kernel(whole_ref, *refs, boxes):
    outs, sems = refs[:-1], refs[-1]
    copies = []
    for (slices, rows, lanes), out_ref in zip(boxes, outs):
        for k, s in enumerate(slices):
            source = whole_ref.at[s, :, pl.ds(*rows), pl.ds(*lanes)]
            copies.append(pltpu.make_async_copy(source, out_ref.at[pl.ds(2 * k, 2)], sems.at[len(copies)]))
    for copy in copies:
        copy.start()
    for copy in copies:
        copy.wait()


def pack(whole, boxes):
    count = sum(len(slices) for slices, _, _ in boxes)
    return pl.pallas_call(
        functools.partial(pack_kernel, boxes=boxes),
        in_specs=[FAR],
        out_specs=[VMEM] * len(boxes),
        out_shape=[F32((2 * len(slices), rows[1], lanes[1])) for slices, rows, lanes in boxes],
        scratch_shapes=[pltpu.SemaphoreType.DMA((count,))],
        compiler_params=LIMIT,
    )(in_hbm(whole))


def in_hbm(array):
    return pltpu.with_memory_space_constraint(array, pltpu.MemorySpace.HBM)


def body(
    specimen_slices,
    illumination_probe,
    propagation_phase,
    amplitudes,
    positions,
    counts,
    measurement_index,
):
    tile_px = specimen_slices.shape[2]
    width = illumination_probe.shape[1]
    spots = positions.shape[2]
    ext = tile_px + width
    across = tile_px - width
    cos, sin = jnp.cos(propagation_phase), jnp.sin(propagation_phase)
    numbers = jnp.concatenate([positions.reshape(-1), counts.reshape(-1), measurement_index.reshape(-1)])
    numbers = jnp.pad(numbers, (0, LANES - numbers.shape[0])).reshape(1, LANES)
    scalars = (numbers,)
    static = dict(spots=spots, width=width)
    ext_space = pltpu.VMEM((2, ext // LANES, ext, LANES), jnp.float32)
    wave_space = pltpu.VMEM((spots, 2, width, width), jnp.float32)
    wave = F32((spots, 2, width, width))
    square = F32((2, width, width))
    squares = F32((4, width, width))
    whole = F32((2, tile_px, tile_px))
    strip = F32((2, width, tile_px))
    gradient = [whole, strip, square, square, square]

    left, low, full = (0, width), (width, across), (0, tile_px)
    up_one, top = pack(specimen_slices, [((0,), left, left), ((0, 1), left, full)])
    upper_one = from_behind(up_one, "col", -1)
    below = from_behind(top, "row", -1)
    up_two, left_low = pack(specimen_slices, [((1,), left, left), ((0, 1), low, left)])
    upper_two = from_behind(up_two, "col", -1)
    lower = from_behind(left_low, "col", -1)
    far = (specimen_slices, illumination_probe, amplitudes[0, 0], jnp.asarray(dft_operands(width)))
    tile, probe, measured, table = pl.pallas_call(
        stage_kernel,
        in_specs=[FAR] * len(far),
        out_specs=[VMEM] * len(far),
        out_shape=[jax.ShapeDtypeStruct(x.shape, x.dtype) for x in far],
        scratch_shapes=[pltpu.SemaphoreType.DMA((len(far),))],
        compiler_params=LIMIT,
        name="stage",
    )(*[in_hbm(x) for x in far])
    corner_one = from_behind(upper_one, "row", -1)
    corner_two = from_behind(upper_two, "row", -1)
    for i in range(ITERS):
        if i == 0:
            own_two, down_two, up_two, low_two, diag_two, back = call(
                wave_kernel, scalars,
                (tile, below, upper_one, upper_two, lower, corner_one, corner_two, cos, sin, probe, measured, table),
                [*gradient, wave], [ext_space, ext_space, ext_space, wave_space, wave_space], **static,
            )
        else:
            (moved,) = call(
                forward_kernel, scalars, (*halo[0], cos, sin, probe, table),
                [wave], [ext_space, wave_space], **static,
            )
            own_two, down_two, up_two, low_two, diag_two, back = call(
                residual_kernel, scalars, (*halo[1], moved, measured, table),
                [*gradient, wave], [ext_space, ext_space, wave_space], **static,
            )
        low_two = from_behind(low_two, "col", 1)
        corner_two = from_behind(diag_two, "row", 1)
        own_one, down, up_one, low_one, diag_one = call(
            backward_kernel, scalars, (back, down_two, cos, sin, probe, table),
            [whole, F32((4, width, tile_px)), square, square, square], [ext_space], **static,
        )
        low_one = from_behind(low_one, "col", 1)
        corner_one = from_behind(diag_one, "row", 1)
        above = from_behind(down, "row", 1)
        up_two = up_two + corner_two
        up_one = up_one + corner_one
        up_two = from_behind(up_two, "col", 1)
        up_one = from_behind(up_one, "col", 1)
        if i + 1 < ITERS:
            left_one, left_two = call(
                update_low_kernel, (), (tile, own_one, own_two, low_one, low_two),
                [F32((2, across, width))] * 2, [], width=width,
            )
            lower_one = from_behind(left_one, "col", -1)
            rest_one, rest_two, right = call(
                update_rest_kernel, (), (tile, own_one, own_two, above, low_one, low_two),
                [whole, whole, F32((4, width, across))], [], width=width,
            )
            below_right = from_behind(right, "row", -1)
            quad_one, quad_two, left = call(
                update_quad_kernel, (),
                (tile, own_one, own_two, above, up_one, up_two),
                [square, square, squares], [], width=width,
            )
            upper_one = from_behind(quad_one, "col", -1)
            upper_two = from_behind(quad_two, "col", -1)
            below_left = from_behind(left, "row", -1)
            lower_two = from_behind(left_two, "col", -1)
            corner_one = from_behind(upper_one, "row", -1)
            corner_two = from_behind(upper_two, "row", -1)
            halo = (
                (rest_one, quad_one, below_left, below_right, upper_one, lower_one, corner_one),
                (rest_two, quad_two, below_left, below_right, upper_two, lower_two, corner_two),
            )
        else:
            end = dict(
                out_specs=FAR,
                out_shape=F32(specimen_slices.shape),
                compiler_params=LIMIT,
            )
            part = pl.pallas_call(
                functools.partial(finish_low_kernel, width=width),
                in_specs=[VMEM] * 6,
                scratch_shapes=[
                    pltpu.VMEM((2, 2, across, tile_px), jnp.float32), pltpu.SemaphoreType.DMA(()),
                ],
                name="finish_low",
                **end,
            )(rest_one, rest_two, own_one, own_two, low_one, low_two)
            updated = pl.pallas_call(
                functools.partial(finish_top_kernel, width=width),
                in_specs=[VMEM] * 9 + [FAR],
                input_output_aliases={9: 0},
                scratch_shapes=[
                    pltpu.VMEM((2, 2, width, tile_px), jnp.float32), pltpu.SemaphoreType.DMA((4,)),
                ],
                name="finish_top",
                **end,
            )(
                rest_one, rest_two, quad_one, quad_two, own_one, own_two, above, up_one, up_two, in_hbm(part),
            )
    return updated


def solution(mesh):
    placed = (
        P(None, None, "row", "col"),
        P(),
        P(),
        P("row", "col", None, None, None),
        P("row", "col", None, None),
        P("row", "col"),
        P("row", "col", None),
    )

    return jax.shard_map(body, mesh=mesh, in_specs=placed, out_specs=P(None, None, "row", "col"), check_vma=False)
```

```python
import functools
import math

import jax
import jax.numpy as jnp
import ml_dtypes
import numpy as np
from jax import lax
from jax.experimental import pallas as pl
from jax.experimental.pallas import tpu as pltpu
from jax.sharding import PartitionSpec as P


ITERS = 2
LANES = 128

step_size = 0.02
floor_amp = 0.5


def from_behind(block, axis, distance):
    devices = range(lax.axis_size(axis))
    route = [((i - distance) % len(devices), i) for i in devices]
    return lax.ppermute(block, axis, route)


def two_parts(value):
    high = value.astype(ml_dtypes.bfloat16)
    low = (value - high.astype(np.float64)).astype(ml_dtypes.bfloat16)
    return high, low


def dft_operands(width):
    index = np.arange(width)
    angle = (index[:, None] * index[None, :] % width) * (2.0 * math.pi / width)
    real = np.cos(angle) / math.sqrt(width)
    imag = -np.sin(angle) / math.sqrt(width)
    right = np.block([[real, imag], [-imag, real]])
    right_high, right_low = two_parts(right)
    left_high, left_low = two_parts(right.T)
    return np.stack([right_high, right_low, left_high, left_low])


def split(value):
    high = value.astype(jnp.bfloat16)
    low = (value - high.astype(jnp.float32)).astype(jnp.bfloat16)
    return high, low


def rows_of(j, width):
    return slice(j * width, (j + 1) * width)


def product(left, right):
    return jnp.dot(left, right, preferred_element_type=jnp.float32)


def right_side(pairs, table_ref):
    high, low = split(jnp.concatenate([jnp.concatenate(pair, 1) for pair in pairs], 0))
    return product(high, table_ref[0]) + product(low, table_ref[0]) + product(high, table_ref[1])


def left_side(half, table_ref, width):
    count = half.shape[0] // width
    parts = [half[rows_of(k, width)] for k in range(count)]
    tall = [jnp.concatenate([part[:, :width], part[:, width:]], 0) for part in parts]
    high, low = split(jnp.concatenate(tall, 1))
    both = product(table_ref[2], jnp.concatenate([high, low], 1))
    full = both[:, :high.shape[1]] + both[:, high.shape[1]:] + product(table_ref[3], high)
    return [(full[:width, rows_of(k, width)], full[width:, rows_of(k, width)]) for k in range(count)]


def interleave(chains, lag):
    waiting = [(n * lag, chain) for n, chain in enumerate(chains)]
    while waiting:
        after = []
        for delay, chain in waiting:
            if delay:
                after.append((delay - 1, chain))
            elif next(chain, None) is not None:
                after.append((0, chain))
        waiting = after


def fill_ext(ext_ref, pieces):
    for row, col, source in pieces:
        height, across = source.shape[1:]
        for c in range(2):
            for b in range(across // LANES):
                ext_ref[c, col // LANES + b, row:row + height, :] = source[c, :, b * LANES:(b + 1) * LANES]


def pick(numbers_ref, k):
    values = numbers_ref[...].astype(jnp.float32)
    lane = lax.broadcasted_iota(jnp.int32, values.shape, 1)
    return jnp.sum(jnp.where(lane == k, values, 0.0)).astype(jnp.int32)


def places(numbers_ref, spots):
    spot_list = []
    for j in range(spots):
        row, col = pick(numbers_ref, 2 * j), pick(numbers_ref, 2 * j + 1)
        spot_list.append((row, col // LANES, col % LANES))
    return spot_list


def window(ext_ref, c, spot, width, lane):
    row, block, shift = spot
    near = ext_ref[c, block, pl.ds(row, width), :]
    far = ext_ref[c, block + 1, pl.ds(row, width), :]
    return pltpu.roll(jnp.where(lane >= shift, near, far), LANES - shift, 1)


def scatter(grad_ref, c, spot, width, lane, used, update):
    row, block, shift = spot
    turned = pltpu.roll(jnp.where(used, update, 0.0), shift, 1)
    near = lane >= shift
    grad_ref[c, block, pl.ds(row, width), :] += jnp.where(near, turned, 0.0)
    grad_ref[c, block + 1, pl.ds(row, width), :] += jnp.where(near, 0.0, turned)


def emit(grad_ref, own_ref, down_ref, upper_ref, lower_ref, diag_ref, width):
    tile_px = own_ref.shape[1]
    blocks = tile_px // LANES
    for c in range(2):
        for b in range(blocks):
            lanes = slice(b * LANES, (b + 1) * LANES)
            own_ref[c, :, lanes] = grad_ref[c, b, :tile_px, :]
            down_ref[c, :, lanes] = grad_ref[c, b, tile_px:, :]
        upper_ref[c] = grad_ref[c, blocks, :width, :]
        lower_ref[c] = grad_ref[c, blocks, width:tile_px, :]
        diag_ref[c] = grad_ref[c, blocks, tile_px:, :]


def lanes_of(width):
    return lax.broadcasted_iota(jnp.int32, (width, LANES), 1)


LAG = 0


def groups_of(spots):
    return [range(j, j + 1) for j in range(spots)]


def forward_steps(group, enter_ref, leave_ref, cos_ref, sin_ref, table_ref, width):
    half = right_side([(enter_ref[j, 0], enter_ref[j, 1]) for j in group], table_ref)
    yield True
    pairs = left_side(half, table_ref, width)
    yield True
    half = right_side([
        (cos_ref[...] * real - sin_ref[...] * imag, -(cos_ref[...] * imag + sin_ref[...] * real))
        for real, imag in pairs
    ], table_ref)
    yield True
    pairs = left_side(half, table_ref, width)
    yield True
    for j, (real, negative) in zip(group, pairs):
        leave_ref[j, 0] = real
        leave_ref[j, 1] = -negative


def residual_steps(group, moved_ref, win_ref, measured_of, finish, table_ref, width):
    half = right_side([
        (
            moved_ref[j, 0] * win_ref[j, 0] - moved_ref[j, 1] * win_ref[j, 1],
            moved_ref[j, 0] * win_ref[j, 1] + moved_ref[j, 1] * win_ref[j, 0],
        )
        for j in group
    ], table_ref)
    yield True
    pairs = left_side(half, table_ref, width)
    yield True
    residuals = []
    for j, (real, imag) in zip(group, pairs):
        power = jnp.maximum(real * real + imag * imag, floor_amp * floor_amp)
        factor = 1.0 - measured_of(j) * lax.rsqrt(power)
        residuals.append((real * factor, -(imag * factor)))
    half = right_side(residuals, table_ref)
    yield True
    pairs = left_side(half, table_ref, width)
    yield True
    for j, (real, negative) in zip(group, pairs):
        finish(j, real, -negative)


def by_count(total, spots, run):
    groups = groups_of(spots)
    lower = 0
    for size in sorted({1, (len(groups) + 1) // 2, len(groups)}):
        fits = (total > lower) if size == len(groups) else (total > lower) & (total <= size)
        pl.when(fits)(functools.partial(run, groups[:size]))
        lower = size


def joined(*parts):
    for part in parts:
        yield from part


def whole_pieces(refs, s, tile_px, width):
    tile_ref, below_ref, upper_ref, lower_ref, corner_ref = refs
    both = pl.ds(2 * s, 2)
    return [
        (0, 0, tile_ref.at[s]),
        (tile_px, 0, below_ref.at[both]),
        (0, tile_px, upper_ref),
        (width, tile_px, lower_ref.at[both]),
        (tile_px, tile_px, corner_ref),
    ]


def slice_pieces(refs, s, tile_px, width):
    rest_ref, quad_ref, below_left_ref, below_right_ref, upper_ref, lower_ref, corner_ref = refs
    both = pl.ds(2 * s, 2)
    across = tile_px - width
    return [
        (width, 0, rest_ref.at[:, pl.ds(width, across), :]),
        (0, width, rest_ref.at[:, pl.ds(0, width), pl.ds(width, across)]),
        (0, 0, quad_ref),
        (tile_px, 0, below_left_ref.at[both]),
        (tile_px, width, below_right_ref.at[both]),
        (0, tile_px, upper_ref),
        (width, tile_px, lower_ref),
        (tile_px, tile_px, corner_ref),
    ]


def take_windows(ext_ref, spot_list, probes, win_ref, width, lane):
    for j in probes:
        spot = spot_list[j]
        win_ref[j, 0] = window(ext_ref, 0, spot, width, lane)
        win_ref[j, 1] = window(ext_ref, 1, spot, width, lane)


def light(ext_ref, spot_list, probes, probe_ref, enter_ref, width, lane):
    for j in probes:
        spot = spot_list[j]
        real = window(ext_ref, 0, spot, width, lane)
        imag = window(ext_ref, 1, spot, width, lane)
        enter_ref[j, 0] = probe_ref[0] * real - probe_ref[1] * imag
        enter_ref[j, 1] = probe_ref[0] * imag + probe_ref[1] * real


def residual_end(total, spot_list, ext_ref, moved_ref, win_ref, back_ref, width, lane):
    def finish(j, real, imag):
        used = j < total
        scatter(ext_ref, 0, spot_list[j], width, lane, used, moved_ref[j, 0] * real + moved_ref[j, 1] * imag)
        scatter(ext_ref, 1, spot_list[j], width, lane, used, moved_ref[j, 0] * imag - moved_ref[j, 1] * real)
        back_ref[j, 0] = win_ref[j, 0] * real + win_ref[j, 1] * imag
        back_ref[j, 1] = win_ref[j, 0] * imag - win_ref[j, 1] * real

    return finish


def wave_kernel(
    numbers_ref, tile_ref, below_ref, upper_one, upper_two, lower_ref, corner_one, corner_two,
    cos_ref, sin_ref, probe_ref, amp_ref, table_ref,
    own_ref, down_ref, up_out_ref, low_out_ref, diag_ref, back_ref,
    ext_ref, other_ref, grad_ref, win_ref, moved_ref, *, spots, width,
):
    lane = lanes_of(width)
    tile_px = own_ref.shape[1]
    first = (tile_ref, below_ref, upper_one, lower_ref, corner_one)
    second = (tile_ref, below_ref, upper_two, lower_ref, corner_two)
    fill_ext(ext_ref, whole_pieces(first, 0, tile_px, width))
    fill_ext(other_ref, whole_pieces(second, 1, tile_px, width))
    grad_ref[...] = jnp.zeros(grad_ref.shape, jnp.float32)
    spot_list = places(numbers_ref, spots)
    total = pick(numbers_ref, 2 * spots)
    finish = residual_end(total, spot_list, grad_ref, moved_ref, win_ref, back_ref, width, lane)
    measured_of = lambda j: amp_ref[pick(numbers_ref, 2 * spots + 1 + j)]

    def run(groups):
        probes = [j for group in groups for j in group]
        light(ext_ref, spot_list, probes, probe_ref, back_ref, width, lane)
        take_windows(other_ref, spot_list, probes, win_ref, width, lane)
        interleave([
            joined(
                forward_steps(group, back_ref, moved_ref, cos_ref, sin_ref, table_ref, width),
                residual_steps(group, moved_ref, win_ref, measured_of, finish, table_ref, width),
            )
            for group in groups
        ], LAG)

    by_count(total, spots, run)
    emit(grad_ref, own_ref, down_ref, up_out_ref, low_out_ref, diag_ref, width)


def forward_kernel(
    numbers_ref, rest_ref, quad_ref, left_ref, right_ref, upper_ref, lower_ref, corner_ref,
    cos_ref, sin_ref, probe_ref, table_ref, moved_ref, ext_ref, enter_ref, *, spots, width,
):
    lane = lanes_of(width)
    halo = (rest_ref, quad_ref, left_ref, right_ref, upper_ref, lower_ref, corner_ref)
    fill_ext(ext_ref, slice_pieces(halo, 0, rest_ref.shape[1], width))
    spot_list = places(numbers_ref, spots)

    def run(groups):
        light(ext_ref, spot_list, [j for group in groups for j in group], probe_ref, enter_ref, width, lane)
        interleave([
            forward_steps(group, enter_ref, moved_ref, cos_ref, sin_ref, table_ref, width) for group in groups
        ], LAG)

    by_count(pick(numbers_ref, 2 * spots), spots, run)


def residual_kernel(
    numbers_ref, rest_ref, quad_ref, left_ref, right_ref, upper_ref, lower_ref, corner_ref,
    moved_ref, amp_ref, table_ref,
    own_ref, down_ref, up_out_ref, low_out_ref, diag_ref, back_ref,
    ext_ref, grad_ref, win_ref, *, spots, width,
):
    lane = lanes_of(width)
    halo = (rest_ref, quad_ref, left_ref, right_ref, upper_ref, lower_ref, corner_ref)
    fill_ext(ext_ref, slice_pieces(halo, 1, rest_ref.shape[1], width))
    grad_ref[...] = jnp.zeros(grad_ref.shape, jnp.float32)
    spot_list = places(numbers_ref, spots)
    total = pick(numbers_ref, 2 * spots)
    finish = residual_end(total, spot_list, grad_ref, moved_ref, win_ref, back_ref, width, lane)
    measured_of = lambda j: amp_ref[pick(numbers_ref, 2 * spots + 1 + j)]

    def run(groups):
        take_windows(ext_ref, spot_list, [j for group in groups for j in group], win_ref, width, lane)
        interleave([
            residual_steps(group, moved_ref, win_ref, measured_of, finish, table_ref, width) for group in groups
        ], LAG)

    by_count(total, spots, run)
    emit(grad_ref, own_ref, down_ref, up_out_ref, low_out_ref, diag_ref, width)


def backward_kernel(
    numbers_ref, back_ref, other_down_ref, cos_ref, sin_ref, probe_ref, table_ref,
    own_ref, down_ref, up_out_ref, low_out_ref, diag_ref, ext_ref, *, spots, width,
):
    lane = lanes_of(width)
    down_ref[2:] = other_down_ref[...]
    spot_list = places(numbers_ref, spots)
    total = pick(numbers_ref, 2 * spots)
    ext_ref[...] = jnp.zeros(ext_ref.shape, jnp.float32)

    def chain(group):
        half = right_side([(back_ref[j, 0], back_ref[j, 1]) for j in group], table_ref)
        yield True
        pairs = left_side(half, table_ref, width)
        yield True
        half = right_side([
            (cos_ref[...] * real + sin_ref[...] * imag, -(cos_ref[...] * imag - sin_ref[...] * real))
            for real, imag in pairs
        ], table_ref)
        yield True
        pairs = left_side(half, table_ref, width)
        yield True
        for j, (real, negative) in zip(group, pairs):
            imag = -negative
            spot = spot_list[j]
            used = j < total
            scatter(ext_ref, 0, spot, width, lane, used, probe_ref[0] * real + probe_ref[1] * imag)
            scatter(ext_ref, 1, spot, width, lane, used, probe_ref[0] * imag - probe_ref[1] * real)

    by_count(total, spots, lambda groups: interleave([chain(group) for group in groups], LAG))
    emit(ext_ref, own_ref, down_ref, up_out_ref, low_out_ref, diag_ref, width)


def step(value, gradient):
    return value - step_size * gradient


def rest_values(tile_ref, own_ref, above_ref, lower_ref, c, width):
    top, right = slice(0, width), slice(width, own_ref.shape[1])
    yield top, right, step(tile_ref[c, top, right], own_ref[c, top, right] + above_ref[c, :, right])
    yield from low_values(tile_ref, own_ref, lower_ref, c, width)


def low_values(tile_ref, own_ref, lower_ref, c, width):
    tile_px = own_ref.shape[1]
    low, left, right = slice(width, tile_px), slice(0, width), slice(width, tile_px)
    yield low, left, step(tile_ref[c, low, left], own_ref[c, low, left] + lower_ref[c])
    yield low, right, step(tile_ref[c, low, right], own_ref[c, low, right])


def quad_value(quad_ref, own_ref, above_ref, upper_ref, c, width):
    top, left = slice(0, width), slice(0, width)
    return step(quad_ref[c, top, left], own_ref[c, top, left] + above_ref[c, :, left] + upper_ref[c])


def update_low_kernel(tile_ref, own_one, own_two, low_one, low_two, left_one, left_two, *, width):
    tile_px = own_one.shape[1]
    low, left = slice(width, tile_px), slice(0, width)
    for s, (own_ref, low_ref, left_ref) in enumerate(((own_one, low_one, left_one), (own_two, low_two, left_two))):
        for c in range(2):
            left_ref[c] = step(tile_ref[s, c, low, left], own_ref[c, low, left] + low_ref[c])


def update_rest_kernel(
    tile_ref, own_one, own_two, above_ref, low_one, low_two, rest_one, rest_two, right_ref, *, width,
):
    parts = ((own_one, low_one, rest_one), (own_two, low_two, rest_two))
    for s, (own_ref, low_ref, rest_ref) in enumerate(parts):
        above = above_ref.at[pl.ds(2 * s, 2)]
        for c in range(2):
            pieces = list(rest_values(tile_ref.at[s], own_ref, above, low_ref, c, width))
            for rows, lanes, value in pieces:
                rest_ref[c, rows, lanes] = value
            right_ref[2 * s + c] = pieces[0][2]


def update_quad_kernel(
    tile_ref, own_one, own_two, above_ref, up_one, up_two, quad_one, quad_two, left_ref, *, width,
):
    parts = ((own_one, up_one, quad_one), (own_two, up_two, quad_two))
    for s, (own_ref, up_ref, quad_ref) in enumerate(parts):
        above = above_ref.at[pl.ds(2 * s, 2)]
        for c in range(2):
            value = quad_value(tile_ref.at[s], own_ref, above, up_ref, c, width)
            quad_ref[c] = value
            left_ref[2 * s + c] = value


def finish_low_kernel(
    rest_one, rest_two, own_one, own_two, low_one, low_two, out_ref, rows_ref, sem, *, width,
):
    tile_px = own_one.shape[1]
    for s, (rest_ref, own_ref, low_ref) in enumerate(((rest_one, own_one, low_one), (rest_two, own_two, low_two))):
        for c in range(2):
            for _, lanes, value in low_values(rest_ref, own_ref, low_ref, c, width):
                rows_ref[s, c, :, lanes] = value
    copy = pltpu.make_async_copy(rows_ref, out_ref.at[:, :, pl.ds(width, tile_px - width), :], sem)
    copy.start()
    copy.wait()


def finish_top_kernel(
    rest_one, rest_two, quad_one, quad_two, own_one, own_two, above_ref, up_one, up_two, part_ref,
    out_ref, rows_ref, sems, *, width,
):
    del part_ref
    tile_px = own_one.shape[1]
    copies = []
    parts = ((rest_one, quad_one, own_one, up_one), (rest_two, quad_two, own_two, up_two))
    for s, (rest_ref, quad_ref, own_ref, up_ref) in enumerate(parts):
        above = above_ref.at[pl.ds(2 * s, 2)]
        for c in range(2):
            top, right = slice(0, width), slice(width, tile_px)
            rows_ref[s, c, :, :width] = quad_value(quad_ref, own_ref, above, up_ref, c, width)
            rows_ref[s, c, :, width:] = step(rest_ref[c, top, right], own_ref[c, top, right] + above[c, :, right])
            copies.append(
                pltpu.make_async_copy(rows_ref.at[s, c], out_ref.at[s, c, pl.ds(0, width), :], sems.at[2 * s + c])
            )
            copies[-1].start()
    for copy in copies:
        copy.wait()


def stage_kernel(*refs):
    sems = refs[-1]
    count = (len(refs) - 1) // 2
    copies = [pltpu.make_async_copy(refs[k], refs[count + k], sems.at[k]) for k in range(count)]
    for copy in copies:
        copy.start()
    for copy in copies:
        copy.wait()


F32 = functools.partial(jax.ShapeDtypeStruct, dtype=jnp.float32)
VMEM = pl.BlockSpec(memory_space=pltpu.VMEM)
LIMIT = pltpu.CompilerParams(vmem_limit_bytes=16 * 1024 * 1024)


FAR = pl.BlockSpec(memory_space=pltpu.MemorySpace.HBM)


def call(kernel, scalars, arrays, outs, scratch, **static):
    return pl.pallas_call(
        functools.partial(kernel, **static),
        in_specs=[VMEM] * (len(scalars) + len(arrays)),
        out_specs=[VMEM] * len(outs),
        out_shape=outs,
        scratch_shapes=scratch,
        compiler_params=LIMIT,
    )(*scalars, *arrays)


def pack_kernel(whole_ref, *refs, boxes):
    outs, sems = refs[:-1], refs[-1]
    copies = []
    for (slices, rows, lanes), out_ref in zip(boxes, outs):
        for k, s in enumerate(slices):
            source = whole_ref.at[s, :, pl.ds(*rows), pl.ds(*lanes)]
            copies.append(pltpu.make_async_copy(source, out_ref.at[pl.ds(2 * k, 2)], sems.at[len(copies)]))
    for copy in copies:
        copy.start()
    for copy in copies:
        copy.wait()


def pack(whole, boxes):
    count = sum(len(slices) for slices, _, _ in boxes)
    return pl.pallas_call(
        functools.partial(pack_kernel, boxes=boxes),
        in_specs=[FAR],
        out_specs=[VMEM] * len(boxes),
        out_shape=[F32((2 * len(slices), rows[1], lanes[1])) for slices, rows, lanes in boxes],
        scratch_shapes=[pltpu.SemaphoreType.DMA((count,))],
        compiler_params=LIMIT,
    )(in_hbm(whole))


def in_hbm(array):
    return pltpu.with_memory_space_constraint(array, pltpu.MemorySpace.HBM)


def body(
    specimen_slices,
    illumination_probe,
    propagation_phase,
    amplitudes,
    positions,
    counts,
    measurement_index,
):
    tile_px = specimen_slices.shape[2]
    width = illumination_probe.shape[1]
    spots = positions.shape[2]
    ext = tile_px + width
    across = tile_px - width
    cos, sin = jnp.cos(propagation_phase), jnp.sin(propagation_phase)
    numbers = jnp.concatenate([positions.reshape(-1), counts.reshape(-1), measurement_index.reshape(-1)])
    numbers = jnp.pad(numbers, (0, LANES - numbers.shape[0])).reshape(1, LANES)
    scalars = (numbers,)
    static = dict(spots=spots, width=width)
    ext_space = pltpu.VMEM((2, ext // LANES, ext, LANES), jnp.float32)
    wave_space = pltpu.VMEM((spots, 2, width, width), jnp.float32)
    wave = F32((spots, 2, width, width))
    square = F32((2, width, width))
    squares = F32((4, width, width))
    whole = F32((2, tile_px, tile_px))
    strip = F32((2, width, tile_px))
    gradient = [whole, strip, square, square, square]

    left, low, full = (0, width), (width, across), (0, tile_px)
    up_one, top = pack(specimen_slices, [((0,), left, left), ((0, 1), left, full)])
    upper_one = from_behind(up_one, "col", -1)
    below = from_behind(top, "row", -1)
    up_two, left_low = pack(specimen_slices, [((1,), left, left), ((0, 1), low, left)])
    upper_two = from_behind(up_two, "col", -1)
    lower = from_behind(left_low, "col", -1)
    far = (specimen_slices, illumination_probe, amplitudes[0, 0], jnp.asarray(dft_operands(width)))
    tile, probe, measured, table = pl.pallas_call(
        stage_kernel,
        in_specs=[FAR] * len(far),
        out_specs=[VMEM] * len(far),
        out_shape=[jax.ShapeDtypeStruct(x.shape, x.dtype) for x in far],
        scratch_shapes=[pltpu.SemaphoreType.DMA((len(far),))],
        compiler_params=LIMIT,
        name="stage",
    )(*[in_hbm(x) for x in far])
    corner_one = from_behind(upper_one, "row", -1)
    corner_two = from_behind(upper_two, "row", -1)
    for i in range(ITERS):
        if i == 0:
            own_two, down_two, up_two, low_two, diag_two, back = call(
                wave_kernel, scalars,
                (tile, below, upper_one, upper_two, lower, corner_one, corner_two, cos, sin, probe, measured, table),
                [*gradient, wave], [ext_space, ext_space, ext_space, wave_space, wave_space], **static,
            )
        else:
            (moved,) = call(
                forward_kernel, scalars, (*halo[0], cos, sin, probe, table),
                [wave], [ext_space, wave_space], **static,
            )
            own_two, down_two, up_two, low_two, diag_two, back = call(
                residual_kernel, scalars, (*halo[1], moved, measured, table),
                [*gradient, wave], [ext_space, ext_space, wave_space], **static,
            )
        low_two = from_behind(low_two, "col", 1)
        corner_two = from_behind(diag_two, "row", 1)
        own_one, down, up_one, low_one, diag_one = call(
            backward_kernel, scalars, (back, down_two, cos, sin, probe, table),
            [whole, F32((4, width, tile_px)), square, square, square], [ext_space], **static,
        )
        low_one = from_behind(low_one, "col", 1)
        corner_one = from_behind(diag_one, "row", 1)
        above = from_behind(down, "row", 1)
        up_two = up_two + corner_two
        up_one = up_one + corner_one
        up_two = from_behind(up_two, "col", 1)
        up_one = from_behind(up_one, "col", 1)
        if i + 1 < ITERS:
            left_one, left_two = call(
                update_low_kernel, (), (tile, own_one, own_two, low_one, low_two),
                [F32((2, across, width))] * 2, [], width=width,
            )
            lower_one = from_behind(left_one, "col", -1)
            rest_one, rest_two, right = call(
                update_rest_kernel, (), (tile, own_one, own_two, above, low_one, low_two),
                [whole, whole, F32((4, width, across))], [], width=width,
            )
            below_right = from_behind(right, "row", -1)
            quad_one, quad_two, left = call(
                update_quad_kernel, (),
                (tile, own_one, own_two, above, up_one, up_two),
                [square, square, squares], [], width=width,
            )
            upper_one = from_behind(quad_one, "col", -1)
            upper_two = from_behind(quad_two, "col", -1)
            below_left = from_behind(left, "row", -1)
            lower_two = from_behind(left_two, "col", -1)
            corner_one = from_behind(upper_one, "row", -1)
            corner_two = from_behind(upper_two, "row", -1)
            halo = (
                (rest_one, quad_one, below_left, below_right, upper_one, lower_one, corner_one),
                (rest_two, quad_two, below_left, below_right, upper_two, lower_two, corner_two),
            )
        else:
            end = dict(
                out_specs=FAR,
                out_shape=F32(specimen_slices.shape),
                compiler_params=LIMIT,
            )
            part = pl.pallas_call(
                functools.partial(finish_low_kernel, width=width),
                in_specs=[VMEM] * 6,
                scratch_shapes=[
                    pltpu.VMEM((2, 2, across, tile_px), jnp.float32), pltpu.SemaphoreType.DMA(()),
                ],
                name="finish_low",
                **end,
            )(rest_one, rest_two, own_one, own_two, low_one, low_two)
            updated = pl.pallas_call(
                functools.partial(finish_top_kernel, width=width),
                in_specs=[VMEM] * 9 + [FAR],
                input_output_aliases={9: 0},
                scratch_shapes=[
                    pltpu.VMEM((2, 2, width, tile_px), jnp.float32), pltpu.SemaphoreType.DMA((4,)),
                ],
                name="finish_top",
                **end,
            )(
                rest_one, rest_two, quad_one, quad_two, own_one, own_two, above, up_one, up_two, in_hbm(part),
            )
    return updated


def solution(mesh):
    placed = (
        P(None, None, "row", "col"),
        P(),
        P(),
        P("row", "col", None, None, None),
        P("row", "col", None, None),
        P("row", "col"),
        P("row", "col", None),
    )

    return jax.shard_map(body, mesh=mesh, in_specs=placed, out_specs=P(None, None, "row", "col"), check_vma=False)
```
